32 devices in a mesh: frame: 8 (over y, x, core), module: 4 (over z).
Axes of the slice: x: 2, y: 2, z: 4, core: 2. Of those that a mesh axis runs over, the one named last changes fastest.
Arguments:
- raw_frames: int32 [2048, 32768], P('frame', 'module'), may hold values from 256 to 3856
- dark_frame: float32 [32768], P('module'), may hold values from 0 to 240
- flat_field: float32 [32768], P('module'), may hold values from 0.125 to 2.625, as said below
- membership: int32 [16, 32768], P(None, 'module'), may hold values from 0 to 1, as said below
Outputs:
- correlation: float32 [16, 8, 5, 256, 256], P('module', 'frame')
The draws below stay inside these ranges and needn't reach their ends.
Inputs may be any that keep to these rules, and one draw needn't show every extreme that they name: `membership`: each pixel belongs to exactly one q-bin, and every module holds exactly 512 pixels of each q-bin, in no particular order. `flat_field`: positive gains.
All inputs are finite; a program needn't handle non-finite values.
Results may differ from the reference program's by a relative error of at most 0.0003.
Values may be sent and summed in bfloat16 or wider, within the bound.
A program may use at most 128 MiB of HBM per device.

```python
import jax
import jax.numpy as jnp
from jax import lax

BLK = 256
QBINS = 16
PIX_DEV = 8192
BLOCKS = 8
FRAMES = 2048
PIXELS = 32768


def bin_labels(key):
    modules = PIXELS // PIX_DEV
    per_bin = PIX_DEV // QBINS
    base_labels = jnp.tile(jnp.arange(PIX_DEV, dtype=jnp.int32) // per_bin, (modules, 1))
    shuffled = jax.random.permutation(jax.random.fold_in(key, 101), base_labels, axis=1, independent=True)
    return shuffled.reshape(PIXELS)


def draw_membership(key, part):
    labels = bin_labels(key)
    return (labels[None, :] == jnp.arange(QBINS, dtype=jnp.int32)[:, None]).astype(jnp.int32)


def draw_flat_field(key, part):
    gain_values = jax.random.uniform(key, (PIXELS,), jnp.float32, 0.25, 1.75)
    return gain_values


def draw_raw_frames(key, part):
    labels = bin_labels(key)
    modules = PIXELS // PIX_DEV
    keys = jax.random.split(jax.random.fold_in(key, 202), 7)
    octave_steps = jax.random.randint(keys[0], (QBINS,), 0, 21)
    window_base = 24 * jnp.left_shift(jnp.ones_like(octave_steps), octave_steps // 4) * (4 + octave_steps % 4) // 4
    window_phase = jax.random.randint(keys[1], (QBINS,), 0, 2)
    block_index = jnp.arange(FRAMES, dtype=jnp.int32) // BLK
    window = window_base[None, :] * (1 + (block_index[:, None] + window_phase[None, :]) % 2)
    frame_stop = jnp.arange(1, FRAMES + 1, dtype=jnp.int32)[:, None]

    def one_module(module):
        module_keys = jax.random.split(jax.random.fold_in(keys[2], module), 3)
        local_labels = lax.dynamic_slice_in_dim(labels, module * PIX_DEV, PIX_DEV)
        local_window = jnp.take(window, local_labels, axis=1)
        window_start = jnp.maximum(frame_stop - local_window, 0)
        fields = []
        for field_key in (module_keys[0], module_keys[1]):
            increments = jax.random.randint(field_key, (FRAMES, PIX_DEV), -15, 16)
            totals = jnp.concatenate([jnp.zeros((1, PIX_DEV), jnp.int32), jnp.cumsum(increments, axis=0, dtype=jnp.int32)], axis=0)
            fields.append(totals[1:] - jnp.take_along_axis(totals, window_start, axis=0))
        divisor = jnp.maximum(160 * local_window // 200, 1)
        speckle = jnp.minimum((fields[0] * fields[0] + fields[1] * fields[1]) // divisor, 836)
        shot_noise = jax.random.randint(module_keys[2], (FRAMES, PIX_DEV), 0, 64)
        level_counts = (speckle + shot_noise) * (modules - 1 + 3 * module) // (modules - 1)
        return 256 + level_counts
    stacked = lax.map(one_module, jnp.arange(modules, dtype=jnp.int32))
    frame_counts = jnp.transpose(stacked, (1, 0, 2)).reshape(FRAMES, PIXELS)
    high_row = jax.random.randint(keys[3], (), 0, FRAMES)
    high_column = jax.random.randint(keys[4], (), 0, PIXELS)
    low_row = (high_row + 1 + jax.random.randint(keys[5], (), 0, FRAMES - 1)) % FRAMES
    low_column = jax.random.randint(keys[6], (), 0, PIXELS)
    frame_counts = frame_counts.at[high_row, high_column].set(3856)
    frame_counts = frame_counts.at[low_row, low_column].set(256)
    return frame_counts.astype(jnp.int32)


def level_of(own_key, shape, pieces, least, largest):
    level = 1.0
    for dim, shards_of in pieces:
        steps = jax.random.uniform(jax.random.fold_in(jax.random.fold_in(own_key, 6), dim), (shards_of,), jnp.float32, least / len(pieces), largest / len(pieces))
        level = level * jnp.repeat(jnp.exp(steps), shape[dim] // shards_of).reshape((-1,) + (1,) * (len(shape) - 1 - dim))
    return level


def setup_inputs(seed: int = 0) -> dict:
    key_of = jax.random.split(jax.random.key(seed), 5)
    return {
        "raw_frames": draw_raw_frames(jax.random.fold_in(key_of[4], 71), 0),
        "dark_frame": jnp.clip(240.0 * jax.random.uniform(key_of[1], (PIXELS,), jnp.float32) ** level_of(key_of[1], (PIXELS,), ((0, 4),), -0.2, 0.2), 0.0, 240.0),
        "flat_field": draw_flat_field(jax.random.fold_in(key_of[4], 71), 0),
        "membership": draw_membership(jax.random.fold_in(key_of[4], 71), 0),
    }


def reference(raw_frames, dark_frame, flat_field, membership):
    intensity = (raw_frames.astype(jnp.float32) - dark_frame[None, :]) * flat_field[None, :]
    members = membership.astype(jnp.float32)
    bin_sums = jnp.dot(intensity, members.T, precision=lax.Precision.HIGHEST)
    counts = lax.optimization_barrier(jnp.sum(members, axis=1))
    scales = jnp.sqrt(counts)[None, :] / bin_sums
    pixel_scale = jnp.dot(scales, members, precision=lax.Precision.HIGHEST)
    scaled = (intensity * pixel_scale).astype(jnp.bfloat16)
    labels = lax.optimization_barrier(jnp.sum(membership * jnp.arange(QBINS, dtype=jnp.int32)[:, None], axis=0)).astype(jnp.int32)
    ordering = jnp.argsort(labels, stable=True)
    per_bin = PIXELS // QBINS
    grouped = jnp.take(scaled, ordering, axis=1).reshape(BLOCKS, BLK, QBINS, per_bin)
    zero_blocks = jnp.zeros((2, BLK, QBINS, per_bin), jnp.bfloat16)
    padded = jnp.concatenate([grouped, zero_blocks], axis=0)

    def single_block(block_index):
        target = lax.dynamic_index_in_dim(grouped, block_index, 0, keepdims=False).astype(jnp.float32)
        partners = lax.dynamic_slice_in_dim(padded, block_index, 3, 0).astype(jnp.float32)
        return jnp.einsum('urp,jvrp->rjuv', target, partners, precision=lax.Precision.HIGHEST)
    forward = lax.map(single_block, jnp.arange(BLOCKS, dtype=jnp.int32))
    zero_one = jnp.zeros((1, QBINS, BLK, BLK), forward.dtype)
    zero_two = jnp.zeros((2, QBINS, BLK, BLK), forward.dtype)
    one_back = jnp.swapaxes(jnp.concatenate([zero_one, forward[:-1, :, 1]], axis=0), 2, 3)
    two_back = jnp.swapaxes(jnp.concatenate([zero_two, forward[:-2, :, 2]], axis=0), 2, 3)
    result = jnp.concatenate([two_back[:, :, None], one_back[:, :, None], forward], axis=2)
    return jnp.transpose(result, (1, 0, 2, 3, 4))
```

```python
import functools

import jax
import jax.numpy as jnp
from jax import lax
from jax.experimental import pallas as pl
from jax.experimental.pallas import tpu as pltpu
from jax.sharding import PartitionSpec as P

MESH = pl.DeviceIdType.MESH
VMEM_BYTES = 60 * 1024 * 1024
LANES = 128


def order_kernel(members, order):
    bins, pixels = members.shape
    per_bin = pixels // bins
    span = 2 * LANES
    rows = pixels // LANES
    f32, bf16 = jnp.float32, jnp.bfloat16
    upto = lax.broadcasted_iota(jnp.int32, (span, span), 0)
    upto = (upto <= lax.broadcasted_iota(jnp.int32, (span, span), 1)).astype(f32).astype(bf16)
    base = lax.broadcasted_iota(jnp.int32, (bins, span), 0).astype(f32) * per_bin - 1.0
    row_of = lax.broadcasted_iota(jnp.int32, (rows, span), 0)
    lane_of = lax.broadcasted_iota(jnp.int32, (LANES, span), 0)
    place = lax.broadcasted_iota(jnp.int32, (rows, span), 1).astype(f32)
    high = jnp.zeros((rows, LANES), f32)
    low = jnp.zeros((rows, LANES), f32)
    for chunk in range(pixels // span):
        one_hot = members[:, chunk * span : (chunk + 1) * span].astype(f32)
        seen = jnp.dot(one_hot.astype(bf16), upto, preferred_element_type=f32)
        slot = jnp.sum(one_hot * (seen + base), axis=0, keepdims=True).astype(jnp.int32)
        base = base + jnp.sum(one_hot, axis=1, keepdims=True)
        in_row = row_of == jnp.broadcast_to(slot // LANES, (rows, span))
        in_lane = lane_of == jnp.broadcast_to(slot % LANES, (LANES, span))
        in_lane = in_lane.astype(f32).astype(bf16)
        lows = jnp.where(in_row, place, 0.0).astype(bf16)
        highs = jnp.where(in_row, float(chunk), 0.0).astype(bf16)
        both = (((1,), (1,)), ((), ()))
        low += lax.dot_general(lows, in_lane, both, preferred_element_type=f32)
        high += lax.dot_general(highs, in_lane, both, preferred_element_type=f32)
    order[...] = (high * span + low).astype(jnp.int32)


def pixel_order(membership):
    pixels = membership.shape[1]
    vmem = pl.BlockSpec(memory_space=pltpu.VMEM)
    table = pl.pallas_call(
        order_kernel,
        out_shape=jax.ShapeDtypeStruct((pixels // LANES, LANES), jnp.int32),
        in_specs=[vmem],
        out_specs=vmem,
    )(membership)
    return table.reshape(pixels)


def turn_kernel(raw, dark, flat, members, turned, sums):
    @pl.when(pl.program_id(0) == 0)
    def _():
        sums[...] = jnp.zeros_like(sums)

    intensity = (raw[...].astype(jnp.float32) - dark[...]) * flat[...]
    lines = intensity.T
    turned[...] = lines
    sums[...] += jnp.dot(
        members[...].astype(jnp.float32),
        lines,
        precision=lax.Precision.HIGHEST,
        preferred_element_type=jnp.float32,
    )


def turn(raw_frames, dark_frame, flat_field, membership):
    frames, pixels = raw_frames.shape
    bins = membership.shape[0]
    chunk = pixels // bins
    return pl.pallas_call(
        turn_kernel,
        out_shape=(
            jax.ShapeDtypeStruct((pixels, frames), jnp.float32),
            jax.ShapeDtypeStruct((bins, frames), jnp.float32),
        ),
        grid=(pixels // chunk,),
        in_specs=[
            pl.BlockSpec((frames, chunk), lambda i: (0, i)),
            pl.BlockSpec((1, chunk), lambda i: (0, i)),
            pl.BlockSpec((1, chunk), lambda i: (0, i)),
            pl.BlockSpec((bins, chunk), lambda i: (0, i)),
        ],
        out_specs=(
            pl.BlockSpec((chunk, frames), lambda i: (i, 0)),
            pl.BlockSpec((bins, frames), lambda i: (0, 0)),
        ),
    )(raw_frames, dark_frame[None, :], flat_field[None, :], membership)


def gram(left, right):
    return lax.dot_general(
        left, right, (((0,), (0,)), ((), ())), preferred_element_type=jnp.float32
    )


def chain_kernel(
    blocks,
    modules,
    order,
    turned,
    sums,
    out,
    all_sums,
    scaled,
    own,
    far,
    near,
    hold,
    staged,
    sum_send,
    sum_recv,
    bin_send,
    bin_recv,
    frame_send,
    frame_recv,
    relay_send,
    relay_recv,
    result_send,
    result_recv,
):
    me = lax.axis_index("frame")
    module = lax.axis_index("module")
    pixels, frames = turned.shape
    bins = sums.shape[0]
    per_bin = pixels // bins
    owned = bins // modules
    even = lax.rem(me, 2) == 0
    odd = lax.rem(me, 2) == 1
    has_down = me >= 2
    has_up = me + 2 < blocks
    mate = me + 1 - 2 * lax.rem(me, 2)
    relayed = blocks == 8
    across = lax.rem(me + 4, 8)
    relaying = (me < 2) | (me >= 6)
    relay_parity = jnp.where(me >= 6, 1 - lax.rem(me, 2), lax.rem(me, 2))
    relay_target = jnp.where(even, 2, 5)

    barrier = pltpu.get_barrier_semaphore()

    def greet(frame, mod):
        pl.semaphore_signal(barrier, inc=1, device_id=(frame, mod), device_id_type=MESH)

    for gap in range(1, modules):
        greet(me, lax.rem(module + gap, modules))
    greet(mate, module)
    if relayed:
        greet(across, module)

    @pl.when(has_down)
    def _():
        greet(me - 2, module)

    @pl.when(has_up)
    def _():
        greet(me + 2, module)

    peers = modules + int(relayed) + has_down.astype(jnp.int32) + has_up.astype(jnp.int32)
    pl.semaphore_wait(barrier, peers)

    def sum_copy(gap):
        return pltpu.make_async_remote_copy(
            src_ref=sums,
            dst_ref=all_sums.at[module],
            send_sem=sum_send.at[gap - 1],
            recv_sem=sum_recv.at[gap - 1],
            device_id=(me, lax.rem(module + gap, modules)),
            device_id_type=MESH,
        )

    for gap in range(1, modules):
        sum_copy(gap).start()
    all_sums[module] = sums[...]
    for gap in range(1, modules):
        sum_copy(gap).wait()
    total = all_sums[0]
    for source in range(1, modules):
        total = total + all_sums[source]
    all_sums[0] = jnp.sqrt(jnp.float32(per_bin * modules)) / total

    half = per_bin // 2
    parts = 2 * modules

    def bin_copy(k, piece):
        gap, part = piece // 2, lax.rem(piece, 2)
        owner = lax.rem(module + gap, modules)
        start = pl.multiple_of(part * half, half)
        landing = pl.multiple_of(module * per_bin + part * half, half)
        return pltpu.make_async_remote_copy(
            src_ref=scaled.at[owner * owned + k, pl.ds(start, half), :],
            dst_ref=own.at[k, pl.ds(landing, half), :],
            send_sem=bin_send.at[k, piece],
            recv_sem=bin_recv.at[k, piece],
            device_id=(me, owner),
            device_id_type=MESH,
        )

    row_index = lax.broadcasted_iota(jnp.int32, (8, frames), 0)

    def fill(label, target, first):
        factor = all_sums[0, pl.ds(label, 1), :]

        def tile(start):
            lines = jnp.broadcast_to(turned[pl.ds(order[start], 1), :], (8, frames))
            for row in range(1, 8):
                line = turned[pl.ds(order[start + row], 1), :]
                lines = jnp.where(row_index == row, line, lines)
            return lines * factor

        def tiles(group, carry):
            start = label * per_bin + group * 16
            both = jnp.concatenate([tile(start), tile(start + 8)], axis=0)
            rows = pl.ds(pl.multiple_of(first + group * 16, 16), 16)
            target[rows, :] = both.astype(jnp.bfloat16)
            return carry

        lax.fori_loop(0, per_bin // 16, tiles, 0, unroll=4)

    def rows_of(j):
        source = lax.rem(module + modules - j // 2, modules)
        return pl.ds(pl.multiple_of(source * per_bin + lax.rem(j, 2) * half, half), half)

    def frame_copy(k, j, slot, target, frame):
        return pltpu.make_async_remote_copy(
            src_ref=own.at[k, rows_of(j), :],
            dst_ref=target.at[k, rows_of(j), :],
            send_sem=frame_send.at[slot, k, j],
            recv_sem=frame_recv.at[slot, k, j],
            device_id=(frame, module),
            device_id_type=MESH,
        )

    def far_copy(k, j):
        return frame_copy(k, j, 0, far, jnp.where(even, me - 2, me + 2))

    def mate_copy(k, j):
        return frame_copy(k, j, 1, near, mate)

    def entry_copy(k, j):
        straight = jnp.where(even, me + 2, me - 2)
        return pltpu.make_async_remote_copy(
            src_ref=own.at[k, rows_of(j), :],
            dst_ref=hold.at[k, rows_of(j), :],
            send_sem=frame_send.at[0, k, j],
            recv_sem=relay_recv.at[k, j],
            device_id=(jnp.where(lax.rem(k, 2) == 0, across, straight), module),
            device_id_type=MESH,
        )

    def exit_copy(k, j):
        return pltpu.make_async_remote_copy(
            src_ref=hold.at[k, rows_of(j), :],
            dst_ref=far.at[k, rows_of(j), :],
            send_sem=relay_send.at[k, j],
            recv_sem=frame_recv.at[0, k, j],
            device_id=(relay_target, module),
            device_id_type=MESH,
        )

    sends_far = (even & has_down) | (odd & has_up)
    diagonal = ((me == 3) | (me == 4)) if relayed else None

    def result_copy(k, stage, place, frame):
        return pltpu.make_async_remote_copy(
            src_ref=staged.at[stage, k],
            dst_ref=out.at[k, place],
            send_sem=result_send.at[stage, k],
            recv_sem=result_recv.at[place, k],
            device_id=(frame, module),
            device_id_type=MESH,
        )

    def pass_on(k, j):
        @pl.when(odd)
        def _():
            mate_copy(k, j).start()

        if relayed:
            @pl.when(diagonal)
            def _():
                entry_copy(k, j).start()

            @pl.when(sends_far & jnp.logical_not(diagonal))
            def _():
                far_copy(k, j).start()
        else:
            @pl.when(sends_far)
            def _():
                far_copy(k, j).start()

    def relay(k, j):
        if relayed:
            @pl.when(relaying & (lax.rem(k, 2) == relay_parity))
            def _():
                entry_copy(k, j).wait_recv()
                exit_copy(k, j).start()

    def await_frames(k, copy):
        for j in range(parts):
            copy(k, j).wait_recv()

    def correlate(k):
        out[k, 2] = gram(own[k], own[k])

        @pl.when(even)
        def _():
            await_frames(k, mate_copy)
            staged[0, k] = gram(near[k], own[k])
            result_copy(k, 0, 1, me + 1).start()
            out[k, 3] = gram(own[k], near[k])

        @pl.when(even & has_up)
        def _():
            await_frames(k, far_copy)
            staged[1, k] = gram(far[k], own[k])
            result_copy(k, 1, 0, me + 2).start()
            staged[2, k] = gram(far[k], near[k])
            result_copy(k, 2, 1, me + 2).start()
            staged[3, k] = gram(near[k], far[k])
            result_copy(k, 3, 3, me + 1).start()
            out[k, 4] = gram(own[k], far[k])

        @pl.when(odd & has_down)
        def _():
            await_frames(k, far_copy)
            staged[0, k] = gram(far[k], own[k])
            result_copy(k, 0, 4, me - 2).start()
            out[k, 0] = gram(own[k], far[k])

    @pl.loop(0, owned)
    def _(k):
        @pl.loop(1, modules)
        def _(gap):
            label = lax.rem(module + gap, modules) * owned + k
            fill(label, scaled.at[label], 0)
            bin_copy(k, 2 * gap).start()
            bin_copy(k, 2 * gap + 1).start()

        fill(module * owned + k, own.at[k], module * per_bin)
        pass_on(k, 0)
        pass_on(k, 1)

    @pl.loop(0, owned)
    def _(k):
        relay(k, 0)
        relay(k, 1)

    def receive(k, gaps):
        pieces = [2 * gap + part for gap in gaps for part in range(2)]
        for index, piece in enumerate(pieces):
            bin_copy(k, piece).wait()
            pass_on(k, piece)
            if index:
                relay(k, pieces[index - 1])
        relay(k, pieces[-1])

    @pl.loop(0, owned + 1)
    def _(turn_index):
        @pl.when(turn_index < owned)
        def _():
            receive(turn_index, range(1, modules))

        @pl.when(turn_index >= 1)
        def _():
            correlate(turn_index - 1)

    @pl.when(me < 2)
    def _():
        out[:, 0] = jnp.zeros_like(out[:, 0])

    @pl.when(me < 1)
    def _():
        out[:, 1] = jnp.zeros_like(out[:, 1])

    @pl.when(me + 1 >= blocks)
    def _():
        out[:, 3] = jnp.zeros_like(out[:, 3])

    @pl.when(me + 2 >= blocks)
    def _():
        out[:, 4] = jnp.zeros_like(out[:, 4])

    @pl.loop(0, owned)
    def _(k):
        @pl.when(even & has_down)
        def _():
            result_copy(k, 1, 0, me).wait_recv()
            result_copy(k, 2, 1, me).wait_recv()

        @pl.when(odd)
        def _():
            for j in range(parts):
                mate_copy(k, j).wait_send()
            result_copy(k, 0, 1, me).wait_recv()

        @pl.when(sends_far)
        def _():
            for j in range(parts):
                far_copy(k, j).wait_send()

        @pl.when(odd & has_up)
        def _():
            result_copy(k, 3, 3, me).wait_recv()
            result_copy(k, 0, 4, me).wait_recv()

        if relayed:
            @pl.when(relaying & (lax.rem(k, 2) == relay_parity))
            def _():
                for j in range(parts):
                    exit_copy(k, j).wait_send()

        @pl.when(even)
        def _():
            result_copy(k, 0, 1, me + 1).wait_send()

        @pl.when(even & has_up)
        def _():
            result_copy(k, 1, 0, me + 2).wait_send()
            result_copy(k, 2, 1, me + 2).wait_send()
            result_copy(k, 3, 3, me + 1).wait_send()

        @pl.when(odd & has_down)
        def _():
            result_copy(k, 0, 4, me - 2).wait_send()


def correlate_chain(order, turned, sums):
    (pixels, frames), bins = turned.shape, sums.shape[0]
    per_bin = pixels // bins
    blocks, modules = lax.axis_size("frame"), lax.axis_size("module")
    owned = bins // modules
    gathered = per_bin * modules
    vmem = pl.BlockSpec(memory_space=pltpu.VMEM)
    dma = pltpu.SemaphoreType.DMA
    return pl.pallas_call(
        functools.partial(chain_kernel, blocks, modules),
        out_shape=jax.ShapeDtypeStruct((owned, 5, frames, frames), jnp.float32),
        in_specs=[pl.BlockSpec(memory_space=pltpu.SMEM), vmem, vmem],
        out_specs=vmem,
        scratch_shapes=[
            pltpu.VMEM((modules, bins, frames), jnp.float32),
            pltpu.VMEM((bins, per_bin, frames), jnp.bfloat16),
            pltpu.VMEM((owned, gathered, frames), jnp.bfloat16),
            pltpu.VMEM((owned, gathered, frames), jnp.bfloat16),
            pltpu.VMEM((owned, gathered, frames), jnp.bfloat16),
            pltpu.VMEM((owned, gathered, frames), jnp.bfloat16),
            pltpu.VMEM((4, owned, frames, frames), jnp.float32),
            dma((modules - 1,)),
            dma((modules - 1,)),
            dma((owned, 2 * modules)),
            dma((owned, 2 * modules)),
            dma((2, owned, 2 * modules)),
            dma((2, owned, 2 * modules)),
            dma((owned, 2 * modules)),
            dma((owned, 2 * modules)),
            dma((4, owned)),
            dma((5, owned)),
        ],
        compiler_params=pltpu.CompilerParams(
            collective_id=0, has_side_effects=True, vmem_limit_bytes=VMEM_BYTES
        ),
    )(order, turned, sums)


def square_kernel(
    modules,
    order,
    raw,
    dark,
    flat,
    out,
    counts_in,
    turned,
    packed,
    own,
    near,
    first,
    second,
    third,
    staged,
    raw_sem,
    bin_send,
    bin_recv,
    frame_send,
    frame_recv,
    result_send,
    result_recv,
):
    me = lax.axis_index("frame")
    module = lax.axis_index("module")
    pixels, frames = turned.shape
    bins = packed.shape[0]
    per_bin = pixels // bins
    owned = bins // modules
    gathered = per_bin * modules
    half = per_bin // 2
    parts = 2 * modules

    side = me // 4
    sign = 1 - 2 * side

    def flip(block):
        return jnp.where(side == 1, 7 - block, block)

    role = flip(me)
    mate = me + 1 - 2 * lax.rem(me, 2)
    is_one, is_two, is_three = role == 1, role == 2, role == 3

    def place(gap):
        return 2 + sign * gap

    barrier = pltpu.get_barrier_semaphore()

    def greet(frame, mod):
        pl.semaphore_signal(barrier, inc=1, device_id=(frame, mod), device_id_type=MESH)

    for gap in range(1, modules):
        greet(me, lax.rem(module + gap, modules))
    greet(mate, module)

    @pl.when(is_one)
    def _():
        greet(flip(2), module)
        greet(flip(3), module)
        greet(flip(4), module)

    @pl.when(is_two | is_three)
    def _():
        greet(flip(1), module)

    @pl.when(is_three)
    def _():
        greet(flip(6), module)

    slab = counts_in.shape[2]
    slabs = pixels // slab

    def load(index):
        start = pl.multiple_of(index * slab, slab)
        slot = lax.rem(index, 2)
        return pltpu.make_async_copy(
            raw.at[:, pl.ds(start, slab)], counts_in.at[slot], raw_sem.at[slot]
        )

    load(0).start()
    load(1).start()

    @pl.loop(0, slabs)
    def _(index):
        load(index).wait()
        start = pl.multiple_of(index * slab, slab)
        columns = pl.ds(start, slab)
        raw_counts = counts_in[lax.rem(index, 2)].astype(jnp.float32)
        turned[columns, :] = ((raw_counts - dark[:, columns]) * flat[:, columns]).T

        @pl.when(index + 2 < slabs)
        def _():
            load(index + 2).start()

    peers = modules + jnp.where(is_one, 3, jnp.where(is_three, 2, jnp.where(is_two, 1, 0)))
    pl.semaphore_wait(barrier, peers)

    row_index = lax.broadcasted_iota(jnp.int32, (8, frames), 0)

    def fill(label, target, first_row):
        def tile(start):
            lines = jnp.broadcast_to(turned[pl.ds(order[start], 1), :], (8, frames))
            for row in range(1, 8):
                line = turned[pl.ds(order[start + row], 1), :]
                lines = jnp.where(row_index == row, line, lines)
            return lines

        def tiles(group, carry):
            start = label * per_bin + group * 16
            both = jnp.concatenate([tile(start), tile(start + 8)], axis=0)
            rows = pl.ds(pl.multiple_of(first_row + group * 16, 16), 16)
            target[rows, :] = both.astype(jnp.bfloat16)
            return carry

        lax.fori_loop(0, per_bin // 16, tiles, 0, unroll=4)

    def bin_copy(k, piece):
        gap, part = piece // 2, lax.rem(piece, 2)
        owner = lax.rem(module + gap, modules)
        start = pl.multiple_of(part * half, half)
        landing = pl.multiple_of(module * per_bin + part * half, half)
        return pltpu.make_async_remote_copy(
            src_ref=packed.at[owner * owned + k, pl.ds(start, half), :],
            dst_ref=own.at[k, pl.ds(landing, half), :],
            send_sem=bin_send.at[k, piece],
            recv_sem=bin_recv.at[k, piece],
            device_id=(me, owner),
            device_id_type=MESH,
        )

    def rows_of(j):
        source = lax.rem(module + modules - j // 2, modules)
        return pl.ds(pl.multiple_of(source * per_bin + lax.rem(j, 2) * half, half), half)

    def frame_copy(flow, k, j, target, frame):
        return pltpu.make_async_remote_copy(
            src_ref=own.at[k, rows_of(j), :],
            dst_ref=target.at[rows_of(j), :],
            send_sem=frame_send.at[flow, k, j],
            recv_sem=frame_recv.at[flow, k, j],
            device_id=(frame, module),
            device_id_type=MESH,
        )

    def near_copy(k, j):
        return frame_copy(0, k, j, near.at[k], mate)

    def first_copy(k, j):
        return frame_copy(1, k, j, first.at[k], jnp.where(is_one, flip(3), flip(1)))

    def second_copy(k, j):
        return frame_copy(2, k, j, second.at[k], flip(6))

    def third_copy(k, j):
        return frame_copy(3, k, j, third.at[k // 2], flip(1))

    def shared(k):
        return lax.rem(k, 2) == side

    def pass_on(k, j):
        @pl.when(is_one | is_two)
        def _():
            first_copy(k, j).start()

        @pl.when(is_three)
        def _():
            second_copy(k, j).start()

        @pl.when(is_three & shared(k))
        def _():
            third_copy(k, j).start()

        near_copy(k, j).start()

    def result_copy(k, stage, spot, frame):
        return pltpu.make_async_remote_copy(
            src_ref=staged.at[stage, k],
            dst_ref=out.at[k, spot],
            send_sem=result_send.at[stage, k],
            recv_sem=result_recv.at[spot, k],
            device_id=(frame, module),
            device_id_type=MESH,
        )

    one_results = ((2, 0), (2, 4), (4, 2), (0, 2), (3, 4), (4, 3))
    three_results = ((1, 3), (2, 1))

    def result_of(k, stage, pair):
        return result_copy(k, stage, place(pair[1] - pair[0]), flip(pair[0]))

    def scale_of(block):
        down = jnp.ones((8, gathered), jnp.bfloat16)
        across = jnp.ones((gathered, LANES), jnp.bfloat16)
        root = jnp.sqrt(jnp.float32(gathered))
        row = jnp.dot(down, block, preferred_element_type=jnp.float32)[:1]
        column = gram(block, across)
        column = jnp.concatenate([column] * (frames // LANES), axis=1)
        return root / column, root / row

    def await_frames(k, copy):
        for j in range(parts):
            copy(k, j).wait_recv()

    def correlate(k):
        scales = {0: scale_of(own[k])}
        out[k, 2] = gram(own[k], own[k]) * scales[0][0] * scales[0][1]
        await_frames(k, near_copy)
        near_scale = scale_of(near[k])
        own_scale = scales[0]
        out[k, mate - me + 2] = gram(own[k], near[k]) * own_scale[0] * near_scale[1]

        @pl.when(is_three)
        def _():
            await_frames(k, first_copy)
            scale = scale_of(first[k])
            staged[0, k] = gram(first[k], own[k]) * scale[0] * own_scale[1]
            result_of(k, 0, three_results[0]).start()
            staged[1, k] = gram(near[k], first[k]) * near_scale[0] * scale[1]
            result_of(k, 1, three_results[1]).start()
            out[k, place(-2)] = gram(own[k], first[k]) * own_scale[0] * scale[1]

        @pl.when(is_one)
        def _():
            await_frames(k, first_copy)
            scale = scale_of(first[k])
            staged[0, k] = gram(first[k], near[k]) * scale[0] * near_scale[1]
            result_of(k, 0, one_results[0]).start()
            await_frames(k, second_copy)
            far_scale = scale_of(second[k])
            staged[1, k] = gram(first[k], second[k]) * scale[0] * far_scale[1]
            result_of(k, 1, one_results[1]).start()
            staged[2, k] = gram(second[k], first[k]) * far_scale[0] * scale[1]
            result_of(k, 2, one_results[2]).start()

            @pl.when(shared(k))
            def _():
                await_frames(k, third_copy)
                block = third.at[k // 2]
                third_scale = scale_of(block[...])
                staged[4, k] = gram(block[...], second[k]) * third_scale[0] * far_scale[1]
                result_of(k, 4, one_results[4]).start()
                staged[5, k] = gram(second[k], block[...]) * far_scale[0] * third_scale[1]
                result_of(k, 5, one_results[5]).start()

            staged[3, k] = gram(near[k], first[k]) * near_scale[0] * scale[1]
            result_of(k, 3, one_results[3]).start()
            out[k, place(1)] = gram(own[k], first[k]) * own_scale[0] * scale[1]

    @pl.loop(0, owned)
    def _(k):
        @pl.loop(1, modules)
        def _(gap):
            label = lax.rem(module + gap, modules) * owned + k
            fill(label, packed.at[label], 0)
            bin_copy(k, 2 * gap).start()
            bin_copy(k, 2 * gap + 1).start()

        fill(module * owned + k, own.at[k], module * per_bin)
        pass_on(k, 0)
        pass_on(k, 1)

    @pl.when(role == 0)
    def _():
        for k in range(owned):
            out[k, place(-1)] = jnp.zeros((frames, frames), jnp.float32)

    @pl.when(role < 2)
    def _():
        for k in range(owned):
            out[k, place(-2)] = jnp.zeros((frames, frames), jnp.float32)

    @pl.loop(0, owned + 1)
    def _(turn_index):
        @pl.when(turn_index < owned)
        def _():
            for piece in range(2, parts):
                bin_copy(turn_index, piece).wait()
                pass_on(turn_index, piece)

        @pl.when(turn_index >= 1)
        def _():
            correlate(turn_index - 1)

    @pl.loop(0, owned)
    def _(k):
        for j in range(parts):
            near_copy(k, j).wait_send()

        @pl.when(is_one | is_two)
        def _():
            for j in range(parts):
                first_copy(k, j).wait_send()

        @pl.when(is_three)
        def _():
            for j in range(parts):
                second_copy(k, j).wait_send()

        @pl.when(is_three & shared(k))
        def _():
            for j in range(parts):
                third_copy(k, j).wait_send()

        @pl.when(is_one)
        def _():
            for stage in range(4):
                result_of(k, stage, one_results[stage]).wait_send()

        @pl.when(is_one & shared(k))
        def _():
            for stage in range(4, 6):
                result_of(k, stage, one_results[stage]).wait_send()

        @pl.when(is_three)
        def _():
            for stage in range(2):
                result_of(k, stage, three_results[stage]).wait_send()

        result_copy(k, 0, place(2), me).wait_recv()

        @pl.when(is_two)
        def _():
            result_copy(k, 0, place(-2), me).wait_recv()
            result_copy(k, 0, place(-1), me).wait_recv()

        @pl.when(is_three)
        def _():
            result_copy(k, 0, place(1), me).wait_recv()


def correlate_square(order, raw_frames, dark_frame, flat_field, bins):
    frames, pixels = raw_frames.shape
    modules = lax.axis_size("module")
    per_bin = pixels // bins
    owned = bins // modules
    gathered = per_bin * modules
    slab = 2 * per_bin
    vmem = pl.BlockSpec(memory_space=pltpu.VMEM)
    dma = pltpu.SemaphoreType.DMA
    block = (owned, gathered, frames)
    return pl.pallas_call(
        functools.partial(square_kernel, modules),
        out_shape=jax.ShapeDtypeStruct((owned, 5, frames, frames), jnp.float32),
        in_specs=[
            pl.BlockSpec(memory_space=pltpu.SMEM),
            pl.BlockSpec(memory_space=pl.ANY),
            vmem,
            vmem,
        ],
        out_specs=vmem,
        scratch_shapes=[
            pltpu.VMEM((2, frames, slab), jnp.int32),
            pltpu.VMEM((pixels, frames), jnp.float32),
            pltpu.VMEM((bins, per_bin, frames), jnp.bfloat16),
            pltpu.VMEM(block, jnp.bfloat16),
            pltpu.VMEM(block, jnp.bfloat16),
            pltpu.VMEM(block, jnp.bfloat16),
            pltpu.VMEM(block, jnp.bfloat16),
            pltpu.VMEM((owned // 2, gathered, frames), jnp.bfloat16),
            pltpu.VMEM((6, owned, frames, frames), jnp.float32),
            dma((2,)),
            dma((owned, 2 * modules)),
            dma((owned, 2 * modules)),
            dma((4, owned, 2 * modules)),
            dma((4, owned, 2 * modules)),
            dma((6, owned)),
            dma((5, owned)),
        ],
        compiler_params=pltpu.CompilerParams(
            collective_id=1, has_side_effects=True, vmem_limit_bytes=VMEM_BYTES
        ),
    )(order, raw_frames, dark_frame[None, :], flat_field[None, :])


def per_device(raw_frames, dark_frame, flat_field, membership):
    order = pixel_order(membership)
    if lax.axis_size("frame") == 8:
        bins = membership.shape[0]
        result = correlate_square(order, raw_frames, dark_frame, flat_field, bins)
    else:
        turned, sums = turn(raw_frames, dark_frame, flat_field, membership)
        result = correlate_chain(order, turned, sums)
    return result[:, None]


def solution(mesh):
    in_specs = (P("frame", "module"), P("module"), P("module"), P(None, "module"))
    out_specs = P("module", "frame", None, None, None)
    return jax.shard_map(
        per_device, mesh=mesh, in_specs=in_specs, out_specs=out_specs, check_vma=False
    )
```

```python
import functools

import jax
import jax.numpy as jnp
from jax import lax
from jax.experimental import pallas as pl
from jax.experimental.pallas import tpu as pltpu
from jax.sharding import PartitionSpec as P

MESH = pl.DeviceIdType.MESH
VMEM_BYTES = 60 * 1024 * 1024
SQUARE_BYTES = 57 * 1024 * 1024
LANES = 128
SEND_ORDER = ((3, 2, 1), (2, 3, 0), (1, 0, 3), (0, 1, 2))
TAKE_ORDER = ((1, 3, 2), (0, 2, 3), (3, 1, 0), (2, 0, 1))


def sort_pixels(members, lows_highs, lanes):
    bins, pixels = members.shape
    per_bin = pixels // bins
    span = 2 * LANES
    rows = pixels // LANES
    f32, bf16 = jnp.float32, jnp.bfloat16
    shape = (span, span + LANES)
    upto = lax.broadcasted_iota(jnp.int32, shape, 0) <= lax.broadcasted_iota(jnp.int32, shape, 1)
    upto = upto.astype(f32).astype(bf16)
    base = lax.broadcasted_iota(jnp.int32, (bins, span), 0).astype(f32) * per_bin - 1.0
    row_of = lax.broadcasted_iota(jnp.int32, (rows, span), 0)
    lane_of = lax.broadcasted_iota(jnp.int32, (LANES, span), 0)
    place = lax.broadcasted_iota(jnp.int32, (rows, span), 1).astype(f32)
    for chunk in range(pixels // span):
        columns = slice(chunk * span, (chunk + 1) * span)
        one_hot = members[:, columns].astype(f32)
        seen = jnp.dot(one_hot.astype(bf16), upto, preferred_element_type=f32)
        slot = one_hot * (seen[:, :span] + base)
        slot = jnp.sum(slot, axis=0, keepdims=True).astype(jnp.int32)
        base = base + jnp.concatenate([seen[:, span:]] * 2, axis=1)
        in_row = row_of == jnp.broadcast_to(slot // LANES, (rows, span))
        in_lane = lane_of == jnp.broadcast_to(slot % LANES, (LANES, span))
        lanes[:, columns] = in_lane.astype(f32).astype(bf16)
        lows_highs[:rows, columns] = jnp.where(in_row, place, 0.0).astype(bf16)
        lows_highs[rows:, columns] = jnp.where(in_row, float(chunk), 0.0).astype(bf16)
    both = (((1,), (1,)), ((), ()))
    table = lax.dot_general(lows_highs[...], lanes[...], both, preferred_element_type=f32)
    table = (table[rows:] * span + table[:rows]).astype(jnp.int32)
    return jnp.clip(table, 0, pixels - 1)


def order_kernel(members, order, lows_highs, lanes):
    order[...] = sort_pixels(members, lows_highs, lanes)


def pixel_order(membership):
    pixels = membership.shape[1]
    vmem = pl.BlockSpec(memory_space=pltpu.VMEM)
    table = pl.pallas_call(
        order_kernel,
        out_shape=jax.ShapeDtypeStruct((pixels // LANES, LANES), jnp.int32),
        in_specs=[vmem],
        out_specs=vmem,
        scratch_shapes=[
            pltpu.VMEM((2 * pixels // LANES, pixels), jnp.bfloat16),
            pltpu.VMEM((LANES, pixels), jnp.bfloat16),
        ],
    )(membership)
    return table.reshape(pixels)


def turn_kernel(raw, dark, flat, members, turned, sums):
    @pl.when(pl.program_id(0) == 0)
    def _():
        sums[...] = jnp.zeros_like(sums)

    intensity = (raw[...].astype(jnp.float32) - dark[...]) * flat[...]
    lines = intensity.T
    turned[...] = lines
    sums[...] += jnp.dot(
        members[...].astype(jnp.float32),
        lines,
        precision=lax.Precision.HIGHEST,
        preferred_element_type=jnp.float32,
    )


def turn(raw_frames, dark_frame, flat_field, membership):
    frames, pixels = raw_frames.shape
    bins = membership.shape[0]
    chunk = pixels // bins
    return pl.pallas_call(
        turn_kernel,
        out_shape=(
            jax.ShapeDtypeStruct((pixels, frames), jnp.float32),
            jax.ShapeDtypeStruct((bins, frames), jnp.float32),
        ),
        grid=(pixels // chunk,),
        in_specs=[
            pl.BlockSpec((frames, chunk), lambda i: (0, i)),
            pl.BlockSpec((1, chunk), lambda i: (0, i)),
            pl.BlockSpec((1, chunk), lambda i: (0, i)),
            pl.BlockSpec((bins, chunk), lambda i: (0, i)),
        ],
        out_specs=(
            pl.BlockSpec((chunk, frames), lambda i: (i, 0)),
            pl.BlockSpec((bins, frames), lambda i: (0, 0)),
        ),
    )(raw_frames, dark_frame[None, :], flat_field[None, :], membership)


def gram(left, right):
    return lax.dot_general(
        left, right, (((0,), (0,)), ((), ())), preferred_element_type=jnp.float32
    )


def chain_kernel(
    blocks,
    modules,
    order,
    turned,
    sums,
    out,
    all_sums,
    scaled,
    own,
    far,
    near,
    hold,
    staged,
    sum_send,
    sum_recv,
    bin_send,
    bin_recv,
    frame_send,
    frame_recv,
    relay_send,
    relay_recv,
    result_send,
    result_recv,
):
    me = lax.axis_index("frame")
    module = lax.axis_index("module")
    pixels, frames = turned.shape
    bins = sums.shape[0]
    per_bin = pixels // bins
    owned = bins // modules
    even = lax.rem(me, 2) == 0
    odd = lax.rem(me, 2) == 1
    has_down = me >= 2
    has_up = me + 2 < blocks
    mate = me + 1 - 2 * lax.rem(me, 2)
    relayed = blocks == 8
    across = lax.rem(me + 4, 8)
    relaying = (me < 2) | (me >= 6)
    relay_parity = jnp.where(me >= 6, 1 - lax.rem(me, 2), lax.rem(me, 2))
    relay_target = jnp.where(even, 2, 5)

    barrier = pltpu.get_barrier_semaphore()

    def greet(frame, mod):
        pl.semaphore_signal(barrier, inc=1, device_id=(frame, mod), device_id_type=MESH)

    for gap in range(1, modules):
        greet(me, lax.rem(module + gap, modules))
    greet(mate, module)
    if relayed:
        greet(across, module)

    @pl.when(has_down)
    def _():
        greet(me - 2, module)

    @pl.when(has_up)
    def _():
        greet(me + 2, module)

    peers = modules + int(relayed) + has_down.astype(jnp.int32) + has_up.astype(jnp.int32)
    pl.semaphore_wait(barrier, peers)

    def sum_copy(gap):
        return pltpu.make_async_remote_copy(
            src_ref=sums,
            dst_ref=all_sums.at[module],
            send_sem=sum_send.at[gap - 1],
            recv_sem=sum_recv.at[gap - 1],
            device_id=(me, lax.rem(module + gap, modules)),
            device_id_type=MESH,
        )

    for gap in range(1, modules):
        sum_copy(gap).start()
    all_sums[module] = sums[...]
    for gap in range(1, modules):
        sum_copy(gap).wait()
    total = all_sums[0]
    for source in range(1, modules):
        total = total + all_sums[source]
    all_sums[0] = jnp.sqrt(jnp.float32(per_bin * modules)) / total

    half = per_bin // 2
    parts = 2 * modules

    def bin_copy(k, piece):
        gap, part = piece // 2, lax.rem(piece, 2)
        owner = lax.rem(module + gap, modules)
        start = pl.multiple_of(part * half, half)
        landing = pl.multiple_of(module * per_bin + part * half, half)
        return pltpu.make_async_remote_copy(
            src_ref=scaled.at[owner * owned + k, pl.ds(start, half), :],
            dst_ref=own.at[k, pl.ds(landing, half), :],
            send_sem=bin_send.at[k, piece],
            recv_sem=bin_recv.at[k, piece],
            device_id=(me, owner),
            device_id_type=MESH,
        )

    row_index = lax.broadcasted_iota(jnp.int32, (8, frames), 0)

    def fill(label, target, first):
        factor = all_sums[0, pl.ds(label, 1), :]

        def tile(start):
            lines = jnp.broadcast_to(turned[pl.ds(order[start], 1), :], (8, frames))
            for row in range(1, 8):
                line = turned[pl.ds(order[start + row], 1), :]
                lines = jnp.where(row_index == row, line, lines)
            return lines * factor

        def tiles(group, carry):
            start = label * per_bin + group * 16
            both = jnp.concatenate([tile(start), tile(start + 8)], axis=0)
            rows = pl.ds(pl.multiple_of(first + group * 16, 16), 16)
            target[rows, :] = both.astype(jnp.bfloat16)
            return carry

        lax.fori_loop(0, per_bin // 16, tiles, 0, unroll=4)

    def rows_of(j):
        source = lax.rem(module + modules - j // 2, modules)
        return pl.ds(pl.multiple_of(source * per_bin + lax.rem(j, 2) * half, half), half)

    def frame_copy(k, j, slot, target, frame):
        return pltpu.make_async_remote_copy(
            src_ref=own.at[k, rows_of(j), :],
            dst_ref=target.at[k, rows_of(j), :],
            send_sem=frame_send.at[slot, k, j],
            recv_sem=frame_recv.at[slot, k, j],
            device_id=(frame, module),
            device_id_type=MESH,
        )

    def far_copy(k, j):
        return frame_copy(k, j, 0, far, jnp.where(even, me - 2, me + 2))

    def mate_copy(k, j):
        return frame_copy(k, j, 1, near, mate)

    def entry_copy(k, j):
        straight = jnp.where(even, me + 2, me - 2)
        return pltpu.make_async_remote_copy(
            src_ref=own.at[k, rows_of(j), :],
            dst_ref=hold.at[k, rows_of(j), :],
            send_sem=frame_send.at[0, k, j],
            recv_sem=relay_recv.at[k, j],
            device_id=(jnp.where(lax.rem(k, 2) == 0, across, straight), module),
            device_id_type=MESH,
        )

    def exit_copy(k, j):
        return pltpu.make_async_remote_copy(
            src_ref=hold.at[k, rows_of(j), :],
            dst_ref=far.at[k, rows_of(j), :],
            send_sem=relay_send.at[k, j],
            recv_sem=frame_recv.at[0, k, j],
            device_id=(relay_target, module),
            device_id_type=MESH,
        )

    sends_far = (even & has_down) | (odd & has_up)
    diagonal = ((me == 3) | (me == 4)) if relayed else None

    def result_copy(k, stage, place, frame):
        return pltpu.make_async_remote_copy(
            src_ref=staged.at[stage, k],
            dst_ref=out.at[k, place],
            send_sem=result_send.at[stage, k],
            recv_sem=result_recv.at[place, k],
            device_id=(frame, module),
            device_id_type=MESH,
        )

    def pass_on(k, j):
        @pl.when(odd)
        def _():
            mate_copy(k, j).start()

        if relayed:
            @pl.when(diagonal)
            def _():
                entry_copy(k, j).start()

            @pl.when(sends_far & jnp.logical_not(diagonal))
            def _():
                far_copy(k, j).start()
        else:
            @pl.when(sends_far)
            def _():
                far_copy(k, j).start()

    def relay(k, j):
        if relayed:
            @pl.when(relaying & (lax.rem(k, 2) == relay_parity))
            def _():
                entry_copy(k, j).wait_recv()
                exit_copy(k, j).start()

    def await_frames(k, copy):
        for j in range(parts):
            copy(k, j).wait_recv()

    def correlate(k):
        out[k, 2] = gram(own[k], own[k])

        @pl.when(even)
        def _():
            await_frames(k, mate_copy)
            staged[0, k] = gram(near[k], own[k])
            result_copy(k, 0, 1, me + 1).start()
            out[k, 3] = gram(own[k], near[k])

        @pl.when(even & has_up)
        def _():
            await_frames(k, far_copy)
            staged[1, k] = gram(far[k], own[k])
            result_copy(k, 1, 0, me + 2).start()
            staged[2, k] = gram(far[k], near[k])
            result_copy(k, 2, 1, me + 2).start()
            staged[3, k] = gram(near[k], far[k])
            result_copy(k, 3, 3, me + 1).start()
            out[k, 4] = gram(own[k], far[k])

        @pl.when(odd & has_down)
        def _():
            await_frames(k, far_copy)
            staged[0, k] = gram(far[k], own[k])
            result_copy(k, 0, 4, me - 2).start()
            out[k, 0] = gram(own[k], far[k])

    @pl.loop(0, owned)
    def _(k):
        @pl.loop(1, modules)
        def _(gap):
            label = lax.rem(module + gap, modules) * owned + k
            fill(label, scaled.at[label], 0)
            bin_copy(k, 2 * gap).start()
            bin_copy(k, 2 * gap + 1).start()

        fill(module * owned + k, own.at[k], module * per_bin)
        pass_on(k, 0)
        pass_on(k, 1)

    @pl.loop(0, owned)
    def _(k):
        relay(k, 0)
        relay(k, 1)

    def receive(k, gaps):
        pieces = [2 * gap + part for gap in gaps for part in range(2)]
        for index, piece in enumerate(pieces):
            bin_copy(k, piece).wait()
            pass_on(k, piece)
            if index:
                relay(k, pieces[index - 1])
        relay(k, pieces[-1])

    @pl.loop(0, owned + 1)
    def _(turn_index):
        @pl.when(turn_index < owned)
        def _():
            receive(turn_index, range(1, modules))

        @pl.when(turn_index >= 1)
        def _():
            correlate(turn_index - 1)

    @pl.when(me < 2)
    def _():
        out[:, 0] = jnp.zeros_like(out[:, 0])

    @pl.when(me < 1)
    def _():
        out[:, 1] = jnp.zeros_like(out[:, 1])

    @pl.when(me + 1 >= blocks)
    def _():
        out[:, 3] = jnp.zeros_like(out[:, 3])

    @pl.when(me + 2 >= blocks)
    def _():
        out[:, 4] = jnp.zeros_like(out[:, 4])

    @pl.loop(0, owned)
    def _(k):
        @pl.when(even & has_down)
        def _():
            result_copy(k, 1, 0, me).wait_recv()
            result_copy(k, 2, 1, me).wait_recv()

        @pl.when(odd)
        def _():
            for j in range(parts):
                mate_copy(k, j).wait_send()
            result_copy(k, 0, 1, me).wait_recv()

        @pl.when(sends_far)
        def _():
            for j in range(parts):
                far_copy(k, j).wait_send()

        @pl.when(odd & has_up)
        def _():
            result_copy(k, 3, 3, me).wait_recv()
            result_copy(k, 0, 4, me).wait_recv()

        if relayed:
            @pl.when(relaying & (lax.rem(k, 2) == relay_parity))
            def _():
                for j in range(parts):
                    exit_copy(k, j).wait_send()

        @pl.when(even)
        def _():
            result_copy(k, 0, 1, me + 1).wait_send()

        @pl.when(even & has_up)
        def _():
            result_copy(k, 1, 0, me + 2).wait_send()
            result_copy(k, 2, 1, me + 2).wait_send()
            result_copy(k, 3, 3, me + 1).wait_send()

        @pl.when(odd & has_down)
        def _():
            result_copy(k, 0, 4, me - 2).wait_send()


def correlate_chain(order, turned, sums):
    (pixels, frames), bins = turned.shape, sums.shape[0]
    per_bin = pixels // bins
    blocks, modules = lax.axis_size("frame"), lax.axis_size("module")
    owned = bins // modules
    gathered = per_bin * modules
    vmem = pl.BlockSpec(memory_space=pltpu.VMEM)
    dma = pltpu.SemaphoreType.DMA
    return pl.pallas_call(
        functools.partial(chain_kernel, blocks, modules),
        out_shape=jax.ShapeDtypeStruct((owned, 5, frames, frames), jnp.float32),
        in_specs=[pl.BlockSpec(memory_space=pltpu.SMEM), vmem, vmem],
        out_specs=vmem,
        scratch_shapes=[
            pltpu.VMEM((modules, bins, frames), jnp.float32),
            pltpu.VMEM((bins, per_bin, frames), jnp.bfloat16),
            pltpu.VMEM((owned, gathered, frames), jnp.bfloat16),
            pltpu.VMEM((owned, gathered, frames), jnp.bfloat16),
            pltpu.VMEM((owned, gathered, frames), jnp.bfloat16),
            pltpu.VMEM((owned, gathered, frames), jnp.bfloat16),
            pltpu.VMEM((4, owned, frames, frames), jnp.float32),
            dma((modules - 1,)),
            dma((modules - 1,)),
            dma((owned, 2 * modules)),
            dma((owned, 2 * modules)),
            dma((2, owned, 2 * modules)),
            dma((2, owned, 2 * modules)),
            dma((owned, 2 * modules)),
            dma((owned, 2 * modules)),
            dma((4, owned)),
            dma((5, owned)),
        ],
        compiler_params=pltpu.CompilerParams(
            collective_id=0, has_side_effects=True, vmem_limit_bytes=VMEM_BYTES
        ),
    )(order, turned, sums)


def square_kernel(
    modules,
    raw,
    dark_frame,
    flat_field,
    membership,
    total,
    dark,
    flat,
    members,
    lows_highs,
    lanes,
    table,
    order,
    counts_in,
    turned,
    sums,
    all_sums,
    packed,
    own,
    near,
    first,
    second,
    third,
    direct,
    coded,
    coded_peak,
    landed,
    landed_peak,
    raw_sem,
    order_sem,
    sum_send,
    sum_recv,
    bin_send,
    bin_recv,
    frame_send,
    frame_recv,
    direct_send,
    direct_recv,
    coded_send,
    coded_recv,
):
    me = lax.axis_index("frame")
    module = lax.axis_index("module")
    pixels, frames = turned.shape
    bins = packed.shape[0]
    per_bin = pixels // bins
    owned = bins // modules
    gathered = per_bin * modules
    half = per_bin // 2
    parts = 2 * modules
    f32, bf16 = jnp.float32, jnp.bfloat16

    send_order, take_order = SEND_ORDER, TAKE_ORDER
    if modules != 4:
        send_order = [[(m + gap) % modules for gap in range(1, modules)] for m in range(modules)]
        take_order = [[(m - gap) % modules for gap in range(1, modules)] for m in range(modules)]

    side = me // 4
    sign = 1 - 2 * side

    def flip(block):
        return jnp.where(side == 1, 7 - block, block)

    role = flip(me)
    mate = me + 1 - 2 * lax.rem(me, 2)
    is_one, is_two, is_three = role == 1, role == 2, role == 3

    def place(gap):
        return 2 + sign * gap

    barrier = pltpu.get_barrier_semaphore()

    def greet(frame, mod):
        pl.semaphore_signal(barrier, inc=1, device_id=(frame, mod), device_id_type=MESH)

    for gap in range(1, modules):
        greet(me, lax.rem(module + gap, modules))
    greet(mate, module)

    @pl.when(is_one)
    def _():
        greet(flip(2), module)
        greet(flip(3), module)
        greet(flip(4), module)

    @pl.when(is_two | is_three)
    def _():
        greet(flip(1), module)

    @pl.when(is_three)
    def _():
        greet(flip(6), module)

    slabs, _, slab = counts_in.shape

    def columns_of(index):
        return pl.ds(pl.multiple_of(index * slab, slab), slab)

    def load(index):
        return pltpu.make_async_copy(
            raw.at[:, columns_of(index)], counts_in.at[index], raw_sem.at[index]
        )

    def intensity(index):
        columns = columns_of(index)
        return (counts_in[index].astype(f32) - dark[:, columns]) * flat[:, columns]

    fetch = pltpu.make_async_copy(membership, members, order_sem.at[0])
    fetch.start()
    fetch_dark = pltpu.make_async_copy(dark_frame, dark, order_sem.at[2])
    fetch_dark.start()
    fetch_flat = pltpu.make_async_copy(flat_field, flat, order_sem.at[3])
    fetch_flat.start()
    sums[...] = jnp.zeros_like(sums)
    fetch.wait()
    for index in range(slabs):
        load(index).start()
    table[...] = sort_pixels(members, lows_highs, lanes)
    spread = pltpu.make_async_copy(table, order, order_sem.at[1])
    spread.start()
    fetch_dark.wait()
    fetch_flat.wait()

    @pl.loop(0, slabs)
    def _(index):
        load(index).wait()
        values = intensity(index)
        high = values.astype(bf16)
        low = (values - high.astype(f32)).astype(bf16)
        one_hot = members[:, columns_of(index)].astype(f32).astype(bf16)
        both = (((1,), (1,)), ((), ()))
        sums[...] += lax.dot_general(
            one_hot, high, both, preferred_element_type=f32
        ) + lax.dot_general(one_hot, low, both, preferred_element_type=f32)

    peers = modules + jnp.where(is_one, 3, jnp.where(is_three, 2, jnp.where(is_two, 1, 0)))
    pl.semaphore_wait(barrier, peers)

    def sum_copy(gap):
        return pltpu.make_async_remote_copy(
            src_ref=sums,
            dst_ref=all_sums.at[module],
            send_sem=sum_send.at[gap - 1],
            recv_sem=sum_recv.at[gap - 1],
            device_id=(me, lax.rem(module + gap, modules)),
            device_id_type=MESH,
        )

    for gap in range(1, modules):
        sum_copy(gap).start()
    all_sums[module] = sums[...]

    @pl.loop(0, slabs)
    def _(index):
        turned[columns_of(index), :] = intensity(index).T

    for gap in range(1, modules):
        sum_copy(gap).wait()
    bin_sums = all_sums[0]
    for source in range(1, modules):
        bin_sums = bin_sums + all_sums[source]
    all_sums[0] = jnp.sqrt(f32(gathered)) / bin_sums

    spread.wait()
    row_index = lax.broadcasted_iota(jnp.int32, (8, frames), 0)

    def fill(label, part, target, first_row):
        factor = all_sums[0, pl.ds(label, 1), :]

        def tile(start):
            line, lane = start // LANES, lax.rem(start, LANES)
            lines = jnp.broadcast_to(turned[pl.ds(order[line, lane], 1), :], (8, frames))
            for row in range(1, 8):
                line_at = turned[pl.ds(order[line, lane + row], 1), :]
                lines = jnp.where(row_index == row, line_at, lines)
            return lines * factor

        def tiles(group, carry):
            start = label * per_bin + part * half + group * 16
            both = jnp.concatenate([tile(start), tile(start + 8)], axis=0)
            rows = pl.ds(pl.multiple_of(first_row + group * 16, 16), 16)
            target[rows, :] = both.astype(bf16)
            return carry

        lax.fori_loop(0, half // 16, tiles, 0, unroll=4)

    def bin_copy(k, piece):
        gap, part = piece // 2, lax.rem(piece, 2)
        owner = lax.rem(module + gap, modules)
        start = pl.multiple_of(part * half, half)
        landing = pl.multiple_of(module * per_bin + part * half, half)
        return pltpu.make_async_remote_copy(
            src_ref=packed.at[owner * owned + k, pl.ds(start, half), :],
            dst_ref=own.at[k, pl.ds(landing, half), :],
            send_sem=bin_send.at[0],
            recv_sem=bin_recv.at[k, piece],
            device_id=(me, owner),
            device_id_type=MESH,
        )

    def rows_of(j):
        source = lax.rem(module + modules - j // 2, modules)
        return pl.ds(pl.multiple_of(source * per_bin + lax.rem(j, 2) * half, half), half)

    def frame_copy(flow, k, j, target, frame):
        return pltpu.make_async_remote_copy(
            src_ref=own.at[k, rows_of(j), :],
            dst_ref=target.at[rows_of(j), :],
            send_sem=frame_send.at[flow],
            recv_sem=frame_recv.at[flow, k],
            device_id=(frame, module),
            device_id_type=MESH,
        )

    def whole_copy(flow, k, source, target, frame):
        return pltpu.make_async_remote_copy(
            src_ref=source,
            dst_ref=target,
            send_sem=frame_send.at[flow],
            recv_sem=frame_recv.at[flow, k],
            device_id=(frame, module),
            device_id_type=MESH,
        )

    def near_copy(k, j):
        return frame_copy(0, k, j, near.at[k], mate)

    def first_copy(k, j):
        return frame_copy(1, k, j, first.at[k], jnp.where(is_one, flip(3), flip(1)))

    def second_copy(k, j):
        return frame_copy(2, k, j, second.at[k], flip(6))

    def third_copy(k, j):
        return frame_copy(3, k, j, third.at[k // 2], flip(1))

    def shared(k):
        return lax.rem(k, 2) == side

    def pass_on(k, j):
        @pl.when(is_one | is_two)
        def _():
            first_copy(k, j).start()

        @pl.when(is_three)
        def _():
            second_copy(k, j).start()

        @pl.when(is_three & shared(k))
        def _():
            third_copy(k, j).start()

        near_copy(k, j).start()

    def pick(table, turn):
        found = turn * 0
        for row, others in enumerate(table):
            for column, other in enumerate(others):
                here = (module == row) & (turn == column)
                found = jnp.where(here, (other - row) % modules, found)
        return found

    def fill_for(k, turn):
        gap = pick(send_order, turn - 1)
        label = lax.rem(module + gap, modules) * owned + k

        @pl.loop(0, 2)
        def _(part):
            fill(label, part, packed.at[label], part * half)
            bin_copy(k, 2 * gap + part).start()

    def fill_own(k):
        @pl.loop(0, 2)
        def _(part):
            first_row = module * per_bin + part * half
            fill(module * owned + k, part, own.at[k], first_row)
            pass_on(k, part)

    one_results = ((2, 0, 1), (2, 4, 0), (4, 2, 0), (3, 4, 1), (4, 3, 1))
    three_results = ((1, 3, 0),)

    def coded_copies(k, stage, slot, frame):
        pairs = ((coded, landed), (coded_peak, landed_peak))
        return [
            pltpu.make_async_remote_copy(
                src_ref=source.at[stage, k],
                dst_ref=target.at[slot, k],
                send_sem=coded_send.at[index],
                recv_sem=coded_recv.at[index, slot, k],
                device_id=(frame, module),
                device_id_type=MESH,
            )
            for index, (source, target) in enumerate(pairs)
        ]

    def send_coded(k, stage, result, values):
        peak = jnp.max(values, axis=0, keepdims=True)
        levels = values * (32767.0 / peak) + 0.5
        coded[stage, k] = levels.astype(jnp.int32).astype(jnp.int16)
        coded_peak[stage, k] = jnp.broadcast_to(peak * (1.0 / 32767.0), (8, frames))
        for copy in coded_copies(k, stage, result[2], flip(result[0])):
            copy.start()

    def decode(k, slot, gap):
        for copy in coded_copies(k, 0, slot, me):
            copy.wait_recv()
        values = landed[slot, k].astype(jnp.int32).astype(f32)
        total[k, place(gap)] = values * landed_peak[slot, k, :1, :]

    def direct_copy(k):
        return pltpu.make_async_remote_copy(
            src_ref=direct.at[k],
            dst_ref=total.at[k, jnp.where(role < 2, place(2), place(-1))],
            send_sem=direct_send.at[0],
            recv_sem=direct_recv.at[k],
            device_id=(mate, module),
            device_id_type=MESH,
        )

    def await_frames(k, flow, target):
        whole_copy(flow, k, own.at[k], target, mate).wait_recv()

    def work(k, step):
        if step == 0:
            await_frames(k, 0, near.at[k])

            @pl.when(is_one)
            def _():
                await_frames(k, 1, first.at[k])
                send_coded(k, 0, one_results[0], gram(first[k], near[k]))

            @pl.when(is_three)
            def _():
                await_frames(k, 1, first.at[k])
                send_coded(k, 0, three_results[0], gram(first[k], own[k]))

        if step == 1:

            @pl.when(is_one)
            def _():
                await_frames(k, 2, second.at[k])
                send_coded(k, 1, one_results[1], gram(first[k], second[k]))

            @pl.when(is_three)
            def _():
                direct[k] = gram(near[k], first[k])
                direct_copy(k).start()

        if step == 2:

            @pl.when(is_one & shared(k))
            def _():
                await_frames(k, 3, third.at[k // 2])
                send_coded(k, 3, one_results[3], gram(third[k // 2], second[k]))

            @pl.when(is_three)
            def _():
                total[k, place(-2)] = gram(own[k], first[k])

        if step == 3:

            @pl.when(is_one)
            def _():
                send_coded(k, 2, one_results[2], gram(second[k], first[k]))

            @pl.when(is_one & shared(k))
            def _():
                send_coded(k, 4, one_results[4], gram(second[k], third[k // 2]))

        if step == 4:

            @pl.when(is_one)
            def _():
                direct[k] = gram(near[k], first[k])
                direct_copy(k).start()
                total[k, place(1)] = gram(own[k], first[k])

        if step == 5:
            total[k, mate - me + 2] = gram(own[k], near[k])
            total[k, 2] = gram(own[k], own[k])

    def finish(k):
        @pl.when((role == 0) | is_two)
        def _():
            direct_copy(k).wait_recv()

        @pl.when(role > 0)
        def _():
            decode(k, 0, 2)

        @pl.when(is_two)
        def _():
            decode(k, 1, -2)

        @pl.when(is_three)
        def _():
            decode(k, 1, 1)

    for k in range(2):
        @pl.loop(1, modules)
        def _(gap):
            fill_for(k, gap)

        fill_own(k)

    @pl.when(role == 0)
    def _():
        for k in range(owned):
            total[k, place(-1)] = jnp.zeros((frames, frames), f32)

    @pl.when(role < 2)
    def _():
        for k in range(owned):
            total[k, place(-2)] = jnp.zeros((frames, frames), f32)

    def take(k, column, part):
        gap = modules - pick(take_order, jnp.int32(column))
        piece = 2 * gap + part
        bin_copy(k, piece).wait_recv()
        pass_on(k, piece)

    take(0, 0, 0)
    take(0, 0, 1)

    @pl.loop(0, owned + 1)
    def _(turn_index):
        for step in range(2, parts):
            column = step // 2 - 1
            taken = turn_index + int(column == 0)

            @pl.when(taken < owned)
            def _():
                take(taken, column, step % 2)

            @pl.when(turn_index + 2 < owned)
            def _():
                if step - 1 < modules:
                    fill_for(turn_index + 2, step - 1)
                elif step - 1 == modules:
                    fill_own(turn_index + 2)

            @pl.when(turn_index >= 1)
            def _():
                work(turn_index - 1, step - 2)

        @pl.when(turn_index >= 2)
        def _():
            finish(turn_index - 2)

    finish(owned - 1)

    sent = packed.at[pl.ds(0, bins - owned)]
    pltpu.make_async_remote_copy(
        src_ref=sent,
        dst_ref=sent,
        send_sem=bin_send.at[0],
        recv_sem=bin_recv.at[0, 0],
        device_id=(mate, module),
        device_id_type=MESH,
    ).wait_send()
    whole_copy(0, 0, own, near, mate).wait_send()

    def await_coded(rows):
        for index, source in enumerate((coded, coded_peak)):
            pltpu.make_async_remote_copy(
                src_ref=source.at[pl.ds(0, rows)],
                dst_ref=source.at[pl.ds(0, rows)],
                send_sem=coded_send.at[index],
                recv_sem=coded_recv.at[index, 0, 0],
                device_id=(mate, module),
                device_id_type=MESH,
            ).wait_send()

    @pl.when(is_one | is_two)
    def _():
        whole_copy(1, 0, own, first, mate).wait_send()

    @pl.when(is_three)
    def _():
        whole_copy(2, 0, own, second, mate).wait_send()
        whole_copy(3, 0, own.at[pl.ds(0, owned // 2)], third, mate).wait_send()
        await_coded(1)

    @pl.when(is_one)
    def _():
        await_coded(4)

    @pl.when(is_one | is_three)
    def _():
        pltpu.make_async_remote_copy(
            src_ref=direct,
            dst_ref=direct,
            send_sem=direct_send.at[0],
            recv_sem=direct_recv.at[0],
            device_id=(mate, module),
            device_id_type=MESH,
        ).wait_send()


def correlate_square(raw_frames, dark_frame, flat_field, membership):
    frames, pixels = raw_frames.shape
    bins = membership.shape[0]
    modules = lax.axis_size("module")
    per_bin = pixels // bins
    owned = bins // modules
    gathered = per_bin * modules
    slab = 2 * per_bin
    vmem = pl.BlockSpec(memory_space=pltpu.VMEM)
    dma = pltpu.SemaphoreType.DMA
    f32, bf16 = jnp.float32, jnp.bfloat16
    block = (owned, gathered, frames)
    return pl.pallas_call(
        functools.partial(square_kernel, modules),
        out_shape=pltpu.VMEM((owned, 5, frames, frames), f32),
        in_specs=[
            pl.BlockSpec(memory_space=pl.ANY),
            pl.BlockSpec(memory_space=pl.ANY),
            pl.BlockSpec(memory_space=pl.ANY),
            pl.BlockSpec(memory_space=pl.ANY),
        ],
        out_specs=vmem,
        scratch_shapes=[
            pltpu.VMEM((1, pixels), f32),
            pltpu.VMEM((1, pixels), f32),
            pltpu.VMEM((bins, pixels), jnp.int32),
            pltpu.VMEM((2 * pixels // LANES, pixels), bf16),
            pltpu.VMEM((LANES, pixels), bf16),
            pltpu.VMEM((pixels // LANES, LANES), jnp.int32),
            pltpu.SMEM((pixels // LANES, LANES), jnp.int32),
            pltpu.VMEM((pixels // slab, frames, slab), jnp.int32),
            pltpu.VMEM((pixels, frames), f32),
            pltpu.VMEM((bins, frames), f32),
            pltpu.VMEM((modules, bins, frames), f32),
            pltpu.VMEM((bins, per_bin, frames), bf16),
            pltpu.VMEM(block, bf16),
            pltpu.VMEM(block, bf16),
            pltpu.VMEM(block, bf16),
            pltpu.VMEM(block, bf16),
            pltpu.VMEM((owned // 2, gathered, frames), bf16),
            pltpu.VMEM((owned, frames, frames), f32),
            pltpu.VMEM((5, owned, frames, frames), jnp.int16),
            pltpu.VMEM((5, owned, 8, frames), f32),
            pltpu.VMEM((2, owned, frames, frames), jnp.int16),
            pltpu.VMEM((2, owned, 8, frames), f32),
            dma((pixels // slab,)),
            dma((4,)),
            dma((modules - 1,)),
            dma((modules - 1,)),
            dma((1,)),
            dma((owned, 2 * modules)),
            dma((4,)),
            dma((4, owned)),
            dma((1,)),
            dma((owned,)),
            dma((2,)),
            dma((2, 2, owned)),
        ],
        compiler_params=pltpu.CompilerParams(
            collective_id=1, has_side_effects=True, vmem_limit_bytes=SQUARE_BYTES
        ),
    )(raw_frames, dark_frame[None, :], flat_field[None, :], membership)


def per_device(raw_frames, dark_frame, flat_field, membership):
    if lax.axis_size("frame") == 8:
        result = correlate_square(raw_frames, dark_frame, flat_field, membership)
    else:
        order = pixel_order(membership)
        turned, sums = turn(raw_frames, dark_frame, flat_field, membership)
        result = correlate_chain(order, turned, sums)
    return result[:, None]


def solution(mesh):
    in_specs = (P("frame", "module"), P("module"), P("module"), P(None, "module"))
    out_specs = P("module", "frame", None, None, None)
    return jax.shard_map(
        per_device, mesh=mesh, in_specs=in_specs, out_specs=out_specs, check_vma=False
    )
```

```python
import functools

import jax
import jax.numpy as jnp
from jax import lax
from jax.experimental import pallas as pl
from jax.experimental.pallas import tpu as pltpu
from jax.sharding import PartitionSpec as P

MESH = pl.DeviceIdType.MESH
VMEM_BYTES = 60 * 1024 * 1024
SQUARE_BYTES = 57 * 1024 * 1024
LANES = 128
SEND_ORDER = ((3, 2, 1), (2, 3, 0), (1, 0, 3), (0, 1, 2))
HEARD = ((1, 3, 2), (0, 3, 2), (3, 0, 1), (2, 0, 1))
END_ARRIVALS = ((0, 0), (0, 1), (1, 0), (1, 1), (0, 2), (2, 0), (2, 1), (3, 0), (3, 1), (1, 2), (2, 2), (3, 2))
MIDDLE_ARRIVALS = ((0, 0), (0, 1), (1, 0), (1, 1), (0, 2), (2, 0), (2, 1), (1, 2), (3, 1), (3, 0), (2, 2), (3, 2))


def sort_pixels(members, lows_highs, lanes):
    bins, pixels = members.shape
    per_bin = pixels // bins
    span = 2 * LANES
    rows = pixels // LANES
    f32, bf16 = jnp.float32, jnp.bfloat16
    shape = (span, span + LANES)
    upto = lax.broadcasted_iota(jnp.int32, shape, 0) <= lax.broadcasted_iota(jnp.int32, shape, 1)
    upto = upto.astype(f32).astype(bf16)
    base = lax.broadcasted_iota(jnp.int32, (bins, span), 0).astype(f32) * per_bin - 1.0
    row_of = lax.broadcasted_iota(jnp.int32, (rows, span), 0)
    lane_of = lax.broadcasted_iota(jnp.int32, (LANES, span), 0)
    place = lax.broadcasted_iota(jnp.int32, (rows, span), 1).astype(f32)
    for chunk in range(pixels // span):
        columns = slice(chunk * span, (chunk + 1) * span)
        one_hot = members[:, columns].astype(f32)
        seen = jnp.dot(one_hot.astype(bf16), upto, preferred_element_type=f32)
        slot = one_hot * (seen[:, :span] + base)
        slot = jnp.sum(slot, axis=0, keepdims=True).astype(jnp.int32)
        base = base + jnp.concatenate([seen[:, span:]] * 2, axis=1)
        in_row = row_of == jnp.broadcast_to(slot // LANES, (rows, span))
        in_lane = lane_of == jnp.broadcast_to(slot % LANES, (LANES, span))
        lanes[:, columns] = in_lane.astype(f32).astype(bf16)
        lows_highs[:rows, columns] = jnp.where(in_row, place, 0.0).astype(bf16)
        lows_highs[rows:, columns] = jnp.where(in_row, float(chunk), 0.0).astype(bf16)
    both = (((1,), (1,)), ((), ()))
    table = lax.dot_general(lows_highs[...], lanes[...], both, preferred_element_type=f32)
    table = (table[rows:] * span + table[:rows]).astype(jnp.int32)
    return jnp.clip(table, 0, pixels - 1)


def order_kernel(members, order, lows_highs, lanes):
    order[...] = sort_pixels(members, lows_highs, lanes)


def pixel_order(membership):
    pixels = membership.shape[1]
    vmem = pl.BlockSpec(memory_space=pltpu.VMEM)
    table = pl.pallas_call(
        order_kernel,
        out_shape=jax.ShapeDtypeStruct((pixels // LANES, LANES), jnp.int32),
        in_specs=[vmem],
        out_specs=vmem,
        scratch_shapes=[
            pltpu.VMEM((2 * pixels // LANES, pixels), jnp.bfloat16),
            pltpu.VMEM((LANES, pixels), jnp.bfloat16),
        ],
    )(membership)
    return table.reshape(pixels)


def turn_kernel(raw, dark, flat, members, turned, sums):
    @pl.when(pl.program_id(0) == 0)
    def _():
        sums[...] = jnp.zeros_like(sums)

    intensity = (raw[...].astype(jnp.float32) - dark[...]) * flat[...]
    lines = intensity.T
    turned[...] = lines
    sums[...] += jnp.dot(
        members[...].astype(jnp.float32),
        lines,
        precision=lax.Precision.HIGHEST,
        preferred_element_type=jnp.float32,
    )


def turn(raw_frames, dark_frame, flat_field, membership):
    frames, pixels = raw_frames.shape
    bins = membership.shape[0]
    chunk = pixels // bins
    return pl.pallas_call(
        turn_kernel,
        out_shape=(
            jax.ShapeDtypeStruct((pixels, frames), jnp.float32),
            jax.ShapeDtypeStruct((bins, frames), jnp.float32),
        ),
        grid=(pixels // chunk,),
        in_specs=[
            pl.BlockSpec((frames, chunk), lambda i: (0, i)),
            pl.BlockSpec((1, chunk), lambda i: (0, i)),
            pl.BlockSpec((1, chunk), lambda i: (0, i)),
            pl.BlockSpec((bins, chunk), lambda i: (0, i)),
        ],
        out_specs=(
            pl.BlockSpec((chunk, frames), lambda i: (i, 0)),
            pl.BlockSpec((bins, frames), lambda i: (0, 0)),
        ),
    )(raw_frames, dark_frame[None, :], flat_field[None, :], membership)


def gram(left, right):
    return lax.dot_general(
        left, right, (((0,), (0,)), ((), ())), preferred_element_type=jnp.float32
    )


def chain_kernel(
    blocks,
    modules,
    order,
    turned,
    sums,
    out,
    all_sums,
    scaled,
    own,
    far,
    near,
    hold,
    staged,
    sum_send,
    sum_recv,
    bin_send,
    bin_recv,
    frame_send,
    frame_recv,
    relay_send,
    relay_recv,
    result_send,
    result_recv,
):
    me = lax.axis_index("frame")
    module = lax.axis_index("module")
    pixels, frames = turned.shape
    bins = sums.shape[0]
    per_bin = pixels // bins
    owned = bins // modules
    even = lax.rem(me, 2) == 0
    odd = lax.rem(me, 2) == 1
    has_down = me >= 2
    has_up = me + 2 < blocks
    mate = me + 1 - 2 * lax.rem(me, 2)
    relayed = blocks == 8
    across = lax.rem(me + 4, 8)
    relaying = (me < 2) | (me >= 6)
    relay_parity = jnp.where(me >= 6, 1 - lax.rem(me, 2), lax.rem(me, 2))
    relay_target = jnp.where(even, 2, 5)

    barrier = pltpu.get_barrier_semaphore()

    def greet(frame, mod):
        pl.semaphore_signal(barrier, inc=1, device_id=(frame, mod), device_id_type=MESH)

    for gap in range(1, modules):
        greet(me, lax.rem(module + gap, modules))
    greet(mate, module)
    if relayed:
        greet(across, module)

    @pl.when(has_down)
    def _():
        greet(me - 2, module)

    @pl.when(has_up)
    def _():
        greet(me + 2, module)

    peers = modules + int(relayed) + has_down.astype(jnp.int32) + has_up.astype(jnp.int32)
    pl.semaphore_wait(barrier, peers)

    def sum_copy(gap):
        return pltpu.make_async_remote_copy(
            src_ref=sums,
            dst_ref=all_sums.at[module],
            send_sem=sum_send.at[gap - 1],
            recv_sem=sum_recv.at[gap - 1],
            device_id=(me, lax.rem(module + gap, modules)),
            device_id_type=MESH,
        )

    for gap in range(1, modules):
        sum_copy(gap).start()
    all_sums[module] = sums[...]
    for gap in range(1, modules):
        sum_copy(gap).wait()
    total = all_sums[0]
    for source in range(1, modules):
        total = total + all_sums[source]
    all_sums[0] = jnp.sqrt(jnp.float32(per_bin * modules)) / total

    half = per_bin // 2
    parts = 2 * modules

    def bin_copy(k, piece):
        gap, part = piece // 2, lax.rem(piece, 2)
        owner = lax.rem(module + gap, modules)
        start = pl.multiple_of(part * half, half)
        landing = pl.multiple_of(module * per_bin + part * half, half)
        return pltpu.make_async_remote_copy(
            src_ref=scaled.at[owner * owned + k, pl.ds(start, half), :],
            dst_ref=own.at[k, pl.ds(landing, half), :],
            send_sem=bin_send.at[k, piece],
            recv_sem=bin_recv.at[k, piece],
            device_id=(me, owner),
            device_id_type=MESH,
        )

    row_index = lax.broadcasted_iota(jnp.int32, (8, frames), 0)

    def fill(label, target, first):
        factor = all_sums[0, pl.ds(label, 1), :]

        def tile(start):
            lines = jnp.broadcast_to(turned[pl.ds(order[start], 1), :], (8, frames))
            for row in range(1, 8):
                line = turned[pl.ds(order[start + row], 1), :]
                lines = jnp.where(row_index == row, line, lines)
            return lines * factor

        def tiles(group, carry):
            start = label * per_bin + group * 16
            both = jnp.concatenate([tile(start), tile(start + 8)], axis=0)
            rows = pl.ds(pl.multiple_of(first + group * 16, 16), 16)
            target[rows, :] = both.astype(jnp.bfloat16)
            return carry

        lax.fori_loop(0, per_bin // 16, tiles, 0, unroll=4)

    def rows_of(j):
        source = lax.rem(module + modules - j // 2, modules)
        return pl.ds(pl.multiple_of(source * per_bin + lax.rem(j, 2) * half, half), half)

    def frame_copy(k, j, slot, target, frame):
        return pltpu.make_async_remote_copy(
            src_ref=own.at[k, rows_of(j), :],
            dst_ref=target.at[k, rows_of(j), :],
            send_sem=frame_send.at[slot, k, j],
            recv_sem=frame_recv.at[slot, k, j],
            device_id=(frame, module),
            device_id_type=MESH,
        )

    def far_copy(k, j):
        return frame_copy(k, j, 0, far, jnp.where(even, me - 2, me + 2))

    def mate_copy(k, j):
        return frame_copy(k, j, 1, near, mate)

    def entry_copy(k, j):
        straight = jnp.where(even, me + 2, me - 2)
        return pltpu.make_async_remote_copy(
            src_ref=own.at[k, rows_of(j), :],
            dst_ref=hold.at[k, rows_of(j), :],
            send_sem=frame_send.at[0, k, j],
            recv_sem=relay_recv.at[k, j],
            device_id=(jnp.where(lax.rem(k, 2) == 0, across, straight), module),
            device_id_type=MESH,
        )

    def exit_copy(k, j):
        return pltpu.make_async_remote_copy(
            src_ref=hold.at[k, rows_of(j), :],
            dst_ref=far.at[k, rows_of(j), :],
            send_sem=relay_send.at[k, j],
            recv_sem=frame_recv.at[0, k, j],
            device_id=(relay_target, module),
            device_id_type=MESH,
        )

    sends_far = (even & has_down) | (odd & has_up)
    diagonal = ((me == 3) | (me == 4)) if relayed else None

    def result_copy(k, stage, place, frame):
        return pltpu.make_async_remote_copy(
            src_ref=staged.at[stage, k],
            dst_ref=out.at[k, place],
            send_sem=result_send.at[stage, k],
            recv_sem=result_recv.at[place, k],
            device_id=(frame, module),
            device_id_type=MESH,
        )

    def pass_on(k, j):
        @pl.when(odd)
        def _():
            mate_copy(k, j).start()

        if relayed:
            @pl.when(diagonal)
            def _():
                entry_copy(k, j).start()

            @pl.when(sends_far & jnp.logical_not(diagonal))
            def _():
                far_copy(k, j).start()
        else:
            @pl.when(sends_far)
            def _():
                far_copy(k, j).start()

    def relay(k, j):
        if relayed:
            @pl.when(relaying & (lax.rem(k, 2) == relay_parity))
            def _():
                entry_copy(k, j).wait_recv()
                exit_copy(k, j).start()

    def await_frames(k, copy):
        for j in range(parts):
            copy(k, j).wait_recv()

    def correlate(k):
        out[k, 2] = gram(own[k], own[k])

        @pl.when(even)
        def _():
            await_frames(k, mate_copy)
            staged[0, k] = gram(near[k], own[k])
            result_copy(k, 0, 1, me + 1).start()
            out[k, 3] = gram(own[k], near[k])

        @pl.when(even & has_up)
        def _():
            await_frames(k, far_copy)
            staged[1, k] = gram(far[k], own[k])
            result_copy(k, 1, 0, me + 2).start()
            staged[2, k] = gram(far[k], near[k])
            result_copy(k, 2, 1, me + 2).start()
            staged[3, k] = gram(near[k], far[k])
            result_copy(k, 3, 3, me + 1).start()
            out[k, 4] = gram(own[k], far[k])

        @pl.when(odd & has_down)
        def _():
            await_frames(k, far_copy)
            staged[0, k] = gram(far[k], own[k])
            result_copy(k, 0, 4, me - 2).start()
            out[k, 0] = gram(own[k], far[k])

    @pl.loop(0, owned)
    def _(k):
        @pl.loop(1, modules)
        def _(gap):
            label = lax.rem(module + gap, modules) * owned + k
            fill(label, scaled.at[label], 0)
            bin_copy(k, 2 * gap).start()
            bin_copy(k, 2 * gap + 1).start()

        fill(module * owned + k, own.at[k], module * per_bin)
        pass_on(k, 0)
        pass_on(k, 1)

    @pl.loop(0, owned)
    def _(k):
        relay(k, 0)
        relay(k, 1)

    def receive(k, gaps):
        pieces = [2 * gap + part for gap in gaps for part in range(2)]
        for index, piece in enumerate(pieces):
            bin_copy(k, piece).wait()
            pass_on(k, piece)
            if index:
                relay(k, pieces[index - 1])
        relay(k, pieces[-1])

    @pl.loop(0, owned + 1)
    def _(turn_index):
        @pl.when(turn_index < owned)
        def _():
            receive(turn_index, range(1, modules))

        @pl.when(turn_index >= 1)
        def _():
            correlate(turn_index - 1)

    @pl.when(me < 2)
    def _():
        out[:, 0] = jnp.zeros_like(out[:, 0])

    @pl.when(me < 1)
    def _():
        out[:, 1] = jnp.zeros_like(out[:, 1])

    @pl.when(me + 1 >= blocks)
    def _():
        out[:, 3] = jnp.zeros_like(out[:, 3])

    @pl.when(me + 2 >= blocks)
    def _():
        out[:, 4] = jnp.zeros_like(out[:, 4])

    @pl.loop(0, owned)
    def _(k):
        @pl.when(even & has_down)
        def _():
            result_copy(k, 1, 0, me).wait_recv()
            result_copy(k, 2, 1, me).wait_recv()

        @pl.when(odd)
        def _():
            for j in range(parts):
                mate_copy(k, j).wait_send()
            result_copy(k, 0, 1, me).wait_recv()

        @pl.when(sends_far)
        def _():
            for j in range(parts):
                far_copy(k, j).wait_send()

        @pl.when(odd & has_up)
        def _():
            result_copy(k, 3, 3, me).wait_recv()
            result_copy(k, 0, 4, me).wait_recv()

        if relayed:
            @pl.when(relaying & (lax.rem(k, 2) == relay_parity))
            def _():
                for j in range(parts):
                    exit_copy(k, j).wait_send()

        @pl.when(even)
        def _():
            result_copy(k, 0, 1, me + 1).wait_send()

        @pl.when(even & has_up)
        def _():
            result_copy(k, 1, 0, me + 2).wait_send()
            result_copy(k, 2, 1, me + 2).wait_send()
            result_copy(k, 3, 3, me + 1).wait_send()

        @pl.when(odd & has_down)
        def _():
            result_copy(k, 0, 4, me - 2).wait_send()


def correlate_chain(order, turned, sums):
    (pixels, frames), bins = turned.shape, sums.shape[0]
    per_bin = pixels // bins
    blocks, modules = lax.axis_size("frame"), lax.axis_size("module")
    owned = bins // modules
    gathered = per_bin * modules
    vmem = pl.BlockSpec(memory_space=pltpu.VMEM)
    dma = pltpu.SemaphoreType.DMA
    return pl.pallas_call(
        functools.partial(chain_kernel, blocks, modules),
        out_shape=jax.ShapeDtypeStruct((owned, 5, frames, frames), jnp.float32),
        in_specs=[pl.BlockSpec(memory_space=pltpu.SMEM), vmem, vmem],
        out_specs=vmem,
        scratch_shapes=[
            pltpu.VMEM((modules, bins, frames), jnp.float32),
            pltpu.VMEM((bins, per_bin, frames), jnp.bfloat16),
            pltpu.VMEM((owned, gathered, frames), jnp.bfloat16),
            pltpu.VMEM((owned, gathered, frames), jnp.bfloat16),
            pltpu.VMEM((owned, gathered, frames), jnp.bfloat16),
            pltpu.VMEM((owned, gathered, frames), jnp.bfloat16),
            pltpu.VMEM((4, owned, frames, frames), jnp.float32),
            dma((modules - 1,)),
            dma((modules - 1,)),
            dma((owned, 2 * modules)),
            dma((owned, 2 * modules)),
            dma((2, owned, 2 * modules)),
            dma((2, owned, 2 * modules)),
            dma((owned, 2 * modules)),
            dma((owned, 2 * modules)),
            dma((4, owned)),
            dma((5, owned)),
        ],
        compiler_params=pltpu.CompilerParams(
            collective_id=0, has_side_effects=True, vmem_limit_bytes=VMEM_BYTES
        ),
    )(order, turned, sums)


def square_kernel(
    modules,
    raw,
    dark_frame,
    flat_field,
    membership,
    total,
    dark,
    flat,
    members,
    lows_highs,
    lanes,
    table,
    order,
    counts_in,
    turned,
    sums,
    all_sums,
    packed,
    own,
    near,
    first,
    second,
    third,
    direct,
    coded,
    coded_peak,
    landed,
    landed_peak,
    raw_sem,
    order_sem,
    sum_send,
    sum_recv,
    bin_send,
    bin_recv,
    frame_send,
    frame_recv,
    direct_send,
    direct_recv,
    coded_send,
    coded_recv,
):
    me = lax.axis_index("frame")
    module = lax.axis_index("module")
    pixels, frames = turned.shape
    bins = packed.shape[0]
    per_bin = pixels // bins
    owned = bins // modules
    gathered = per_bin * modules
    half = per_bin // 2
    parts = 2 * modules
    f32, bf16 = jnp.float32, jnp.bfloat16

    side = me // 4
    sign = 1 - 2 * side

    def flip(block):
        return jnp.where(side == 1, 7 - block, block)

    role = flip(me)
    mate = me + 1 - 2 * lax.rem(me, 2)
    is_one, is_two, is_three = role == 1, role == 2, role == 3

    def place(gap):
        return 2 + sign * gap

    barrier = pltpu.get_barrier_semaphore()

    def greet(frame, mod):
        pl.semaphore_signal(barrier, inc=1, device_id=(frame, mod), device_id_type=MESH)

    for gap in range(1, modules):
        greet(me, lax.rem(module + gap, modules))
    greet(mate, module)

    @pl.when(is_one)
    def _():
        greet(flip(2), module)
        greet(flip(3), module)
        greet(flip(4), module)

    @pl.when(is_two | is_three)
    def _():
        greet(flip(1), module)

    @pl.when(is_three)
    def _():
        greet(flip(6), module)

    slabs, _, slab = counts_in.shape

    def columns_of(index):
        return pl.ds(pl.multiple_of(index * slab, slab), slab)

    def load(index):
        return pltpu.make_async_copy(
            raw.at[:, columns_of(index)], counts_in.at[index], raw_sem.at[index]
        )

    def intensity(index):
        columns = columns_of(index)
        return (counts_in[index].astype(f32) - dark[:, columns]) * flat[:, columns]

    fetch = pltpu.make_async_copy(membership, members, order_sem.at[0])
    fetch.start()
    fetch_dark = pltpu.make_async_copy(dark_frame, dark, order_sem.at[1])
    fetch_dark.start()
    fetch_flat = pltpu.make_async_copy(flat_field, flat, order_sem.at[2])
    fetch_flat.start()
    sums[...] = jnp.zeros_like(sums)
    load(0).start()
    fetch.wait()
    for index in range(1, slabs):
        load(index).start()
    fetch_dark.wait()
    fetch_flat.wait()

    @pl.loop(0, slabs)
    def _(index):
        load(index).wait()
        values = intensity(index)
        high = values.astype(bf16)
        low = (values - high.astype(f32)).astype(bf16)
        one_hot = members[:, columns_of(index)].astype(f32).astype(bf16)
        both = (((1,), (1,)), ((), ()))
        sums[...] += lax.dot_general(
            one_hot, high, both, preferred_element_type=f32
        ) + lax.dot_general(one_hot, low, both, preferred_element_type=f32)

    peers = modules + jnp.where(is_one, 3, jnp.where(is_three, 2, jnp.where(is_two, 1, 0)))
    pl.semaphore_wait(barrier, peers)

    def sum_copy(gap):
        return pltpu.make_async_remote_copy(
            src_ref=sums,
            dst_ref=all_sums.at[module],
            send_sem=sum_send.at[gap - 1],
            recv_sem=sum_recv.at[gap - 1],
            device_id=(me, lax.rem(module + gap, modules)),
            device_id_type=MESH,
        )

    for gap in range(1, modules):
        sum_copy(gap).start()
    all_sums[module] = sums[...]
    table[...] = sort_pixels(members, lows_highs, lanes)

    def spread(line):
        return pltpu.make_async_copy(
            table.at[line], order.at[pl.ds(line * LANES, LANES)], order_sem.at[3 + line]
        )

    for line in range(table.shape[0]):
        spread(line).start()

    @pl.loop(0, slabs)
    def _(index):
        turned[columns_of(index), :] = intensity(index).T

    for gap in range(1, modules):
        sum_copy(gap).wait()
    bin_sums = all_sums[0]
    for source in range(1, modules):
        bin_sums = bin_sums + all_sums[source]
    all_sums[0] = jnp.sqrt(f32(gathered)) / bin_sums

    for line in range(table.shape[0]):
        spread(line).wait()
    row_index = lax.broadcasted_iota(jnp.int32, (8, frames), 0)

    def fill(label, part, target, first_row):
        factor = all_sums[0, pl.ds(label, 1), :]

        def tile(start):
            lines = jnp.broadcast_to(turned[pl.ds(order[start], 1), :], (8, frames))
            for row in range(1, 8):
                line = turned[pl.ds(order[start + row], 1), :]
                lines = jnp.where(row_index == row, line, lines)
            return lines * factor

        def tiles(group, carry):
            start = label * per_bin + part * half + group * 16
            both = jnp.concatenate([tile(start), tile(start + 8)], axis=0)
            rows = pl.ds(pl.multiple_of(first_row + group * 16, 16), 16)
            target[rows, :] = both.astype(bf16)
            return carry

        lax.fori_loop(0, half // 16, tiles, 0, unroll=4)

    def bin_copy(k, piece):
        gap, part = piece // 2, lax.rem(piece, 2)
        owner = lax.rem(module + gap, modules)
        start = pl.multiple_of(part * half, half)
        landing = pl.multiple_of(module * per_bin + part * half, half)
        return pltpu.make_async_remote_copy(
            src_ref=packed.at[owner * owned + k, pl.ds(start, half), :],
            dst_ref=own.at[k, pl.ds(landing, half), :],
            send_sem=bin_send.at[0],
            recv_sem=bin_recv.at[k, piece],
            device_id=(me, owner),
            device_id_type=MESH,
        )

    def rows_of(j):
        source = lax.rem(module + modules - j // 2, modules)
        return pl.ds(pl.multiple_of(source * per_bin + lax.rem(j, 2) * half, half), half)

    def frame_copy(flow, k, j, target, frame):
        return pltpu.make_async_remote_copy(
            src_ref=own.at[k, rows_of(j), :],
            dst_ref=target.at[rows_of(j), :],
            send_sem=frame_send.at[flow],
            recv_sem=frame_recv.at[flow, k],
            device_id=(frame, module),
            device_id_type=MESH,
        )

    def whole_copy(flow, k, source, target, frame):
        return pltpu.make_async_remote_copy(
            src_ref=source,
            dst_ref=target,
            send_sem=frame_send.at[flow],
            recv_sem=frame_recv.at[flow, k],
            device_id=(frame, module),
            device_id_type=MESH,
        )

    def near_copy(k, j):
        return frame_copy(0, k, j, near.at[k], mate)

    def first_copy(k, j):
        return frame_copy(1, k, j, first.at[k], jnp.where(is_one, flip(3), flip(1)))

    def second_copy(k, j):
        return frame_copy(2, k, j, second.at[k], flip(6))

    def third_copy(k, j):
        return frame_copy(3, k, j, third.at[k // 2], flip(1))

    def shared(k):
        return lax.rem(k, 2) == side

    def pass_on(k, j):
        @pl.when(is_one | is_two)
        def _():
            first_copy(k, j).start()

        @pl.when(is_three)
        def _():
            second_copy(k, j).start()

        @pl.when(is_three & shared(k))
        def _():
            third_copy(k, j).start()

        near_copy(k, j).start()

    def pick(table, turn):
        found = turn * 0
        for row, others in enumerate(table):
            for column, other in enumerate(others):
                here = (module == row) & (turn == column)
                found = jnp.where(here, (other - row) % modules, found)
        return found

    def fill_for(k, turn):
        gap = pick(SEND_ORDER, turn - 1)
        label = lax.rem(module + gap, modules) * owned + k

        @pl.loop(0, 2)
        def _(part):
            fill(label, part, packed.at[label], part * half)
            bin_copy(k, 2 * gap + part).start()

    def fill_own(k):
        @pl.loop(0, 2)
        def _(part):
            first_row = module * per_bin + part * half
            fill(module * owned + k, part, own.at[k], first_row)
            pass_on(k, part)

    one_results = ((2, 0, 1), (2, 4, 0), (4, 2, 0), (3, 4, 1), (4, 3, 1))
    three_results = ((1, 3, 0),)

    def coded_copies(k, stage, slot, frame):
        pairs = ((coded, landed), (coded_peak, landed_peak))
        return [
            pltpu.make_async_remote_copy(
                src_ref=source.at[stage, k],
                dst_ref=target.at[slot, k],
                send_sem=coded_send.at[index],
                recv_sem=coded_recv.at[index, slot, k],
                device_id=(frame, module),
                device_id_type=MESH,
            )
            for index, (source, target) in enumerate(pairs)
        ]

    def send_coded(k, stage, result, values):
        peak = jnp.max(values, axis=0, keepdims=True)
        levels = values * (32767.0 / peak) + 0.5
        coded[stage, k] = levels.astype(jnp.int32).astype(jnp.int16)
        coded_peak[stage, k] = jnp.broadcast_to(peak * (1.0 / 32767.0), (8, frames))
        for copy in coded_copies(k, stage, result[2], flip(result[0])):
            copy.start()

    def decode(k, slot, gap):
        for copy in coded_copies(k, 0, slot, me):
            copy.wait_recv()
        values = landed[slot, k].astype(jnp.int32).astype(f32)
        total[k, place(gap)] = values * landed_peak[slot, k, :1, :]

    def direct_copy(k):
        return pltpu.make_async_remote_copy(
            src_ref=direct.at[k],
            dst_ref=total.at[k, jnp.where(role < 2, place(2), place(-1))],
            send_sem=direct_send.at[0],
            recv_sem=direct_recv.at[k],
            device_id=(mate, module),
            device_id_type=MESH,
        )

    def await_frames(k, flow, target):
        whole_copy(flow, k, own.at[k], target, mate).wait_recv()

    def work(k, step):
        if step == 0:
            await_frames(k, 0, near.at[k])

            @pl.when(is_one)
            def _():
                await_frames(k, 1, first.at[k])
                send_coded(k, 0, one_results[0], gram(first[k], near[k]))

            @pl.when(is_three)
            def _():
                await_frames(k, 1, first.at[k])
                send_coded(k, 0, three_results[0], gram(first[k], own[k]))

        if step == 1:

            @pl.when(is_one)
            def _():
                await_frames(k, 2, second.at[k])
                send_coded(k, 2, one_results[2], gram(second[k], first[k]))

            @pl.when(is_three)
            def _():
                direct[k] = gram(near[k], first[k])
                direct_copy(k).start()

        if step == 2:

            @pl.when(is_one)
            def _():
                send_coded(k, 1, one_results[1], gram(first[k], second[k]))

            @pl.when(is_three)
            def _():
                total[k, place(-2)] = gram(own[k], first[k])

        if step == 3:

            @pl.when(is_one & shared(k))
            def _():
                await_frames(k, 3, third.at[k // 2])
                send_coded(k, 4, one_results[4], gram(second[k], third[k // 2]))
                send_coded(k, 3, one_results[3], gram(third[k // 2], second[k]))

        if step == 4:

            @pl.when(is_one)
            def _():
                direct[k] = gram(near[k], first[k])
                direct_copy(k).start()
                total[k, place(1)] = gram(own[k], first[k])

        if step == 5:
            total[k, mate - me + 2] = gram(own[k], near[k])
            total[k, 2] = gram(own[k], own[k])

    def finish(k):
        @pl.when((role == 0) | is_two)
        def _():
            direct_copy(k).wait_recv()

        @pl.when(role > 0)
        def _():
            decode(k, 0, 2)

        @pl.when(is_two)
        def _():
            decode(k, 1, -2)

        @pl.when(is_three)
        def _():
            decode(k, 1, 1)

    @pl.loop(0, owned)
    def _(k):
        @pl.loop(1, modules)
        def _(turn):
            fill_for(k, turn)

        fill_own(k)

    @pl.when(role == 0)
    def _():
        for k in range(owned):
            total[k, place(-1)] = jnp.zeros((frames, frames), f32)

    @pl.when(role < 2)
    def _():
        for k in range(owned):
            total[k, place(-2)] = jnp.zeros((frames, frames), f32)

    at_end = (module == 0) | (module == modules - 1)

    def choose(values, index):
        found = index * 0 + values[0]
        for spot, value in enumerate(values):
            found = jnp.where(index == spot, value, found)
        return found

    def take(spot):
        end_k, end_column = (choose(values, spot) for values in zip(*END_ARRIVALS))
        middle_k, middle_column = (choose(values, spot) for values in zip(*MIDDLE_ARRIVALS))
        k = jnp.where(at_end, end_k, middle_k)
        gap = modules - pick(HEARD, jnp.where(at_end, end_column, middle_column))

        @pl.loop(0, 2)
        def _(part):
            piece = 2 * gap + part
            bin_copy(k, piece).wait_recv()
            pass_on(k, piece)

    early = 8

    @pl.loop(0, early)
    def _(spot):
        take(spot)

    @pl.loop(0, owned)
    def _(k):
        for stage in range(6):
            work(k, stage)

        @pl.when(k < owned - 1)
        def _():
            take(early + k + jnp.minimum(k, 1))

        @pl.when(k == 0)
        def _():
            take(early + 1 + k)

        @pl.when(k >= 1)
        def _():
            finish(k - 1)

    finish(owned - 1)

    sent = packed.at[pl.ds(0, bins - owned)]
    pltpu.make_async_remote_copy(
        src_ref=sent,
        dst_ref=sent,
        send_sem=bin_send.at[0],
        recv_sem=bin_recv.at[0, 0],
        device_id=(mate, module),
        device_id_type=MESH,
    ).wait_send()
    whole_copy(0, 0, own, near, mate).wait_send()

    def await_coded(rows):
        for index, source in enumerate((coded, coded_peak)):
            pltpu.make_async_remote_copy(
                src_ref=source.at[pl.ds(0, rows)],
                dst_ref=source.at[pl.ds(0, rows)],
                send_sem=coded_send.at[index],
                recv_sem=coded_recv.at[index, 0, 0],
                device_id=(mate, module),
                device_id_type=MESH,
            ).wait_send()

    @pl.when(is_one | is_two)
    def _():
        whole_copy(1, 0, own, first, mate).wait_send()

    @pl.when(is_three)
    def _():
        whole_copy(2, 0, own, second, mate).wait_send()
        whole_copy(3, 0, own.at[pl.ds(0, owned // 2)], third, mate).wait_send()
        await_coded(1)

    @pl.when(is_one)
    def _():
        await_coded(4)

    @pl.when(is_one | is_three)
    def _():
        pltpu.make_async_remote_copy(
            src_ref=direct,
            dst_ref=direct,
            send_sem=direct_send.at[0],
            recv_sem=direct_recv.at[0],
            device_id=(mate, module),
            device_id_type=MESH,
        ).wait_send()


def correlate_square(raw_frames, dark_frame, flat_field, membership):
    frames, pixels = raw_frames.shape
    bins = membership.shape[0]
    modules = lax.axis_size("module")
    per_bin = pixels // bins
    owned = bins // modules
    gathered = per_bin * modules
    slab = 2 * per_bin
    vmem = pl.BlockSpec(memory_space=pltpu.VMEM)
    dma = pltpu.SemaphoreType.DMA
    f32, bf16 = jnp.float32, jnp.bfloat16
    block = (owned, gathered, frames)
    return pl.pallas_call(
        functools.partial(square_kernel, modules),
        out_shape=pltpu.VMEM((owned, 5, frames, frames), f32),
        in_specs=[
            pl.BlockSpec(memory_space=pl.ANY),
            pl.BlockSpec(memory_space=pl.ANY),
            pl.BlockSpec(memory_space=pl.ANY),
            pl.BlockSpec(memory_space=pl.ANY),
        ],
        out_specs=vmem,
        scratch_shapes=[
            pltpu.VMEM((1, pixels), f32),
            pltpu.VMEM((1, pixels), f32),
            pltpu.VMEM((bins, pixels), jnp.int32),
            pltpu.VMEM((2 * pixels // LANES, pixels), bf16),
            pltpu.VMEM((LANES, pixels), bf16),
            pltpu.VMEM((pixels // LANES, LANES), jnp.int32),
            pltpu.SMEM((pixels,), jnp.int32),
            pltpu.VMEM((pixels // slab, frames, slab), jnp.int32),
            pltpu.VMEM((pixels, frames), f32),
            pltpu.VMEM((bins, frames), f32),
            pltpu.VMEM((modules, bins, frames), f32),
            pltpu.VMEM((bins, per_bin, frames), bf16),
            pltpu.VMEM(block, bf16),
            pltpu.VMEM(block, bf16),
            pltpu.VMEM(block, bf16),
            pltpu.VMEM(block, bf16),
            pltpu.VMEM((owned // 2, gathered, frames), bf16),
            pltpu.VMEM((owned, frames, frames), f32),
            pltpu.VMEM((5, owned, frames, frames), jnp.int16),
            pltpu.VMEM((5, owned, 8, frames), f32),
            pltpu.VMEM((2, owned, frames, frames), jnp.int16),
            pltpu.VMEM((2, owned, 8, frames), f32),
            dma((pixels // slab,)),
            dma((3 + pixels // LANES,)),
            dma((modules - 1,)),
            dma((modules - 1,)),
            dma((1,)),
            dma((owned, 2 * modules)),
            dma((4,)),
            dma((4, owned)),
            dma((1,)),
            dma((owned,)),
            dma((2,)),
            dma((2, 2, owned)),
        ],
        compiler_params=pltpu.CompilerParams(
            collective_id=1, has_side_effects=True, vmem_limit_bytes=SQUARE_BYTES
        ),
    )(raw_frames, dark_frame[None, :], flat_field[None, :], membership)


def per_device(raw_frames, dark_frame, flat_field, membership):
    square = lax.axis_size("frame") == 8 and lax.axis_size("module") == 4
    if square and membership.shape[0] == 16:
        result = correlate_square(raw_frames, dark_frame, flat_field, membership)
    else:
        order = pixel_order(membership)
        turned, sums = turn(raw_frames, dark_frame, flat_field, membership)
        result = correlate_chain(order, turned, sums)
    return result[:, None]


def solution(mesh):
    in_specs = (P("frame", "module"), P("module"), P("module"), P(None, "module"))
    out_specs = P("module", "frame", None, None, None)
    return jax.shard_map(
        per_device, mesh=mesh, in_specs=in_specs, out_specs=out_specs, check_vma=False
    )
```

```python
import functools

import jax
import jax.numpy as jnp
from jax import lax
from jax.experimental import pallas as pl
from jax.experimental.pallas import tpu as pltpu
from jax.sharding import PartitionSpec as P

MESH = pl.DeviceIdType.MESH
VMEM_BYTES = 60 * 1024 * 1024
SQUARE_BYTES = 57 * 1024 * 1024
LANES = 128
PIECES = 4
SEND_ORDER = ((3, 2, 1), (2, 3, 0), (1, 0, 3), (0, 1, 2))
LATE_ORDER = ((3, 2, 1), (3, 2, 0), (0, 1, 3), (0, 1, 2))
LATE = 3
HEARD = ((1, 3, 2), (0, 3, 2), (3, 0, 1), (2, 0, 1))
END_ARRIVALS = ((0, 0), (0, 1), (1, 0), (1, 1), (0, 2), (2, 0), (2, 1), (3, 0), (3, 1), (1, 2), (2, 2), (3, 2))
MIDDLE_ARRIVALS = ((0, 0), (0, 1), (1, 0), (1, 1), (0, 2), (2, 0), (2, 1), (1, 2), (3, 1), (3, 0), (2, 2), (3, 2))


def place_pixels(members, lows_highs, lanes, chunks, base):
    bins, pixels = members.shape
    per_bin = pixels // bins
    span = 2 * LANES
    rows = pixels // LANES
    f32, bf16 = jnp.float32, jnp.bfloat16
    shape = (span, span + LANES)
    upto = lax.broadcasted_iota(jnp.int32, shape, 0) <= lax.broadcasted_iota(jnp.int32, shape, 1)
    upto = upto.astype(f32).astype(bf16)
    if base is None:
        base = lax.broadcasted_iota(jnp.int32, (bins, span), 0).astype(f32) * per_bin - 1.0
    row_of = lax.broadcasted_iota(jnp.int32, (rows, span), 0)
    lane_of = lax.broadcasted_iota(jnp.int32, (LANES, span), 0)
    place = lax.broadcasted_iota(jnp.int32, (rows, span), 1).astype(f32)
    for chunk in chunks:
        columns = slice(chunk * span, (chunk + 1) * span)
        one_hot = members[:, columns].astype(f32)
        seen = jnp.dot(one_hot.astype(bf16), upto, preferred_element_type=f32)
        slot = one_hot * (seen[:, :span] + base)
        slot = jnp.sum(slot, axis=0, keepdims=True).astype(jnp.int32)
        base = base + jnp.concatenate([seen[:, span:]] * 2, axis=1)
        in_row = row_of == jnp.broadcast_to(slot // LANES, (rows, span))
        in_lane = lane_of == jnp.broadcast_to(slot % LANES, (LANES, span))
        lanes[:, columns] = in_lane.astype(f32).astype(bf16)
        lows_highs[:rows, columns] = jnp.where(in_row, place, 0.0).astype(bf16)
        lows_highs[rows:, columns] = jnp.where(in_row, float(chunk), 0.0).astype(bf16)
    return base


def order_table(lows_highs, lanes):
    rows, pixels = lows_highs.shape[0] // 2, lows_highs.shape[1]
    both = (((1,), (1,)), ((), ()))
    table = lax.dot_general(
        lows_highs[...], lanes[...], both, preferred_element_type=jnp.float32
    )
    table = (table[rows:] * (2 * LANES) + table[:rows]).astype(jnp.int32)
    return jnp.clip(table, 0, pixels - 1)


def order_kernel(members, order, lows_highs, lanes):
    chunks = range(members.shape[1] // (2 * LANES))
    place_pixels(members, lows_highs, lanes, chunks, None)
    order[...] = order_table(lows_highs, lanes)


def pixel_order(membership):
    pixels = membership.shape[1]
    vmem = pl.BlockSpec(memory_space=pltpu.VMEM)
    table = pl.pallas_call(
        order_kernel,
        out_shape=jax.ShapeDtypeStruct((pixels // LANES, LANES), jnp.int32),
        in_specs=[vmem],
        out_specs=vmem,
        scratch_shapes=[
            pltpu.VMEM((2 * pixels // LANES, pixels), jnp.bfloat16),
            pltpu.VMEM((LANES, pixels), jnp.bfloat16),
        ],
    )(membership)
    return table.reshape(pixels)


def turn_kernel(raw, dark, flat, members, turned, sums):
    @pl.when(pl.program_id(0) == 0)
    def _():
        sums[...] = jnp.zeros_like(sums)

    intensity = (raw[...].astype(jnp.float32) - dark[...]) * flat[...]
    lines = intensity.T
    turned[...] = lines
    sums[...] += jnp.dot(
        members[...].astype(jnp.float32),
        lines,
        precision=lax.Precision.HIGHEST,
        preferred_element_type=jnp.float32,
    )


def turn(raw_frames, dark_frame, flat_field, membership):
    frames, pixels = raw_frames.shape
    bins = membership.shape[0]
    chunk = pixels // bins
    return pl.pallas_call(
        turn_kernel,
        out_shape=(
            jax.ShapeDtypeStruct((pixels, frames), jnp.float32),
            jax.ShapeDtypeStruct((bins, frames), jnp.float32),
        ),
        grid=(pixels // chunk,),
        in_specs=[
            pl.BlockSpec((frames, chunk), lambda i: (0, i)),
            pl.BlockSpec((1, chunk), lambda i: (0, i)),
            pl.BlockSpec((1, chunk), lambda i: (0, i)),
            pl.BlockSpec((bins, chunk), lambda i: (0, i)),
        ],
        out_specs=(
            pl.BlockSpec((chunk, frames), lambda i: (i, 0)),
            pl.BlockSpec((bins, frames), lambda i: (0, 0)),
        ),
    )(raw_frames, dark_frame[None, :], flat_field[None, :], membership)


def gram(left, right):
    return lax.dot_general(
        left, right, (((0,), (0,)), ((), ())), preferred_element_type=jnp.float32
    )


def chain_kernel(
    blocks,
    modules,
    order,
    turned,
    sums,
    out,
    all_sums,
    scaled,
    own,
    far,
    near,
    hold,
    staged,
    sum_send,
    sum_recv,
    bin_send,
    bin_recv,
    frame_send,
    frame_recv,
    relay_send,
    relay_recv,
    result_send,
    result_recv,
):
    me = lax.axis_index("frame")
    module = lax.axis_index("module")
    pixels, frames = turned.shape
    bins = sums.shape[0]
    per_bin = pixels // bins
    owned = bins // modules
    even = lax.rem(me, 2) == 0
    odd = lax.rem(me, 2) == 1
    has_down = me >= 2
    has_up = me + 2 < blocks
    mate = me + 1 - 2 * lax.rem(me, 2)
    relayed = blocks == 8
    across = lax.rem(me + 4, 8)
    relaying = (me < 2) | (me >= 6)
    relay_parity = jnp.where(me >= 6, 1 - lax.rem(me, 2), lax.rem(me, 2))
    relay_target = jnp.where(even, 2, 5)

    barrier = pltpu.get_barrier_semaphore()

    def greet(frame, mod):
        pl.semaphore_signal(barrier, inc=1, device_id=(frame, mod), device_id_type=MESH)

    for gap in range(1, modules):
        greet(me, lax.rem(module + gap, modules))
    greet(mate, module)
    if relayed:
        greet(across, module)

    @pl.when(has_down)
    def _():
        greet(me - 2, module)

    @pl.when(has_up)
    def _():
        greet(me + 2, module)

    peers = modules + int(relayed) + has_down.astype(jnp.int32) + has_up.astype(jnp.int32)
    pl.semaphore_wait(barrier, peers)

    def sum_copy(gap):
        return pltpu.make_async_remote_copy(
            src_ref=sums,
            dst_ref=all_sums.at[module],
            send_sem=sum_send.at[gap - 1],
            recv_sem=sum_recv.at[gap - 1],
            device_id=(me, lax.rem(module + gap, modules)),
            device_id_type=MESH,
        )

    for gap in range(1, modules):
        sum_copy(gap).start()
    all_sums[module] = sums[...]
    for gap in range(1, modules):
        sum_copy(gap).wait()
    total = all_sums[0]
    for source in range(1, modules):
        total = total + all_sums[source]
    all_sums[0] = jnp.sqrt(jnp.float32(per_bin * modules)) / total

    half = per_bin // 2
    parts = 2 * modules

    def bin_copy(k, piece):
        gap, part = piece // 2, lax.rem(piece, 2)
        owner = lax.rem(module + gap, modules)
        start = pl.multiple_of(part * half, half)
        landing = pl.multiple_of(module * per_bin + part * half, half)
        return pltpu.make_async_remote_copy(
            src_ref=scaled.at[owner * owned + k, pl.ds(start, half), :],
            dst_ref=own.at[k, pl.ds(landing, half), :],
            send_sem=bin_send.at[k, piece],
            recv_sem=bin_recv.at[k, piece],
            device_id=(me, owner),
            device_id_type=MESH,
        )

    row_index = lax.broadcasted_iota(jnp.int32, (8, frames), 0)

    def fill(label, target, first):
        factor = all_sums[0, pl.ds(label, 1), :]

        def tile(start):
            lines = jnp.broadcast_to(turned[pl.ds(order[start], 1), :], (8, frames))
            for row in range(1, 8):
                line = turned[pl.ds(order[start + row], 1), :]
                lines = jnp.where(row_index == row, line, lines)
            return lines * factor

        def tiles(group, carry):
            start = label * per_bin + group * 16
            both = jnp.concatenate([tile(start), tile(start + 8)], axis=0)
            rows = pl.ds(pl.multiple_of(first + group * 16, 16), 16)
            target[rows, :] = both.astype(jnp.bfloat16)
            return carry

        lax.fori_loop(0, per_bin // 16, tiles, 0, unroll=4)

    def rows_of(j):
        source = lax.rem(module + modules - j // 2, modules)
        return pl.ds(pl.multiple_of(source * per_bin + lax.rem(j, 2) * half, half), half)

    def frame_copy(k, j, slot, target, frame):
        return pltpu.make_async_remote_copy(
            src_ref=own.at[k, rows_of(j), :],
            dst_ref=target.at[k, rows_of(j), :],
            send_sem=frame_send.at[slot, k, j],
            recv_sem=frame_recv.at[slot, k, j],
            device_id=(frame, module),
            device_id_type=MESH,
        )

    def far_copy(k, j):
        return frame_copy(k, j, 0, far, jnp.where(even, me - 2, me + 2))

    def mate_copy(k, j):
        return frame_copy(k, j, 1, near, mate)

    def entry_copy(k, j):
        straight = jnp.where(even, me + 2, me - 2)
        return pltpu.make_async_remote_copy(
            src_ref=own.at[k, rows_of(j), :],
            dst_ref=hold.at[k, rows_of(j), :],
            send_sem=frame_send.at[0, k, j],
            recv_sem=relay_recv.at[k, j],
            device_id=(jnp.where(lax.rem(k, 2) == 0, across, straight), module),
            device_id_type=MESH,
        )

    def exit_copy(k, j):
        return pltpu.make_async_remote_copy(
            src_ref=hold.at[k, rows_of(j), :],
            dst_ref=far.at[k, rows_of(j), :],
            send_sem=relay_send.at[k, j],
            recv_sem=frame_recv.at[0, k, j],
            device_id=(relay_target, module),
            device_id_type=MESH,
        )

    sends_far = (even & has_down) | (odd & has_up)
    diagonal = ((me == 3) | (me == 4)) if relayed else None

    def result_copy(k, stage, place, frame):
        return pltpu.make_async_remote_copy(
            src_ref=staged.at[stage, k],
            dst_ref=out.at[k, place],
            send_sem=result_send.at[stage, k],
            recv_sem=result_recv.at[place, k],
            device_id=(frame, module),
            device_id_type=MESH,
        )

    def pass_on(k, j):
        @pl.when(odd)
        def _():
            mate_copy(k, j).start()

        if relayed:
            @pl.when(diagonal)
            def _():
                entry_copy(k, j).start()

            @pl.when(sends_far & jnp.logical_not(diagonal))
            def _():
                far_copy(k, j).start()
        else:
            @pl.when(sends_far)
            def _():
                far_copy(k, j).start()

    def relay(k, j):
        if relayed:
            @pl.when(relaying & (lax.rem(k, 2) == relay_parity))
            def _():
                entry_copy(k, j).wait_recv()
                exit_copy(k, j).start()

    def await_frames(k, copy):
        for j in range(parts):
            copy(k, j).wait_recv()

    def correlate(k):
        out[k, 2] = gram(own[k], own[k])

        @pl.when(even)
        def _():
            await_frames(k, mate_copy)
            staged[0, k] = gram(near[k], own[k])
            result_copy(k, 0, 1, me + 1).start()
            out[k, 3] = gram(own[k], near[k])

        @pl.when(even & has_up)
        def _():
            await_frames(k, far_copy)
            staged[1, k] = gram(far[k], own[k])
            result_copy(k, 1, 0, me + 2).start()
            staged[2, k] = gram(far[k], near[k])
            result_copy(k, 2, 1, me + 2).start()
            staged[3, k] = gram(near[k], far[k])
            result_copy(k, 3, 3, me + 1).start()
            out[k, 4] = gram(own[k], far[k])

        @pl.when(odd & has_down)
        def _():
            await_frames(k, far_copy)
            staged[0, k] = gram(far[k], own[k])
            result_copy(k, 0, 4, me - 2).start()
            out[k, 0] = gram(own[k], far[k])

    @pl.loop(0, owned)
    def _(k):
        @pl.loop(1, modules)
        def _(gap):
            label = lax.rem(module + gap, modules) * owned + k
            fill(label, scaled.at[label], 0)
            bin_copy(k, 2 * gap).start()
            bin_copy(k, 2 * gap + 1).start()

        fill(module * owned + k, own.at[k], module * per_bin)
        pass_on(k, 0)
        pass_on(k, 1)

    @pl.loop(0, owned)
    def _(k):
        relay(k, 0)
        relay(k, 1)

    def receive(k, gaps):
        pieces = [2 * gap + part for gap in gaps for part in range(2)]
        for index, piece in enumerate(pieces):
            bin_copy(k, piece).wait()
            pass_on(k, piece)
            if index:
                relay(k, pieces[index - 1])
        relay(k, pieces[-1])

    @pl.loop(0, owned + 1)
    def _(turn_index):
        @pl.when(turn_index < owned)
        def _():
            receive(turn_index, range(1, modules))

        @pl.when(turn_index >= 1)
        def _():
            correlate(turn_index - 1)

    @pl.when(me < 2)
    def _():
        out[:, 0] = jnp.zeros_like(out[:, 0])

    @pl.when(me < 1)
    def _():
        out[:, 1] = jnp.zeros_like(out[:, 1])

    @pl.when(me + 1 >= blocks)
    def _():
        out[:, 3] = jnp.zeros_like(out[:, 3])

    @pl.when(me + 2 >= blocks)
    def _():
        out[:, 4] = jnp.zeros_like(out[:, 4])

    @pl.loop(0, owned)
    def _(k):
        @pl.when(even & has_down)
        def _():
            result_copy(k, 1, 0, me).wait_recv()
            result_copy(k, 2, 1, me).wait_recv()

        @pl.when(odd)
        def _():
            for j in range(parts):
                mate_copy(k, j).wait_send()
            result_copy(k, 0, 1, me).wait_recv()

        @pl.when(sends_far)
        def _():
            for j in range(parts):
                far_copy(k, j).wait_send()

        @pl.when(odd & has_up)
        def _():
            result_copy(k, 3, 3, me).wait_recv()
            result_copy(k, 0, 4, me).wait_recv()

        if relayed:
            @pl.when(relaying & (lax.rem(k, 2) == relay_parity))
            def _():
                for j in range(parts):
                    exit_copy(k, j).wait_send()

        @pl.when(even)
        def _():
            result_copy(k, 0, 1, me + 1).wait_send()

        @pl.when(even & has_up)
        def _():
            result_copy(k, 1, 0, me + 2).wait_send()
            result_copy(k, 2, 1, me + 2).wait_send()
            result_copy(k, 3, 3, me + 1).wait_send()

        @pl.when(odd & has_down)
        def _():
            result_copy(k, 0, 4, me - 2).wait_send()


def correlate_chain(order, turned, sums):
    (pixels, frames), bins = turned.shape, sums.shape[0]
    per_bin = pixels // bins
    blocks, modules = lax.axis_size("frame"), lax.axis_size("module")
    owned = bins // modules
    gathered = per_bin * modules
    vmem = pl.BlockSpec(memory_space=pltpu.VMEM)
    dma = pltpu.SemaphoreType.DMA
    return pl.pallas_call(
        functools.partial(chain_kernel, blocks, modules),
        out_shape=jax.ShapeDtypeStruct((owned, 5, frames, frames), jnp.float32),
        in_specs=[pl.BlockSpec(memory_space=pltpu.SMEM), vmem, vmem],
        out_specs=vmem,
        scratch_shapes=[
            pltpu.VMEM((modules, bins, frames), jnp.float32),
            pltpu.VMEM((bins, per_bin, frames), jnp.bfloat16),
            pltpu.VMEM((owned, gathered, frames), jnp.bfloat16),
            pltpu.VMEM((owned, gathered, frames), jnp.bfloat16),
            pltpu.VMEM((owned, gathered, frames), jnp.bfloat16),
            pltpu.VMEM((owned, gathered, frames), jnp.bfloat16),
            pltpu.VMEM((4, owned, frames, frames), jnp.float32),
            dma((modules - 1,)),
            dma((modules - 1,)),
            dma((owned, 2 * modules)),
            dma((owned, 2 * modules)),
            dma((2, owned, 2 * modules)),
            dma((2, owned, 2 * modules)),
            dma((owned, 2 * modules)),
            dma((owned, 2 * modules)),
            dma((4, owned)),
            dma((5, owned)),
        ],
        compiler_params=pltpu.CompilerParams(
            collective_id=0, has_side_effects=True, vmem_limit_bytes=VMEM_BYTES
        ),
    )(order, turned, sums)


def square_kernel(
    modules,
    raw,
    dark_frame,
    flat_field,
    membership,
    total,
    dark,
    flat,
    members,
    lows_highs,
    lanes,
    table,
    order,
    counts_in,
    turned,
    sums,
    all_sums,
    packed,
    own,
    near,
    first,
    second,
    third,
    direct,
    coded,
    coded_peak,
    landed,
    landed_peak,
    raw_sem,
    order_sem,
    sum_send,
    sum_recv,
    bin_send,
    bin_recv,
    frame_send,
    frame_recv,
    direct_send,
    direct_recv,
    coded_send,
    coded_recv,
):
    me = lax.axis_index("frame")
    module = lax.axis_index("module")
    pixels, frames = turned.shape
    bins = packed.shape[0]
    per_bin = pixels // bins
    owned = bins // modules
    gathered = per_bin * modules
    share = per_bin // PIECES
    f32, bf16 = jnp.float32, jnp.bfloat16

    side = me // 4
    sign = 1 - 2 * side

    def flip(block):
        return jnp.where(side == 1, 7 - block, block)

    role = flip(me)
    mate = me + 1 - 2 * lax.rem(me, 2)
    is_one, is_two, is_three = role == 1, role == 2, role == 3

    def place(gap):
        return 2 + sign * gap

    barrier = pltpu.get_barrier_semaphore()

    def greet(frame, mod):
        pl.semaphore_signal(barrier, inc=1, device_id=(frame, mod), device_id_type=MESH)

    for gap in range(1, modules):
        greet(me, lax.rem(module + gap, modules))
    greet(mate, module)

    @pl.when(is_one)
    def _():
        greet(flip(2), module)
        greet(flip(3), module)
        greet(flip(4), module)

    @pl.when(is_two | is_three)
    def _():
        greet(flip(1), module)

    @pl.when(is_three)
    def _():
        greet(flip(6), module)

    slabs, _, slab = counts_in.shape

    def columns_of(index):
        return pl.ds(pl.multiple_of(index * slab, slab), slab)

    def load(index):
        return pltpu.make_async_copy(
            raw.at[:, columns_of(index)], counts_in.at[index], raw_sem.at[index]
        )

    def intensity(index):
        columns = columns_of(index)
        return (counts_in[index].astype(f32) - dark[:, columns]) * flat[:, columns]

    fetch = pltpu.make_async_copy(membership, members, order_sem.at[0])
    fetch.start()
    fetch_dark = pltpu.make_async_copy(dark_frame, dark, order_sem.at[1])
    fetch_dark.start()
    fetch_flat = pltpu.make_async_copy(flat_field, flat, order_sem.at[2])
    fetch_flat.start()
    sums[...] = jnp.zeros_like(sums)
    load(0).start()
    fetch.wait()
    for index in range(1, slabs):
        load(index).start()
    chunks = pixels // (2 * LANES)
    base = place_pixels(members, lows_highs, lanes, range(chunks // 2), None)
    fetch_dark.wait()
    fetch_flat.wait()

    @pl.loop(0, slabs)
    def _(index):
        load(index).wait()
        values = intensity(index)
        high = values.astype(bf16)
        low = (values - high.astype(f32)).astype(bf16)
        one_hot = members[:, columns_of(index)].astype(f32).astype(bf16)
        both = (((1,), (1,)), ((), ()))
        sums[...] += lax.dot_general(
            one_hot, high, both, preferred_element_type=f32
        ) + lax.dot_general(one_hot, low, both, preferred_element_type=f32)

    peers = modules + jnp.where(is_one, 3, jnp.where(is_three, 2, jnp.where(is_two, 1, 0)))
    pl.semaphore_wait(barrier, peers)

    def sum_copy(gap):
        return pltpu.make_async_remote_copy(
            src_ref=sums,
            dst_ref=all_sums.at[module],
            send_sem=sum_send.at[gap - 1],
            recv_sem=sum_recv.at[gap - 1],
            device_id=(me, lax.rem(module + gap, modules)),
            device_id_type=MESH,
        )

    for gap in range(1, modules):
        sum_copy(gap).start()
    all_sums[module] = sums[...]
    place_pixels(members, lows_highs, lanes, range(chunks // 2, chunks), base)
    table[...] = order_table(lows_highs, lanes)

    def spread(line):
        return pltpu.make_async_copy(
            table.at[line], order.at[pl.ds(line * LANES, LANES)], order_sem.at[3 + line]
        )

    for line in range(table.shape[0]):
        spread(line).start()

    @pl.loop(0, slabs)
    def _(index):
        turned[columns_of(index), :] = intensity(index).T

    for gap in range(1, modules):
        sum_copy(gap).wait()
    bin_sums = all_sums[0]
    for source in range(1, modules):
        bin_sums = bin_sums + all_sums[source]
    all_sums[0] = jnp.sqrt(f32(gathered)) / bin_sums

    for line in range(table.shape[0]):
        spread(line).wait()
    row_index = lax.broadcasted_iota(jnp.int32, (8, frames), 0)

    def fill(label, part, target, first_row):
        factor = all_sums[0, pl.ds(label, 1), :]

        def tile(start):
            lines = jnp.broadcast_to(turned[pl.ds(order[start], 1), :], (8, frames))
            for row in range(1, 8):
                line = turned[pl.ds(order[start + row], 1), :]
                lines = jnp.where(row_index == row, line, lines)
            return lines * factor

        def tiles(group, carry):
            start = label * per_bin + part * share + group * 16
            both = jnp.concatenate([tile(start), tile(start + 8)], axis=0)
            rows = pl.ds(pl.multiple_of(first_row + group * 16, 16), 16)
            target[rows, :] = both.astype(bf16)
            return carry

        lax.fori_loop(0, share // 16, tiles, 0, unroll=4)

    def bin_copy(k, piece):
        gap, part = piece // PIECES, lax.rem(piece, PIECES)
        owner = lax.rem(module + gap, modules)
        start = pl.multiple_of(part * share, share)
        landing = pl.multiple_of(module * per_bin + part * share, share)
        return pltpu.make_async_remote_copy(
            src_ref=packed.at[owner * owned + k, pl.ds(start, share), :],
            dst_ref=own.at[k, pl.ds(landing, share), :],
            send_sem=bin_send.at[0],
            recv_sem=bin_recv.at[k, piece],
            device_id=(me, owner),
            device_id_type=MESH,
        )

    def rows_of(j):
        source = lax.rem(module + modules - j // PIECES, modules)
        start = source * per_bin + lax.rem(j, PIECES) * share
        return pl.ds(pl.multiple_of(start, share), share)

    def frame_copy(flow, k, j, target, frame):
        return pltpu.make_async_remote_copy(
            src_ref=own.at[k, rows_of(j), :],
            dst_ref=target.at[rows_of(j), :],
            send_sem=frame_send.at[flow],
            recv_sem=frame_recv.at[flow, k],
            device_id=(frame, module),
            device_id_type=MESH,
        )

    def whole_copy(flow, k, source, target, frame):
        return pltpu.make_async_remote_copy(
            src_ref=source,
            dst_ref=target,
            send_sem=frame_send.at[flow],
            recv_sem=frame_recv.at[flow, k],
            device_id=(frame, module),
            device_id_type=MESH,
        )

    def near_copy(k, j):
        return frame_copy(0, k, j, near.at[k], mate)

    def first_copy(k, j):
        return frame_copy(1, k, j, first.at[k], jnp.where(is_one, flip(3), flip(1)))

    def second_copy(k, j):
        return frame_copy(2, k, j, second.at[k], flip(6))

    def third_copy(k, j):
        return frame_copy(3, k, j, third.at[k // 2], flip(1))

    def shared(k):
        return lax.rem(k, 2) == side

    def pass_on(k, j):
        @pl.when(is_one | is_two)
        def _():
            first_copy(k, j).start()

        @pl.when(is_three)
        def _():
            second_copy(k, j).start()

        @pl.when(is_three & shared(k))
        def _():
            third_copy(k, j).start()

        near_copy(k, j).start()

    def pick(table, turn):
        found = turn * 0
        for row, others in enumerate(table):
            for column, other in enumerate(others):
                here = (module == row) & (turn == column)
                found = jnp.where(here, (other - row) % modules, found)
        return found

    def fill_for(k, turn):
        gap = jnp.where(k < LATE, pick(SEND_ORDER, turn - 1), pick(LATE_ORDER, turn - 1))
        label = lax.rem(module + gap, modules) * owned + k

        @pl.loop(0, PIECES)
        def _(part):
            fill(label, part, packed.at[label], part * share)
            bin_copy(k, PIECES * gap + part).start()

    def fill_own(k):
        @pl.loop(0, PIECES)
        def _(part):
            first_row = module * per_bin + part * share
            fill(module * owned + k, part, own.at[k], first_row)
            pass_on(k, part)

    one_results = ((2, 0, 1), (2, 4, 0), (4, 2, 0), (3, 4, 1), (4, 3, 1))
    three_results = ((1, 3, 0),)

    def coded_copies(k, stage, slot, frame):
        pairs = ((coded, landed), (coded_peak, landed_peak))
        return [
            pltpu.make_async_remote_copy(
                src_ref=source.at[stage, k],
                dst_ref=target.at[slot, k],
                send_sem=coded_send.at[index],
                recv_sem=coded_recv.at[index, slot, k],
                device_id=(frame, module),
                device_id_type=MESH,
            )
            for index, (source, target) in enumerate(pairs)
        ]

    def send_coded(k, stage, result, values):
        peak = jnp.max(values, axis=0, keepdims=True)
        levels = values * (32767.0 / peak) + 0.5
        coded[stage, k] = levels.astype(jnp.int32).astype(jnp.int16)
        coded_peak[stage, k] = jnp.broadcast_to(peak * (1.0 / 32767.0), (8, frames))
        for copy in coded_copies(k, stage, result[2], flip(result[0])):
            copy.start()

    def decode(k, slot, gap):
        for copy in coded_copies(k, 0, slot, me):
            copy.wait_recv()
        values = landed[slot, k].astype(jnp.int32).astype(f32)
        total[k, place(gap)] = values * landed_peak[slot, k, :1, :]

    def direct_copy(k):
        return pltpu.make_async_remote_copy(
            src_ref=direct.at[k],
            dst_ref=total.at[k, jnp.where(role < 2, place(2), place(-1))],
            send_sem=direct_send.at[0],
            recv_sem=direct_recv.at[k],
            device_id=(mate, module),
            device_id_type=MESH,
        )

    def await_frames(k, flow, target):
        whole_copy(flow, k, own.at[k], target, mate).wait_recv()

    def work(k, step):
        if step == 0:
            await_frames(k, 0, near.at[k])

            @pl.when(is_one)
            def _():
                await_frames(k, 1, first.at[k])
                send_coded(k, 0, one_results[0], gram(first[k], near[k]))

            @pl.when(is_three)
            def _():
                await_frames(k, 1, first.at[k])
                send_coded(k, 0, three_results[0], gram(first[k], own[k]))

        if step == 1:

            @pl.when(is_one)
            def _():
                await_frames(k, 2, second.at[k])
                send_coded(k, 2, one_results[2], gram(second[k], first[k]))

            @pl.when(is_three)
            def _():
                direct[k] = gram(near[k], first[k])
                direct_copy(k).start()

        if step == 2:

            @pl.when(is_one)
            def _():
                send_coded(k, 1, one_results[1], gram(first[k], second[k]))

            @pl.when(is_three)
            def _():
                total[k, place(-2)] = gram(own[k], first[k])

        if step == 3:

            @pl.when(is_one & shared(k))
            def _():
                await_frames(k, 3, third.at[k // 2])
                send_coded(k, 4, one_results[4], gram(second[k], third[k // 2]))
                send_coded(k, 3, one_results[3], gram(third[k // 2], second[k]))

        if step == 4:

            @pl.when(is_one)
            def _():
                direct[k] = gram(near[k], first[k])
                direct_copy(k).start()
                total[k, place(1)] = gram(own[k], first[k])

        if step == 5:
            total[k, mate - me + 2] = gram(own[k], near[k])
            total[k, 2] = gram(own[k], own[k])

    def finish(k):
        @pl.when((role == 0) | is_two)
        def _():
            direct_copy(k).wait_recv()

        @pl.when(role > 0)
        def _():
            decode(k, 0, 2)

        @pl.when(is_two)
        def _():
            decode(k, 1, -2)

        @pl.when(is_three)
        def _():
            decode(k, 1, 1)

    @pl.loop(0, owned)
    def _(k):
        @pl.loop(1, modules)
        def _(turn):
            fill_for(k, turn)

        fill_own(k)

    @pl.when(role == 0)
    def _():
        for k in range(owned):
            total[k, place(-1)] = jnp.zeros((frames, frames), f32)

    @pl.when(role < 2)
    def _():
        for k in range(owned):
            total[k, place(-2)] = jnp.zeros((frames, frames), f32)

    at_end = (module == 0) | (module == modules - 1)

    def choose(values, index):
        found = index * 0 + values[0]
        for spot, value in enumerate(values):
            found = jnp.where(index == spot, value, found)
        return found

    def take(spot):
        end_k, end_column = (choose(values, spot) for values in zip(*END_ARRIVALS))
        middle_k, middle_column = (choose(values, spot) for values in zip(*MIDDLE_ARRIVALS))
        k = jnp.where(at_end, end_k, middle_k)
        gap = modules - pick(HEARD, jnp.where(at_end, end_column, middle_column))

        @pl.loop(0, PIECES)
        def _(part):
            piece = PIECES * gap + part
            bin_copy(k, piece).wait_recv()
            pass_on(k, piece)

    early = 8

    @pl.loop(0, early)
    def _(spot):
        take(spot)

    @pl.loop(0, owned)
    def _(k):
        for stage in range(6):
            work(k, stage)

        @pl.when(k < owned - 1)
        def _():
            take(early + k + jnp.minimum(k, 1))

        @pl.when(k == 0)
        def _():
            take(early + 1 + k)

        @pl.when(k >= 1)
        def _():
            finish(k - 1)

    finish(owned - 1)

    sent = packed.at[pl.ds(0, bins - owned)]
    pltpu.make_async_remote_copy(
        src_ref=sent,
        dst_ref=sent,
        send_sem=bin_send.at[0],
        recv_sem=bin_recv.at[0, 0],
        device_id=(mate, module),
        device_id_type=MESH,
    ).wait_send()
    whole_copy(0, 0, own, near, mate).wait_send()

    def await_coded(rows):
        for index, source in enumerate((coded, coded_peak)):
            pltpu.make_async_remote_copy(
                src_ref=source.at[pl.ds(0, rows)],
                dst_ref=source.at[pl.ds(0, rows)],
                send_sem=coded_send.at[index],
                recv_sem=coded_recv.at[index, 0, 0],
                device_id=(mate, module),
                device_id_type=MESH,
            ).wait_send()

    @pl.when(is_one | is_two)
    def _():
        whole_copy(1, 0, own, first, mate).wait_send()

    @pl.when(is_three)
    def _():
        whole_copy(2, 0, own, second, mate).wait_send()
        whole_copy(3, 0, own.at[pl.ds(0, owned // 2)], third, mate).wait_send()
        await_coded(1)

    @pl.when(is_one)
    def _():
        await_coded(4)

    @pl.when(is_one | is_three)
    def _():
        pltpu.make_async_remote_copy(
            src_ref=direct,
            dst_ref=direct,
            send_sem=direct_send.at[0],
            recv_sem=direct_recv.at[0],
            device_id=(mate, module),
            device_id_type=MESH,
        ).wait_send()


def correlate_square(raw_frames, dark_frame, flat_field, membership):
    frames, pixels = raw_frames.shape
    bins = membership.shape[0]
    modules = lax.axis_size("module")
    per_bin = pixels // bins
    owned = bins // modules
    gathered = per_bin * modules
    slab = 2 * per_bin
    vmem = pl.BlockSpec(memory_space=pltpu.VMEM)
    dma = pltpu.SemaphoreType.DMA
    f32, bf16 = jnp.float32, jnp.bfloat16
    block = (owned, gathered, frames)
    return pl.pallas_call(
        functools.partial(square_kernel, modules),
        out_shape=pltpu.VMEM((owned, 5, frames, frames), f32),
        in_specs=[
            pl.BlockSpec(memory_space=pl.ANY),
            pl.BlockSpec(memory_space=pl.ANY),
            pl.BlockSpec(memory_space=pl.ANY),
            pl.BlockSpec(memory_space=pl.ANY),
        ],
        out_specs=vmem,
        scratch_shapes=[
            pltpu.VMEM((1, pixels), f32),
            pltpu.VMEM((1, pixels), f32),
            pltpu.VMEM((bins, pixels), jnp.int32),
            pltpu.VMEM((2 * pixels // LANES, pixels), bf16),
            pltpu.VMEM((LANES, pixels), bf16),
            pltpu.VMEM((pixels // LANES, LANES), jnp.int32),
            pltpu.SMEM((pixels,), jnp.int32),
            pltpu.VMEM((pixels // slab, frames, slab), jnp.int32),
            pltpu.VMEM((pixels, frames), f32),
            pltpu.VMEM((bins, frames), f32),
            pltpu.VMEM((modules, bins, frames), f32),
            pltpu.VMEM((bins, per_bin, frames), bf16),
            pltpu.VMEM(block, bf16),
            pltpu.VMEM(block, bf16),
            pltpu.VMEM(block, bf16),
            pltpu.VMEM(block, bf16),
            pltpu.VMEM((owned // 2, gathered, frames), bf16),
            pltpu.VMEM((owned, frames, frames), f32),
            pltpu.VMEM((5, owned, frames, frames), jnp.int16),
            pltpu.VMEM((5, owned, 8, frames), f32),
            pltpu.VMEM((2, owned, frames, frames), jnp.int16),
            pltpu.VMEM((2, owned, 8, frames), f32),
            dma((pixels // slab,)),
            dma((3 + pixels // LANES,)),
            dma((modules - 1,)),
            dma((modules - 1,)),
            dma((1,)),
            dma((owned, PIECES * modules)),
            dma((4,)),
            dma((4, owned)),
            dma((1,)),
            dma((owned,)),
            dma((2,)),
            dma((2, 2, owned)),
        ],
        compiler_params=pltpu.CompilerParams(
            collective_id=1, has_side_effects=True, vmem_limit_bytes=SQUARE_BYTES
        ),
    )(raw_frames, dark_frame[None, :], flat_field[None, :], membership)


def per_device(raw_frames, dark_frame, flat_field, membership):
    square = lax.axis_size("frame") == 8 and lax.axis_size("module") == 4
    if square and membership.shape[0] == 16:
        result = correlate_square(raw_frames, dark_frame, flat_field, membership)
    else:
        order = pixel_order(membership)
        turned, sums = turn(raw_frames, dark_frame, flat_field, membership)
        result = correlate_chain(order, turned, sums)
    return result[:, None]


def solution(mesh):
    in_specs = (P("frame", "module"), P("module"), P("module"), P(None, "module"))
    out_specs = P("module", "frame", None, None, None)
    return jax.shard_map(
        per_device, mesh=mesh, in_specs=in_specs, out_specs=out_specs, check_vma=False
    )
```

```python
import functools

import jax
import jax.numpy as jnp
from jax import lax
from jax.experimental import pallas as pl
from jax.experimental.pallas import tpu as pltpu
from jax.sharding import PartitionSpec as P

MESH = pl.DeviceIdType.MESH
VMEM_BYTES = 60 * 1024 * 1024
SQUARE_BYTES = 57 * 1024 * 1024
LANES = 128
PIECES = 4
SEND_ORDER = ((3, 2, 1), (2, 3, 0), (1, 0, 3), (0, 1, 2))
LATE_ORDER = ((3, 2, 1), (3, 2, 0), (0, 1, 3), (0, 1, 2))
LATE = 3
HEARD = ((1, 3, 2), (0, 3, 2), (3, 0, 1), (2, 0, 1))
END_ARRIVALS = ((0, 0), (0, 1), (1, 0), (1, 1), (0, 2), (2, 0), (2, 1), (3, 0), (3, 1), (1, 2), (2, 2), (3, 2))
MIDDLE_ARRIVALS = ((0, 0), (0, 1), (1, 0), (1, 1), (0, 2), (2, 0), (2, 1), (1, 2), (3, 1), (3, 0), (2, 2), (3, 2))


def place_pixels(members, lows_highs, lanes, chunks, base):
    bins, pixels = members.shape
    per_bin = pixels // bins
    span = 2 * LANES
    rows = pixels // LANES
    f32, bf16 = jnp.float32, jnp.bfloat16
    shape = (span, span + LANES)
    upto = lax.broadcasted_iota(jnp.int32, shape, 0) <= lax.broadcasted_iota(jnp.int32, shape, 1)
    upto = upto.astype(f32).astype(bf16)
    if base is None:
        base = lax.broadcasted_iota(jnp.int32, (bins, span), 0).astype(f32) * per_bin - 1.0
    row_of = lax.broadcasted_iota(jnp.int32, (rows, span), 0)
    lane_of = lax.broadcasted_iota(jnp.int32, (LANES, span), 0)
    place = lax.broadcasted_iota(jnp.int32, (rows, span), 1).astype(f32)
    for chunk in chunks:
        columns = slice(chunk * span, (chunk + 1) * span)
        one_hot = members[:, columns].astype(f32)
        seen = jnp.dot(one_hot.astype(bf16), upto, preferred_element_type=f32)
        slot = one_hot * (seen[:, :span] + base)
        slot = jnp.sum(slot, axis=0, keepdims=True).astype(jnp.int32)
        base = base + jnp.concatenate([seen[:, span:]] * 2, axis=1)
        in_row = row_of == jnp.broadcast_to(slot // LANES, (rows, span))
        in_lane = lane_of == jnp.broadcast_to(slot % LANES, (LANES, span))
        lanes[:, columns] = in_lane.astype(f32).astype(bf16)
        lows_highs[:rows, columns] = jnp.where(in_row, place, 0.0).astype(bf16)
        lows_highs[rows:, columns] = jnp.where(in_row, float(chunk), 0.0).astype(bf16)
    return base


def order_table(lows_highs, lanes):
    rows, pixels = lows_highs.shape[0] // 2, lows_highs.shape[1]
    both = (((1,), (1,)), ((), ()))
    table = lax.dot_general(
        lows_highs[...], lanes[...], both, preferred_element_type=jnp.float32
    )
    table = (table[rows:] * (2 * LANES) + table[:rows]).astype(jnp.int32)
    return jnp.clip(table, 0, pixels - 1)


def order_kernel(members, order, lows_highs, lanes):
    chunks = range(members.shape[1] // (2 * LANES))
    place_pixels(members, lows_highs, lanes, chunks, None)
    order[...] = order_table(lows_highs, lanes)


def pixel_order(membership):
    pixels = membership.shape[1]
    vmem = pl.BlockSpec(memory_space=pltpu.VMEM)
    table = pl.pallas_call(
        order_kernel,
        out_shape=jax.ShapeDtypeStruct((pixels // LANES, LANES), jnp.int32),
        in_specs=[vmem],
        out_specs=vmem,
        scratch_shapes=[
            pltpu.VMEM((2 * pixels // LANES, pixels), jnp.bfloat16),
            pltpu.VMEM((LANES, pixels), jnp.bfloat16),
        ],
    )(membership)
    return table.reshape(pixels)


def turn_kernel(raw, dark, flat, members, turned, sums):
    @pl.when(pl.program_id(0) == 0)
    def _():
        sums[...] = jnp.zeros_like(sums)

    intensity = (raw[...].astype(jnp.float32) - dark[...]) * flat[...]
    lines = intensity.T
    turned[...] = lines
    sums[...] += jnp.dot(
        members[...].astype(jnp.float32),
        lines,
        precision=lax.Precision.HIGHEST,
        preferred_element_type=jnp.float32,
    )


def turn(raw_frames, dark_frame, flat_field, membership):
    frames, pixels = raw_frames.shape
    bins = membership.shape[0]
    chunk = pixels // bins
    return pl.pallas_call(
        turn_kernel,
        out_shape=(
            jax.ShapeDtypeStruct((pixels, frames), jnp.float32),
            jax.ShapeDtypeStruct((bins, frames), jnp.float32),
        ),
        grid=(pixels // chunk,),
        in_specs=[
            pl.BlockSpec((frames, chunk), lambda i: (0, i)),
            pl.BlockSpec((1, chunk), lambda i: (0, i)),
            pl.BlockSpec((1, chunk), lambda i: (0, i)),
            pl.BlockSpec((bins, chunk), lambda i: (0, i)),
        ],
        out_specs=(
            pl.BlockSpec((chunk, frames), lambda i: (i, 0)),
            pl.BlockSpec((bins, frames), lambda i: (0, 0)),
        ),
    )(raw_frames, dark_frame[None, :], flat_field[None, :], membership)


def gram(left, right):
    return lax.dot_general(
        left, right, (((0,), (0,)), ((), ())), preferred_element_type=jnp.float32
    )


def chain_kernel(
    blocks,
    modules,
    order,
    turned,
    sums,
    out,
    all_sums,
    scaled,
    own,
    far,
    near,
    hold,
    staged,
    sum_send,
    sum_recv,
    bin_send,
    bin_recv,
    frame_send,
    frame_recv,
    relay_send,
    relay_recv,
    result_send,
    result_recv,
):
    me = lax.axis_index("frame")
    module = lax.axis_index("module")
    pixels, frames = turned.shape
    bins = sums.shape[0]
    per_bin = pixels // bins
    owned = bins // modules
    even = lax.rem(me, 2) == 0
    odd = lax.rem(me, 2) == 1
    has_down = me >= 2
    has_up = me + 2 < blocks
    mate = me + 1 - 2 * lax.rem(me, 2)
    relayed = blocks == 8
    across = lax.rem(me + 4, 8)
    relaying = (me < 2) | (me >= 6)
    relay_parity = jnp.where(me >= 6, 1 - lax.rem(me, 2), lax.rem(me, 2))
    relay_target = jnp.where(even, 2, 5)

    barrier = pltpu.get_barrier_semaphore()

    def greet(frame, mod):
        pl.semaphore_signal(barrier, inc=1, device_id=(frame, mod), device_id_type=MESH)

    for gap in range(1, modules):
        greet(me, lax.rem(module + gap, modules))
    greet(mate, module)
    if relayed:
        greet(across, module)

    @pl.when(has_down)
    def _():
        greet(me - 2, module)

    @pl.when(has_up)
    def _():
        greet(me + 2, module)

    peers = modules + int(relayed) + has_down.astype(jnp.int32) + has_up.astype(jnp.int32)
    pl.semaphore_wait(barrier, peers)

    def sum_copy(gap):
        return pltpu.make_async_remote_copy(
            src_ref=sums,
            dst_ref=all_sums.at[module],
            send_sem=sum_send.at[gap - 1],
            recv_sem=sum_recv.at[gap - 1],
            device_id=(me, lax.rem(module + gap, modules)),
            device_id_type=MESH,
        )

    for gap in range(1, modules):
        sum_copy(gap).start()
    all_sums[module] = sums[...]
    for gap in range(1, modules):
        sum_copy(gap).wait()
    total = all_sums[0]
    for source in range(1, modules):
        total = total + all_sums[source]
    all_sums[0] = jnp.sqrt(jnp.float32(per_bin * modules)) / total

    half = per_bin // 2
    parts = 2 * modules

    def bin_copy(k, piece):
        gap, part = piece // 2, lax.rem(piece, 2)
        owner = lax.rem(module + gap, modules)
        start = pl.multiple_of(part * half, half)
        landing = pl.multiple_of(module * per_bin + part * half, half)
        return pltpu.make_async_remote_copy(
            src_ref=scaled.at[owner * owned + k, pl.ds(start, half), :],
            dst_ref=own.at[k, pl.ds(landing, half), :],
            send_sem=bin_send.at[k, piece],
            recv_sem=bin_recv.at[k, piece],
            device_id=(me, owner),
            device_id_type=MESH,
        )

    row_index = lax.broadcasted_iota(jnp.int32, (8, frames), 0)

    def fill(label, target, first):
        factor = all_sums[0, pl.ds(label, 1), :]

        def tile(start):
            lines = jnp.broadcast_to(turned[pl.ds(order[start], 1), :], (8, frames))
            for row in range(1, 8):
                line = turned[pl.ds(order[start + row], 1), :]
                lines = jnp.where(row_index == row, line, lines)
            return lines * factor

        def tiles(group, carry):
            start = label * per_bin + group * 16
            both = jnp.concatenate([tile(start), tile(start + 8)], axis=0)
            rows = pl.ds(pl.multiple_of(first + group * 16, 16), 16)
            target[rows, :] = both.astype(jnp.bfloat16)
            return carry

        lax.fori_loop(0, per_bin // 16, tiles, 0, unroll=4)

    def rows_of(j):
        source = lax.rem(module + modules - j // 2, modules)
        return pl.ds(pl.multiple_of(source * per_bin + lax.rem(j, 2) * half, half), half)

    def frame_copy(k, j, slot, target, frame):
        return pltpu.make_async_remote_copy(
            src_ref=own.at[k, rows_of(j), :],
            dst_ref=target.at[k, rows_of(j), :],
            send_sem=frame_send.at[slot, k, j],
            recv_sem=frame_recv.at[slot, k, j],
            device_id=(frame, module),
            device_id_type=MESH,
        )

    def far_copy(k, j):
        return frame_copy(k, j, 0, far, jnp.where(even, me - 2, me + 2))

    def mate_copy(k, j):
        return frame_copy(k, j, 1, near, mate)

    def entry_copy(k, j):
        straight = jnp.where(even, me + 2, me - 2)
        return pltpu.make_async_remote_copy(
            src_ref=own.at[k, rows_of(j), :],
            dst_ref=hold.at[k, rows_of(j), :],
            send_sem=frame_send.at[0, k, j],
            recv_sem=relay_recv.at[k, j],
            device_id=(jnp.where(lax.rem(k, 2) == 0, across, straight), module),
            device_id_type=MESH,
        )

    def exit_copy(k, j):
        return pltpu.make_async_remote_copy(
            src_ref=hold.at[k, rows_of(j), :],
            dst_ref=far.at[k, rows_of(j), :],
            send_sem=relay_send.at[k, j],
            recv_sem=frame_recv.at[0, k, j],
            device_id=(relay_target, module),
            device_id_type=MESH,
        )

    sends_far = (even & has_down) | (odd & has_up)
    diagonal = ((me == 3) | (me == 4)) if relayed else None

    def result_copy(k, stage, place, frame):
        return pltpu.make_async_remote_copy(
            src_ref=staged.at[stage, k],
            dst_ref=out.at[k, place],
            send_sem=result_send.at[stage, k],
            recv_sem=result_recv.at[place, k],
            device_id=(frame, module),
            device_id_type=MESH,
        )

    def pass_on(k, j):
        @pl.when(odd)
        def _():
            mate_copy(k, j).start()

        if relayed:
            @pl.when(diagonal)
            def _():
                entry_copy(k, j).start()

            @pl.when(sends_far & jnp.logical_not(diagonal))
            def _():
                far_copy(k, j).start()
        else:
            @pl.when(sends_far)
            def _():
                far_copy(k, j).start()

    def relay(k, j):
        if relayed:
            @pl.when(relaying & (lax.rem(k, 2) == relay_parity))
            def _():
                entry_copy(k, j).wait_recv()
                exit_copy(k, j).start()

    def await_frames(k, copy):
        for j in range(parts):
            copy(k, j).wait_recv()

    def correlate(k):
        out[k, 2] = gram(own[k], own[k])

        @pl.when(even)
        def _():
            await_frames(k, mate_copy)
            staged[0, k] = gram(near[k], own[k])
            result_copy(k, 0, 1, me + 1).start()
            out[k, 3] = gram(own[k], near[k])

        @pl.when(even & has_up)
        def _():
            await_frames(k, far_copy)
            staged[1, k] = gram(far[k], own[k])
            result_copy(k, 1, 0, me + 2).start()
            staged[2, k] = gram(far[k], near[k])
            result_copy(k, 2, 1, me + 2).start()
            staged[3, k] = gram(near[k], far[k])
            result_copy(k, 3, 3, me + 1).start()
            out[k, 4] = gram(own[k], far[k])

        @pl.when(odd & has_down)
        def _():
            await_frames(k, far_copy)
            staged[0, k] = gram(far[k], own[k])
            result_copy(k, 0, 4, me - 2).start()
            out[k, 0] = gram(own[k], far[k])

    @pl.loop(0, owned)
    def _(k):
        @pl.loop(1, modules)
        def _(gap):
            label = lax.rem(module + gap, modules) * owned + k
            fill(label, scaled.at[label], 0)
            bin_copy(k, 2 * gap).start()
            bin_copy(k, 2 * gap + 1).start()

        fill(module * owned + k, own.at[k], module * per_bin)
        pass_on(k, 0)
        pass_on(k, 1)

    @pl.loop(0, owned)
    def _(k):
        relay(k, 0)
        relay(k, 1)

    def receive(k, gaps):
        pieces = [2 * gap + part for gap in gaps for part in range(2)]
        for index, piece in enumerate(pieces):
            bin_copy(k, piece).wait()
            pass_on(k, piece)
            if index:
                relay(k, pieces[index - 1])
        relay(k, pieces[-1])

    @pl.loop(0, owned + 1)
    def _(turn_index):
        @pl.when(turn_index < owned)
        def _():
            receive(turn_index, range(1, modules))

        @pl.when(turn_index >= 1)
        def _():
            correlate(turn_index - 1)

    @pl.when(me < 2)
    def _():
        out[:, 0] = jnp.zeros_like(out[:, 0])

    @pl.when(me < 1)
    def _():
        out[:, 1] = jnp.zeros_like(out[:, 1])

    @pl.when(me + 1 >= blocks)
    def _():
        out[:, 3] = jnp.zeros_like(out[:, 3])

    @pl.when(me + 2 >= blocks)
    def _():
        out[:, 4] = jnp.zeros_like(out[:, 4])

    @pl.loop(0, owned)
    def _(k):
        @pl.when(even & has_down)
        def _():
            result_copy(k, 1, 0, me).wait_recv()
            result_copy(k, 2, 1, me).wait_recv()

        @pl.when(odd)
        def _():
            for j in range(parts):
                mate_copy(k, j).wait_send()
            result_copy(k, 0, 1, me).wait_recv()

        @pl.when(sends_far)
        def _():
            for j in range(parts):
                far_copy(k, j).wait_send()

        @pl.when(odd & has_up)
        def _():
            result_copy(k, 3, 3, me).wait_recv()
            result_copy(k, 0, 4, me).wait_recv()

        if relayed:
            @pl.when(relaying & (lax.rem(k, 2) == relay_parity))
            def _():
                for j in range(parts):
                    exit_copy(k, j).wait_send()

        @pl.when(even)
        def _():
            result_copy(k, 0, 1, me + 1).wait_send()

        @pl.when(even & has_up)
        def _():
            result_copy(k, 1, 0, me + 2).wait_send()
            result_copy(k, 2, 1, me + 2).wait_send()
            result_copy(k, 3, 3, me + 1).wait_send()

        @pl.when(odd & has_down)
        def _():
            result_copy(k, 0, 4, me - 2).wait_send()


def correlate_chain(order, turned, sums):
    (pixels, frames), bins = turned.shape, sums.shape[0]
    per_bin = pixels // bins
    blocks, modules = lax.axis_size("frame"), lax.axis_size("module")
    owned = bins // modules
    gathered = per_bin * modules
    vmem = pl.BlockSpec(memory_space=pltpu.VMEM)
    dma = pltpu.SemaphoreType.DMA
    return pl.pallas_call(
        functools.partial(chain_kernel, blocks, modules),
        out_shape=jax.ShapeDtypeStruct((owned, 5, frames, frames), jnp.float32),
        in_specs=[pl.BlockSpec(memory_space=pltpu.SMEM), vmem, vmem],
        out_specs=vmem,
        scratch_shapes=[
            pltpu.VMEM((modules, bins, frames), jnp.float32),
            pltpu.VMEM((bins, per_bin, frames), jnp.bfloat16),
            pltpu.VMEM((owned, gathered, frames), jnp.bfloat16),
            pltpu.VMEM((owned, gathered, frames), jnp.bfloat16),
            pltpu.VMEM((owned, gathered, frames), jnp.bfloat16),
            pltpu.VMEM((owned, gathered, frames), jnp.bfloat16),
            pltpu.VMEM((4, owned, frames, frames), jnp.float32),
            dma((modules - 1,)),
            dma((modules - 1,)),
            dma((owned, 2 * modules)),
            dma((owned, 2 * modules)),
            dma((2, owned, 2 * modules)),
            dma((2, owned, 2 * modules)),
            dma((owned, 2 * modules)),
            dma((owned, 2 * modules)),
            dma((4, owned)),
            dma((5, owned)),
        ],
        compiler_params=pltpu.CompilerParams(
            collective_id=0, has_side_effects=True, vmem_limit_bytes=VMEM_BYTES
        ),
    )(order, turned, sums)


def square_kernel(
    modules,
    raw,
    dark_frame,
    flat_field,
    membership,
    total,
    dark,
    flat,
    members,
    lows_highs,
    lanes,
    table,
    order,
    counts_in,
    turned,
    sums,
    all_sums,
    packed,
    own,
    near,
    first,
    second,
    third,
    direct,
    coded,
    coded_peak,
    landed,
    landed_peak,
    raw_sem,
    order_sem,
    sum_send,
    sum_recv,
    bin_send,
    bin_recv,
    frame_send,
    frame_recv,
    direct_send,
    direct_recv,
    coded_send,
    coded_recv,
):
    me = lax.axis_index("frame")
    module = lax.axis_index("module")
    pixels, frames = turned.shape
    bins = packed.shape[0]
    per_bin = pixels // bins
    owned = bins // modules
    gathered = per_bin * modules
    share = per_bin // PIECES
    f32, bf16 = jnp.float32, jnp.bfloat16

    side = me // 4
    sign = 1 - 2 * side

    def flip(block):
        return jnp.where(side == 1, 7 - block, block)

    role = flip(me)
    mate = me + 1 - 2 * lax.rem(me, 2)
    is_one, is_two, is_three = role == 1, role == 2, role == 3

    def place(gap):
        return 2 + sign * gap

    barrier = pltpu.get_barrier_semaphore()

    def greet(frame, mod):
        pl.semaphore_signal(barrier, inc=1, device_id=(frame, mod), device_id_type=MESH)

    for gap in range(1, modules):
        greet(me, lax.rem(module + gap, modules))
    greet(mate, module)

    @pl.when(is_one)
    def _():
        greet(flip(2), module)
        greet(flip(3), module)
        greet(flip(4), module)

    @pl.when(is_two | is_three)
    def _():
        greet(flip(1), module)

    @pl.when(is_three)
    def _():
        greet(flip(6), module)

    slabs, _, slab = counts_in.shape

    def columns_of(index):
        return pl.ds(pl.multiple_of(index * slab, slab), slab)

    def load(index):
        return pltpu.make_async_copy(
            raw.at[:, columns_of(index)], counts_in.at[index], raw_sem.at[index]
        )

    def intensity(index):
        columns = columns_of(index)
        return (counts_in[index].astype(f32) - dark[:, columns]) * flat[:, columns]

    fetch = pltpu.make_async_copy(membership, members, order_sem.at[0])
    fetch.start()
    fetch_dark = pltpu.make_async_copy(dark_frame, dark, order_sem.at[1])
    fetch_dark.start()
    fetch_flat = pltpu.make_async_copy(flat_field, flat, order_sem.at[2])
    fetch_flat.start()
    sums[...] = jnp.zeros_like(sums)
    load(0).start()
    fetch.wait()
    for index in range(1, slabs):
        load(index).start()
    chunks = pixels // (2 * LANES)
    base = place_pixels(members, lows_highs, lanes, range(chunks // 2), None)
    fetch_dark.wait()
    fetch_flat.wait()

    @pl.loop(0, slabs)
    def _(index):
        load(index).wait()
        values = intensity(index)
        high = values.astype(bf16)
        low = (values - high.astype(f32)).astype(bf16)
        one_hot = members[:, columns_of(index)].astype(f32).astype(bf16)
        both = (((1,), (1,)), ((), ()))
        sums[...] += lax.dot_general(
            one_hot, high, both, preferred_element_type=f32
        ) + lax.dot_general(one_hot, low, both, preferred_element_type=f32)

    peers = modules + jnp.where(is_one, 3, jnp.where(is_three, 2, jnp.where(is_two, 1, 0)))
    pl.semaphore_wait(barrier, peers)

    def sum_copy(gap):
        return pltpu.make_async_remote_copy(
            src_ref=sums,
            dst_ref=all_sums.at[module],
            send_sem=sum_send.at[gap - 1],
            recv_sem=sum_recv.at[gap - 1],
            device_id=(me, lax.rem(module + gap, modules)),
            device_id_type=MESH,
        )

    for gap in range(1, modules):
        sum_copy(gap).start()
    all_sums[module] = sums[...]
    place_pixels(members, lows_highs, lanes, range(chunks // 2, chunks), base)
    table[...] = order_table(lows_highs, lanes)

    def spread(line):
        return pltpu.make_async_copy(
            table.at[line], order.at[pl.ds(line * LANES, LANES)], order_sem.at[3 + line]
        )

    for line in range(table.shape[0]):
        spread(line).start()

    for index in range(slabs):
        turned[columns_of(index), :] = intensity(index).T

    for gap in range(1, modules):
        sum_copy(gap).wait()
    bin_sums = all_sums[0]
    for source in range(1, modules):
        bin_sums = bin_sums + all_sums[source]
    all_sums[0] = jnp.sqrt(f32(gathered)) / bin_sums

    for line in range(table.shape[0]):
        spread(line).wait()
    row_index = lax.broadcasted_iota(jnp.int32, (8, frames), 0)

    def fill(label, part, target, first_row):
        factor = all_sums[0, pl.ds(label, 1), :]

        def tile(start):
            lines = jnp.broadcast_to(turned[pl.ds(order[start], 1), :], (8, frames))
            for row in range(1, 8):
                line = turned[pl.ds(order[start + row], 1), :]
                lines = jnp.where(row_index == row, line, lines)
            return lines * factor

        def tiles(group, carry):
            start = label * per_bin + part * share + group * 16
            both = jnp.concatenate([tile(start), tile(start + 8)], axis=0)
            rows = pl.ds(pl.multiple_of(first_row + group * 16, 16), 16)
            target[rows, :] = both.astype(bf16)
            return carry

        lax.fori_loop(0, share // 16, tiles, 0, unroll=4)

    def bin_copy(k, piece):
        gap, part = piece // PIECES, lax.rem(piece, PIECES)
        owner = lax.rem(module + gap, modules)
        start = pl.multiple_of(part * share, share)
        landing = pl.multiple_of(module * per_bin + part * share, share)
        return pltpu.make_async_remote_copy(
            src_ref=packed.at[owner * owned + k, pl.ds(start, share), :],
            dst_ref=own.at[k, pl.ds(landing, share), :],
            send_sem=bin_send.at[0],
            recv_sem=bin_recv.at[k, piece],
            device_id=(me, owner),
            device_id_type=MESH,
        )

    def rows_of(j):
        source = lax.rem(module + modules - j // PIECES, modules)
        start = source * per_bin + lax.rem(j, PIECES) * share
        return pl.ds(pl.multiple_of(start, share), share)

    def frame_copy(flow, k, j, target, frame):
        return pltpu.make_async_remote_copy(
            src_ref=own.at[k, rows_of(j), :],
            dst_ref=target.at[rows_of(j), :],
            send_sem=frame_send.at[flow],
            recv_sem=frame_recv.at[flow, k],
            device_id=(frame, module),
            device_id_type=MESH,
        )

    def whole_copy(flow, k, source, target, frame):
        return pltpu.make_async_remote_copy(
            src_ref=source,
            dst_ref=target,
            send_sem=frame_send.at[flow],
            recv_sem=frame_recv.at[flow, k],
            device_id=(frame, module),
            device_id_type=MESH,
        )

    def near_copy(k, j):
        return frame_copy(0, k, j, near.at[k], mate)

    def first_copy(k, j):
        return frame_copy(1, k, j, first.at[k], jnp.where(is_one, flip(3), flip(1)))

    def second_copy(k, j):
        return frame_copy(2, k, j, second.at[k], flip(6))

    def third_copy(k, j):
        return frame_copy(3, k, j, third.at[k // 2], flip(1))

    def shared(k):
        return lax.rem(k, 2) == side

    def pass_on(k, j):
        @pl.when(is_one | is_two)
        def _():
            first_copy(k, j).start()

        @pl.when(is_three)
        def _():
            second_copy(k, j).start()

        @pl.when(is_three & shared(k))
        def _():
            third_copy(k, j).start()

        near_copy(k, j).start()

    def pick(table, turn):
        found = turn * 0
        for row, others in enumerate(table):
            for column, other in enumerate(others):
                here = (module == row) & (turn == column)
                found = jnp.where(here, (other - row) % modules, found)
        return found

    def fill_for(k, turn):
        gap = jnp.where(k < LATE, pick(SEND_ORDER, turn - 1), pick(LATE_ORDER, turn - 1))
        label = lax.rem(module + gap, modules) * owned + k

        @pl.loop(0, PIECES)
        def _(part):
            fill(label, part, packed.at[label], part * share)
            bin_copy(k, PIECES * gap + part).start()

    def fill_own(k):
        @pl.loop(0, PIECES)
        def _(part):
            first_row = module * per_bin + part * share
            fill(module * owned + k, part, own.at[k], first_row)
            pass_on(k, part)

    one_results = ((2, 0, 1), (2, 4, 0), (4, 2, 0), (3, 4, 1), (4, 3, 1))
    three_results = ((1, 3, 0),)

    def coded_copies(k, stage, slot, frame):
        pairs = ((coded, landed), (coded_peak, landed_peak))
        return [
            pltpu.make_async_remote_copy(
                src_ref=source.at[stage, k],
                dst_ref=target.at[slot, k],
                send_sem=coded_send.at[index],
                recv_sem=coded_recv.at[index, slot, k],
                device_id=(frame, module),
                device_id_type=MESH,
            )
            for index, (source, target) in enumerate(pairs)
        ]

    def send_coded(k, stage, result, values):
        peak = jnp.max(values, axis=0, keepdims=True)
        levels = values * (32767.0 / peak) + 0.5
        coded[stage, k] = levels.astype(jnp.int32).astype(jnp.int16)
        coded_peak[stage, k] = jnp.broadcast_to(peak * (1.0 / 32767.0), (8, frames))
        for copy in coded_copies(k, stage, result[2], flip(result[0])):
            copy.start()

    def decode(k, slot, gap):
        for copy in coded_copies(k, 0, slot, me):
            copy.wait_recv()
        values = landed[slot, k].astype(jnp.int32).astype(f32)
        total[k, place(gap)] = values * landed_peak[slot, k, :1, :]

    def direct_copy(k):
        return pltpu.make_async_remote_copy(
            src_ref=direct.at[k],
            dst_ref=total.at[k, jnp.where(role < 2, place(2), place(-1))],
            send_sem=direct_send.at[0],
            recv_sem=direct_recv.at[k],
            device_id=(mate, module),
            device_id_type=MESH,
        )

    def await_frames(k, flow, target):
        whole_copy(flow, k, own.at[k], target, mate).wait_recv()

    def work(k, step):
        if step == 0:
            await_frames(k, 0, near.at[k])

            @pl.when(is_one)
            def _():
                await_frames(k, 1, first.at[k])
                send_coded(k, 0, one_results[0], gram(first[k], near[k]))

            @pl.when(is_three)
            def _():
                await_frames(k, 1, first.at[k])
                send_coded(k, 0, three_results[0], gram(first[k], own[k]))

        if step == 1:

            @pl.when(is_one)
            def _():
                await_frames(k, 2, second.at[k])
                send_coded(k, 2, one_results[2], gram(second[k], first[k]))

            @pl.when(is_three)
            def _():
                direct[k] = gram(near[k], first[k])
                direct_copy(k).start()

        if step == 2:

            @pl.when(is_one)
            def _():
                send_coded(k, 1, one_results[1], gram(first[k], second[k]))

            @pl.when(is_three)
            def _():
                total[k, place(-2)] = gram(own[k], first[k])

        if step == 3:

            @pl.when(is_one & shared(k))
            def _():
                await_frames(k, 3, third.at[k // 2])
                send_coded(k, 4, one_results[4], gram(second[k], third[k // 2]))
                send_coded(k, 3, one_results[3], gram(third[k // 2], second[k]))

        if step == 4:

            @pl.when(is_one)
            def _():
                direct[k] = gram(near[k], first[k])
                direct_copy(k).start()
                total[k, place(1)] = gram(own[k], first[k])

        if step == 5:
            total[k, mate - me + 2] = gram(own[k], near[k])
            total[k, 2] = gram(own[k], own[k])

    def finish(k):
        @pl.when((role == 0) | is_two)
        def _():
            direct_copy(k).wait_recv()

        @pl.when(role > 0)
        def _():
            decode(k, 0, 2)

        @pl.when(is_two)
        def _():
            decode(k, 1, -2)

        @pl.when(is_three)
        def _():
            decode(k, 1, 1)

    @pl.loop(0, owned)
    def _(k):
        @pl.loop(1, modules)
        def _(turn):
            fill_for(k, turn)

        fill_own(k)

    @pl.when(role == 0)
    def _():
        for k in range(owned):
            total[k, place(-1)] = jnp.zeros((frames, frames), f32)

    @pl.when(role < 2)
    def _():
        for k in range(owned):
            total[k, place(-2)] = jnp.zeros((frames, frames), f32)

    at_end = (module == 0) | (module == modules - 1)

    def choose(values, index):
        found = index * 0 + values[0]
        for spot, value in enumerate(values):
            found = jnp.where(index == spot, value, found)
        return found

    def take(spot):
        end_k, end_column = (choose(values, spot) for values in zip(*END_ARRIVALS))
        middle_k, middle_column = (choose(values, spot) for values in zip(*MIDDLE_ARRIVALS))
        k = jnp.where(at_end, end_k, middle_k)
        gap = modules - pick(HEARD, jnp.where(at_end, end_column, middle_column))

        @pl.loop(0, PIECES)
        def _(part):
            piece = PIECES * gap + part
            bin_copy(k, piece).wait_recv()
            pass_on(k, piece)

    early = 8

    @pl.loop(0, early)
    def _(spot):
        take(spot)

    @pl.loop(0, owned)
    def _(k):
        for stage in range(6):
            work(k, stage)

        @pl.when(k < owned - 1)
        def _():
            take(early + k + jnp.minimum(k, 1))

        @pl.when(k == 0)
        def _():
            take(early + 1 + k)

        @pl.when(k >= 1)
        def _():
            finish(k - 1)

    finish(owned - 1)

    sent = packed.at[pl.ds(0, bins - owned)]
    pltpu.make_async_remote_copy(
        src_ref=sent,
        dst_ref=sent,
        send_sem=bin_send.at[0],
        recv_sem=bin_recv.at[0, 0],
        device_id=(mate, module),
        device_id_type=MESH,
    ).wait_send()
    whole_copy(0, 0, own, near, mate).wait_send()

    def await_coded(rows):
        for index, source in enumerate((coded, coded_peak)):
            pltpu.make_async_remote_copy(
                src_ref=source.at[pl.ds(0, rows)],
                dst_ref=source.at[pl.ds(0, rows)],
                send_sem=coded_send.at[index],
                recv_sem=coded_recv.at[index, 0, 0],
                device_id=(mate, module),
                device_id_type=MESH,
            ).wait_send()

    @pl.when(is_one | is_two)
    def _():
        whole_copy(1, 0, own, first, mate).wait_send()

    @pl.when(is_three)
    def _():
        whole_copy(2, 0, own, second, mate).wait_send()
        whole_copy(3, 0, own.at[pl.ds(0, owned // 2)], third, mate).wait_send()
        await_coded(1)

    @pl.when(is_one)
    def _():
        await_coded(4)

    @pl.when(is_one | is_three)
    def _():
        pltpu.make_async_remote_copy(
            src_ref=direct,
            dst_ref=direct,
            send_sem=direct_send.at[0],
            recv_sem=direct_recv.at[0],
            device_id=(mate, module),
            device_id_type=MESH,
        ).wait_send()


def correlate_square(raw_frames, dark_frame, flat_field, membership):
    frames, pixels = raw_frames.shape
    bins = membership.shape[0]
    modules = lax.axis_size("module")
    per_bin = pixels // bins
    owned = bins // modules
    gathered = per_bin * modules
    slab = 2 * per_bin
    vmem = pl.BlockSpec(memory_space=pltpu.VMEM)
    dma = pltpu.SemaphoreType.DMA
    f32, bf16 = jnp.float32, jnp.bfloat16
    block = (owned, gathered, frames)
    return pl.pallas_call(
        functools.partial(square_kernel, modules),
        out_shape=pltpu.VMEM((owned, 5, frames, frames), f32),
        in_specs=[
            pl.BlockSpec(memory_space=pl.ANY),
            pl.BlockSpec(memory_space=pl.ANY),
            pl.BlockSpec(memory_space=pl.ANY),
            pl.BlockSpec(memory_space=pl.ANY),
        ],
        out_specs=vmem,
        scratch_shapes=[
            pltpu.VMEM((1, pixels), f32),
            pltpu.VMEM((1, pixels), f32),
            pltpu.VMEM((bins, pixels), jnp.int32),
            pltpu.VMEM((2 * pixels // LANES, pixels), bf16),
            pltpu.VMEM((LANES, pixels), bf16),
            pltpu.VMEM((pixels // LANES, LANES), jnp.int32),
            pltpu.SMEM((pixels,), jnp.int32),
            pltpu.VMEM((pixels // slab, frames, slab), jnp.int32),
            pltpu.VMEM((pixels, frames), f32),
            pltpu.VMEM((bins, frames), f32),
            pltpu.VMEM((modules, bins, frames), f32),
            pltpu.VMEM((bins, per_bin, frames), bf16),
            pltpu.VMEM(block, bf16),
            pltpu.VMEM(block, bf16),
            pltpu.VMEM(block, bf16),
            pltpu.VMEM(block, bf16),
            pltpu.VMEM((owned // 2, gathered, frames), bf16),
            pltpu.VMEM((owned, frames, frames), f32),
            pltpu.VMEM((5, owned, frames, frames), jnp.int16),
            pltpu.VMEM((5, owned, 8, frames), f32),
            pltpu.VMEM((2, owned, frames, frames), jnp.int16),
            pltpu.VMEM((2, owned, 8, frames), f32),
            dma((pixels // slab,)),
            dma((3 + pixels // LANES,)),
            dma((modules - 1,)),
            dma((modules - 1,)),
            dma((1,)),
            dma((owned, PIECES * modules)),
            dma((4,)),
            dma((4, owned)),
            dma((1,)),
            dma((owned,)),
            dma((2,)),
            dma((2, 2, owned)),
        ],
        compiler_params=pltpu.CompilerParams(
            collective_id=1, has_side_effects=True, vmem_limit_bytes=SQUARE_BYTES
        ),
    )(raw_frames, dark_frame[None, :], flat_field[None, :], membership)


def per_device(raw_frames, dark_frame, flat_field, membership):
    square = lax.axis_size("frame") == 8 and lax.axis_size("module") == 4
    if square and membership.shape[0] == 16:
        result = correlate_square(raw_frames, dark_frame, flat_field, membership)
    else:
        order = pixel_order(membership)
        turned, sums = turn(raw_frames, dark_frame, flat_field, membership)
        result = correlate_chain(order, turned, sums)
    return result[:, None]


def solution(mesh):
    in_specs = (P("frame", "module"), P("module"), P("module"), P(None, "module"))
    out_specs = P("module", "frame", None, None, None)
    return jax.shard_map(
        per_device, mesh=mesh, in_specs=in_specs, out_specs=out_specs, check_vma=False
    )
```

```python
import functools

import jax
import jax.numpy as jnp
from jax import lax
from jax.experimental import pallas as pl
from jax.experimental.pallas import tpu as pltpu
from jax.sharding import PartitionSpec as P

MESH = pl.DeviceIdType.MESH
VMEM_BYTES = 60 * 1024 * 1024
SQUARE_BYTES = 57 * 1024 * 1024
LANES = 128
PIECES = 8
SEND_ORDER = ((3, 2, 1), (2, 3, 0), (1, 0, 3), (0, 1, 2))
LATE_ORDER = ((3, 2, 1), (3, 2, 0), (0, 1, 3), (0, 1, 2))
LATE = 3
HEARD = ((1, 3, 2), (0, 3, 2), (3, 0, 1), (2, 0, 1))
END_ARRIVALS = ((0, 0), (0, 1), (1, 0), (1, 1), (0, 2), (2, 0), (2, 1), (3, 0), (3, 1), (1, 2), (2, 2), (3, 2))
MIDDLE_ARRIVALS = ((0, 0), (0, 1), (1, 0), (1, 1), (0, 2), (2, 0), (2, 1), (1, 2), (3, 1), (3, 0), (2, 2), (3, 2))


def place_pixels(members, lows_highs, lanes, chunks, base):
    bins, pixels = members.shape
    per_bin = pixels // bins
    span = 2 * LANES
    rows = pixels // LANES
    f32, bf16 = jnp.float32, jnp.bfloat16
    shape = (span, span + LANES)
    upto = lax.broadcasted_iota(jnp.int32, shape, 0) <= lax.broadcasted_iota(jnp.int32, shape, 1)
    upto = upto.astype(f32).astype(bf16)
    if base is None:
        base = lax.broadcasted_iota(jnp.int32, (bins, span), 0).astype(f32) * per_bin - 1.0
    row_of = lax.broadcasted_iota(jnp.int32, (rows, span), 0)
    lane_of = lax.broadcasted_iota(jnp.int32, (LANES, span), 0)
    place = lax.broadcasted_iota(jnp.int32, (rows, span), 1).astype(f32)
    for chunk in chunks:
        columns = slice(chunk * span, (chunk + 1) * span)
        one_hot = members[:, columns].astype(f32)
        seen = jnp.dot(one_hot.astype(bf16), upto, preferred_element_type=f32)
        slot = one_hot * (seen[:, :span] + base)
        slot = jnp.sum(slot, axis=0, keepdims=True).astype(jnp.int32)
        base = base + jnp.concatenate([seen[:, span:]] * 2, axis=1)
        in_row = row_of == jnp.broadcast_to(slot // LANES, (rows, span))
        in_lane = lane_of == jnp.broadcast_to(slot % LANES, (LANES, span))
        lanes[:, columns] = in_lane.astype(f32).astype(bf16)
        lows_highs[:rows, columns] = jnp.where(in_row, place, 0.0).astype(bf16)
        lows_highs[rows:, columns] = jnp.where(in_row, float(chunk), 0.0).astype(bf16)
    return base


def order_table(lows_highs, lanes):
    rows, pixels = lows_highs.shape[0] // 2, lows_highs.shape[1]
    both = (((1,), (1,)), ((), ()))
    table = lax.dot_general(
        lows_highs[...], lanes[...], both, preferred_element_type=jnp.float32
    )
    table = (table[rows:] * (2 * LANES) + table[:rows]).astype(jnp.int32)
    return jnp.clip(table, 0, pixels - 1)


def order_kernel(members, order, lows_highs, lanes):
    chunks = range(members.shape[1] // (2 * LANES))
    place_pixels(members, lows_highs, lanes, chunks, None)
    order[...] = order_table(lows_highs, lanes)


def pixel_order(membership):
    pixels = membership.shape[1]
    vmem = pl.BlockSpec(memory_space=pltpu.VMEM)
    table = pl.pallas_call(
        order_kernel,
        out_shape=jax.ShapeDtypeStruct((pixels // LANES, LANES), jnp.int32),
        in_specs=[vmem],
        out_specs=vmem,
        scratch_shapes=[
            pltpu.VMEM((2 * pixels // LANES, pixels), jnp.bfloat16),
            pltpu.VMEM((LANES, pixels), jnp.bfloat16),
        ],
    )(membership)
    return table.reshape(pixels)


def turn_kernel(raw, dark, flat, members, turned, sums):
    @pl.when(pl.program_id(0) == 0)
    def _():
        sums[...] = jnp.zeros_like(sums)

    intensity = (raw[...].astype(jnp.float32) - dark[...]) * flat[...]
    lines = intensity.T
    turned[...] = lines
    sums[...] += jnp.dot(
        members[...].astype(jnp.float32),
        lines,
        precision=lax.Precision.HIGHEST,
        preferred_element_type=jnp.float32,
    )


def turn(raw_frames, dark_frame, flat_field, membership):
    frames, pixels = raw_frames.shape
    bins = membership.shape[0]
    chunk = pixels // bins
    return pl.pallas_call(
        turn_kernel,
        out_shape=(
            jax.ShapeDtypeStruct((pixels, frames), jnp.float32),
            jax.ShapeDtypeStruct((bins, frames), jnp.float32),
        ),
        grid=(pixels // chunk,),
        in_specs=[
            pl.BlockSpec((frames, chunk), lambda i: (0, i)),
            pl.BlockSpec((1, chunk), lambda i: (0, i)),
            pl.BlockSpec((1, chunk), lambda i: (0, i)),
            pl.BlockSpec((bins, chunk), lambda i: (0, i)),
        ],
        out_specs=(
            pl.BlockSpec((chunk, frames), lambda i: (i, 0)),
            pl.BlockSpec((bins, frames), lambda i: (0, 0)),
        ),
    )(raw_frames, dark_frame[None, :], flat_field[None, :], membership)


def gram(left, right):
    return lax.dot_general(
        left, right, (((0,), (0,)), ((), ())), preferred_element_type=jnp.float32
    )


def chain_kernel(
    blocks,
    modules,
    order,
    turned,
    sums,
    out,
    all_sums,
    scaled,
    own,
    far,
    near,
    hold,
    staged,
    sum_send,
    sum_recv,
    bin_send,
    bin_recv,
    frame_send,
    frame_recv,
    relay_send,
    relay_recv,
    result_send,
    result_recv,
):
    me = lax.axis_index("frame")
    module = lax.axis_index("module")
    pixels, frames = turned.shape
    bins = sums.shape[0]
    per_bin = pixels // bins
    owned = bins // modules
    even = lax.rem(me, 2) == 0
    odd = lax.rem(me, 2) == 1
    has_down = me >= 2
    has_up = me + 2 < blocks
    mate = me + 1 - 2 * lax.rem(me, 2)
    relayed = blocks == 8
    across = lax.rem(me + 4, 8)
    relaying = (me < 2) | (me >= 6)
    relay_parity = jnp.where(me >= 6, 1 - lax.rem(me, 2), lax.rem(me, 2))
    relay_target = jnp.where(even, 2, 5)

    barrier = pltpu.get_barrier_semaphore()

    def greet(frame, mod):
        pl.semaphore_signal(barrier, inc=1, device_id=(frame, mod), device_id_type=MESH)

    for gap in range(1, modules):
        greet(me, lax.rem(module + gap, modules))
    greet(mate, module)
    if relayed:
        greet(across, module)

    @pl.when(has_down)
    def _():
        greet(me - 2, module)

    @pl.when(has_up)
    def _():
        greet(me + 2, module)

    peers = modules + int(relayed) + has_down.astype(jnp.int32) + has_up.astype(jnp.int32)
    pl.semaphore_wait(barrier, peers)

    def sum_copy(gap):
        return pltpu.make_async_remote_copy(
            src_ref=sums,
            dst_ref=all_sums.at[module],
            send_sem=sum_send.at[gap - 1],
            recv_sem=sum_recv.at[gap - 1],
            device_id=(me, lax.rem(module + gap, modules)),
            device_id_type=MESH,
        )

    for gap in range(1, modules):
        sum_copy(gap).start()
    all_sums[module] = sums[...]
    for gap in range(1, modules):
        sum_copy(gap).wait()
    total = all_sums[0]
    for source in range(1, modules):
        total = total + all_sums[source]
    all_sums[0] = jnp.sqrt(jnp.float32(per_bin * modules)) / total

    half = per_bin // 2
    parts = 2 * modules

    def bin_copy(k, piece):
        gap, part = piece // 2, lax.rem(piece, 2)
        owner = lax.rem(module + gap, modules)
        start = pl.multiple_of(part * half, half)
        landing = pl.multiple_of(module * per_bin + part * half, half)
        return pltpu.make_async_remote_copy(
            src_ref=scaled.at[owner * owned + k, pl.ds(start, half), :],
            dst_ref=own.at[k, pl.ds(landing, half), :],
            send_sem=bin_send.at[k, piece],
            recv_sem=bin_recv.at[k, piece],
            device_id=(me, owner),
            device_id_type=MESH,
        )

    row_index = lax.broadcasted_iota(jnp.int32, (8, frames), 0)

    def fill(label, target, first):
        factor = all_sums[0, pl.ds(label, 1), :]

        def tile(start):
            lines = jnp.broadcast_to(turned[pl.ds(order[start], 1), :], (8, frames))
            for row in range(1, 8):
                line = turned[pl.ds(order[start + row], 1), :]
                lines = jnp.where(row_index == row, line, lines)
            return lines * factor

        def tiles(group, carry):
            start = label * per_bin + group * 16
            both = jnp.concatenate([tile(start), tile(start + 8)], axis=0)
            rows = pl.ds(pl.multiple_of(first + group * 16, 16), 16)
            target[rows, :] = both.astype(jnp.bfloat16)
            return carry

        lax.fori_loop(0, per_bin // 16, tiles, 0, unroll=4)

    def rows_of(j):
        source = lax.rem(module + modules - j // 2, modules)
        return pl.ds(pl.multiple_of(source * per_bin + lax.rem(j, 2) * half, half), half)

    def frame_copy(k, j, slot, target, frame):
        return pltpu.make_async_remote_copy(
            src_ref=own.at[k, rows_of(j), :],
            dst_ref=target.at[k, rows_of(j), :],
            send_sem=frame_send.at[slot, k, j],
            recv_sem=frame_recv.at[slot, k, j],
            device_id=(frame, module),
            device_id_type=MESH,
        )

    def far_copy(k, j):
        return frame_copy(k, j, 0, far, jnp.where(even, me - 2, me + 2))

    def mate_copy(k, j):
        return frame_copy(k, j, 1, near, mate)

    def entry_copy(k, j):
        straight = jnp.where(even, me + 2, me - 2)
        return pltpu.make_async_remote_copy(
            src_ref=own.at[k, rows_of(j), :],
            dst_ref=hold.at[k, rows_of(j), :],
            send_sem=frame_send.at[0, k, j],
            recv_sem=relay_recv.at[k, j],
            device_id=(jnp.where(lax.rem(k, 2) == 0, across, straight), module),
            device_id_type=MESH,
        )

    def exit_copy(k, j):
        return pltpu.make_async_remote_copy(
            src_ref=hold.at[k, rows_of(j), :],
            dst_ref=far.at[k, rows_of(j), :],
            send_sem=relay_send.at[k, j],
            recv_sem=frame_recv.at[0, k, j],
            device_id=(relay_target, module),
            device_id_type=MESH,
        )

    sends_far = (even & has_down) | (odd & has_up)
    diagonal = ((me == 3) | (me == 4)) if relayed else None

    def result_copy(k, stage, place, frame):
        return pltpu.make_async_remote_copy(
            src_ref=staged.at[stage, k],
            dst_ref=out.at[k, place],
            send_sem=result_send.at[stage, k],
            recv_sem=result_recv.at[place, k],
            device_id=(frame, module),
            device_id_type=MESH,
        )

    def pass_on(k, j):
        @pl.when(odd)
        def _():
            mate_copy(k, j).start()

        if relayed:
            @pl.when(diagonal)
            def _():
                entry_copy(k, j).start()

            @pl.when(sends_far & jnp.logical_not(diagonal))
            def _():
                far_copy(k, j).start()
        else:
            @pl.when(sends_far)
            def _():
                far_copy(k, j).start()

    def relay(k, j):
        if relayed:
            @pl.when(relaying & (lax.rem(k, 2) == relay_parity))
            def _():
                entry_copy(k, j).wait_recv()
                exit_copy(k, j).start()

    def await_frames(k, copy):
        for j in range(parts):
            copy(k, j).wait_recv()

    def correlate(k):
        out[k, 2] = gram(own[k], own[k])

        @pl.when(even)
        def _():
            await_frames(k, mate_copy)
            staged[0, k] = gram(near[k], own[k])
            result_copy(k, 0, 1, me + 1).start()
            out[k, 3] = gram(own[k], near[k])

        @pl.when(even & has_up)
        def _():
            await_frames(k, far_copy)
            staged[1, k] = gram(far[k], own[k])
            result_copy(k, 1, 0, me + 2).start()
            staged[2, k] = gram(far[k], near[k])
            result_copy(k, 2, 1, me + 2).start()
            staged[3, k] = gram(near[k], far[k])
            result_copy(k, 3, 3, me + 1).start()
            out[k, 4] = gram(own[k], far[k])

        @pl.when(odd & has_down)
        def _():
            await_frames(k, far_copy)
            staged[0, k] = gram(far[k], own[k])
            result_copy(k, 0, 4, me - 2).start()
            out[k, 0] = gram(own[k], far[k])

    @pl.loop(0, owned)
    def _(k):
        @pl.loop(1, modules)
        def _(gap):
            label = lax.rem(module + gap, modules) * owned + k
            fill(label, scaled.at[label], 0)
            bin_copy(k, 2 * gap).start()
            bin_copy(k, 2 * gap + 1).start()

        fill(module * owned + k, own.at[k], module * per_bin)
        pass_on(k, 0)
        pass_on(k, 1)

    @pl.loop(0, owned)
    def _(k):
        relay(k, 0)
        relay(k, 1)

    def receive(k, gaps):
        pieces = [2 * gap + part for gap in gaps for part in range(2)]
        for index, piece in enumerate(pieces):
            bin_copy(k, piece).wait()
            pass_on(k, piece)
            if index:
                relay(k, pieces[index - 1])
        relay(k, pieces[-1])

    @pl.loop(0, owned + 1)
    def _(turn_index):
        @pl.when(turn_index < owned)
        def _():
            receive(turn_index, range(1, modules))

        @pl.when(turn_index >= 1)
        def _():
            correlate(turn_index - 1)

    @pl.when(me < 2)
    def _():
        out[:, 0] = jnp.zeros_like(out[:, 0])

    @pl.when(me < 1)
    def _():
        out[:, 1] = jnp.zeros_like(out[:, 1])

    @pl.when(me + 1 >= blocks)
    def _():
        out[:, 3] = jnp.zeros_like(out[:, 3])

    @pl.when(me + 2 >= blocks)
    def _():
        out[:, 4] = jnp.zeros_like(out[:, 4])

    @pl.loop(0, owned)
    def _(k):
        @pl.when(even & has_down)
        def _():
            result_copy(k, 1, 0, me).wait_recv()
            result_copy(k, 2, 1, me).wait_recv()

        @pl.when(odd)
        def _():
            for j in range(parts):
                mate_copy(k, j).wait_send()
            result_copy(k, 0, 1, me).wait_recv()

        @pl.when(sends_far)
        def _():
            for j in range(parts):
                far_copy(k, j).wait_send()

        @pl.when(odd & has_up)
        def _():
            result_copy(k, 3, 3, me).wait_recv()
            result_copy(k, 0, 4, me).wait_recv()

        if relayed:
            @pl.when(relaying & (lax.rem(k, 2) == relay_parity))
            def _():
                for j in range(parts):
                    exit_copy(k, j).wait_send()

        @pl.when(even)
        def _():
            result_copy(k, 0, 1, me + 1).wait_send()

        @pl.when(even & has_up)
        def _():
            result_copy(k, 1, 0, me + 2).wait_send()
            result_copy(k, 2, 1, me + 2).wait_send()
            result_copy(k, 3, 3, me + 1).wait_send()

        @pl.when(odd & has_down)
        def _():
            result_copy(k, 0, 4, me - 2).wait_send()


def correlate_chain(order, turned, sums):
    (pixels, frames), bins = turned.shape, sums.shape[0]
    per_bin = pixels // bins
    blocks, modules = lax.axis_size("frame"), lax.axis_size("module")
    owned = bins // modules
    gathered = per_bin * modules
    vmem = pl.BlockSpec(memory_space=pltpu.VMEM)
    dma = pltpu.SemaphoreType.DMA
    return pl.pallas_call(
        functools.partial(chain_kernel, blocks, modules),
        out_shape=jax.ShapeDtypeStruct((owned, 5, frames, frames), jnp.float32),
        in_specs=[pl.BlockSpec(memory_space=pltpu.SMEM), vmem, vmem],
        out_specs=vmem,
        scratch_shapes=[
            pltpu.VMEM((modules, bins, frames), jnp.float32),
            pltpu.VMEM((bins, per_bin, frames), jnp.bfloat16),
            pltpu.VMEM((owned, gathered, frames), jnp.bfloat16),
            pltpu.VMEM((owned, gathered, frames), jnp.bfloat16),
            pltpu.VMEM((owned, gathered, frames), jnp.bfloat16),
            pltpu.VMEM((owned, gathered, frames), jnp.bfloat16),
            pltpu.VMEM((4, owned, frames, frames), jnp.float32),
            dma((modules - 1,)),
            dma((modules - 1,)),
            dma((owned, 2 * modules)),
            dma((owned, 2 * modules)),
            dma((2, owned, 2 * modules)),
            dma((2, owned, 2 * modules)),
            dma((owned, 2 * modules)),
            dma((owned, 2 * modules)),
            dma((4, owned)),
            dma((5, owned)),
        ],
        compiler_params=pltpu.CompilerParams(
            collective_id=0, has_side_effects=True, vmem_limit_bytes=VMEM_BYTES
        ),
    )(order, turned, sums)


def square_kernel(
    modules,
    raw,
    dark_frame,
    flat_field,
    membership,
    total,
    dark,
    flat,
    members,
    lows_highs,
    lanes,
    table,
    order,
    counts_in,
    turned,
    sums,
    all_sums,
    packed,
    own,
    near,
    first,
    second,
    third,
    direct,
    coded,
    coded_peak,
    landed,
    landed_peak,
    raw_sem,
    order_sem,
    sum_send,
    sum_recv,
    bin_send,
    bin_recv,
    frame_send,
    frame_recv,
    direct_send,
    direct_recv,
    coded_send,
    coded_recv,
):
    me = lax.axis_index("frame")
    module = lax.axis_index("module")
    pixels, frames = turned.shape
    bins = packed.shape[0]
    per_bin = pixels // bins
    owned = bins // modules
    gathered = per_bin * modules
    share = per_bin // PIECES
    f32, bf16 = jnp.float32, jnp.bfloat16

    side = me // 4
    sign = 1 - 2 * side

    def flip(block):
        return jnp.where(side == 1, 7 - block, block)

    role = flip(me)
    mate = me + 1 - 2 * lax.rem(me, 2)
    is_one, is_two, is_three = role == 1, role == 2, role == 3

    def place(gap):
        return 2 + sign * gap

    barrier = pltpu.get_barrier_semaphore()

    def greet(frame, mod):
        pl.semaphore_signal(barrier, inc=1, device_id=(frame, mod), device_id_type=MESH)

    for gap in range(1, modules):
        greet(me, lax.rem(module + gap, modules))
    greet(mate, module)

    @pl.when(is_one)
    def _():
        greet(flip(2), module)
        greet(flip(3), module)
        greet(flip(4), module)

    @pl.when(is_two | is_three)
    def _():
        greet(flip(1), module)

    @pl.when(is_three)
    def _():
        greet(flip(6), module)

    slabs, _, slab = counts_in.shape

    def columns_of(index):
        return pl.ds(pl.multiple_of(index * slab, slab), slab)

    def load(index):
        return pltpu.make_async_copy(
            raw.at[:, columns_of(index)], counts_in.at[index], raw_sem.at[index]
        )

    def intensity(index):
        columns = columns_of(index)
        return (counts_in[index].astype(f32) - dark[:, columns]) * flat[:, columns]

    fetch = pltpu.make_async_copy(membership, members, order_sem.at[0])
    fetch.start()
    fetch_dark = pltpu.make_async_copy(dark_frame, dark, order_sem.at[1])
    fetch_dark.start()
    fetch_flat = pltpu.make_async_copy(flat_field, flat, order_sem.at[2])
    fetch_flat.start()
    sums[...] = jnp.zeros_like(sums)
    load(0).start()
    fetch.wait()
    for index in range(1, slabs):
        load(index).start()
    chunks = pixels // (2 * LANES)
    base = place_pixels(members, lows_highs, lanes, range(chunks // 2), None)
    fetch_dark.wait()
    fetch_flat.wait()

    @pl.loop(0, slabs)
    def _(index):
        load(index).wait()
        values = intensity(index)
        high = values.astype(bf16)
        low = (values - high.astype(f32)).astype(bf16)
        one_hot = members[:, columns_of(index)].astype(f32).astype(bf16)
        both = (((1,), (1,)), ((), ()))
        sums[...] += lax.dot_general(
            one_hot, high, both, preferred_element_type=f32
        ) + lax.dot_general(one_hot, low, both, preferred_element_type=f32)

    peers = modules + jnp.where(is_one, 3, jnp.where(is_three, 2, jnp.where(is_two, 1, 0)))
    pl.semaphore_wait(barrier, peers)

    def sum_copy(gap):
        return pltpu.make_async_remote_copy(
            src_ref=sums,
            dst_ref=all_sums.at[module],
            send_sem=sum_send.at[gap - 1],
            recv_sem=sum_recv.at[gap - 1],
            device_id=(me, lax.rem(module + gap, modules)),
            device_id_type=MESH,
        )

    for gap in range(1, modules):
        sum_copy(gap).start()
    all_sums[module] = sums[...]
    place_pixels(members, lows_highs, lanes, range(chunks // 2, chunks), base)
    table[...] = order_table(lows_highs, lanes)

    def spread(line):
        return pltpu.make_async_copy(
            table.at[line], order.at[pl.ds(line * LANES, LANES)], order_sem.at[3 + line]
        )

    for line in range(table.shape[0]):
        spread(line).start()

    for index in range(slabs):
        turned[columns_of(index), :] = intensity(index).T

    for gap in range(1, modules):
        sum_copy(gap).wait()
    bin_sums = all_sums[0]
    for source in range(1, modules):
        bin_sums = bin_sums + all_sums[source]
    all_sums[0] = jnp.sqrt(f32(gathered)) / bin_sums

    for line in range(table.shape[0]):
        spread(line).wait()
    row_index = lax.broadcasted_iota(jnp.int32, (8, frames), 0)

    def fill(label, part, target, first_row):
        factor = all_sums[0, pl.ds(label, 1), :]

        def tile(start):
            lines = jnp.broadcast_to(turned[pl.ds(order[start], 1), :], (8, frames))
            for row in range(1, 8):
                line = turned[pl.ds(order[start + row], 1), :]
                lines = jnp.where(row_index == row, line, lines)
            return lines * factor

        def tiles(group, carry):
            start = label * per_bin + part * share + group * 16
            both = jnp.concatenate([tile(start), tile(start + 8)], axis=0)
            rows = pl.ds(pl.multiple_of(first_row + group * 16, 16), 16)
            target[rows, :] = both.astype(bf16)
            return carry

        lax.fori_loop(0, share // 16, tiles, 0, unroll=4)

    def bin_copy(k, piece):
        gap, part = piece // PIECES, lax.rem(piece, PIECES)
        owner = lax.rem(module + gap, modules)
        start = pl.multiple_of(part * share, share)
        landing = pl.multiple_of(module * per_bin + part * share, share)
        return pltpu.make_async_remote_copy(
            src_ref=packed.at[owner * owned + k, pl.ds(start, share), :],
            dst_ref=own.at[k, pl.ds(landing, share), :],
            send_sem=bin_send.at[0],
            recv_sem=bin_recv.at[k, piece],
            device_id=(me, owner),
            device_id_type=MESH,
        )

    def rows_of(j):
        source = lax.rem(module + modules - j // PIECES, modules)
        start = source * per_bin + lax.rem(j, PIECES) * share
        return pl.ds(pl.multiple_of(start, share), share)

    def frame_copy(flow, k, j, target, frame):
        return pltpu.make_async_remote_copy(
            src_ref=own.at[k, rows_of(j), :],
            dst_ref=target.at[rows_of(j), :],
            send_sem=frame_send.at[flow],
            recv_sem=frame_recv.at[flow, k],
            device_id=(frame, module),
            device_id_type=MESH,
        )

    def whole_copy(flow, k, source, target, frame):
        return pltpu.make_async_remote_copy(
            src_ref=source,
            dst_ref=target,
            send_sem=frame_send.at[flow],
            recv_sem=frame_recv.at[flow, k],
            device_id=(frame, module),
            device_id_type=MESH,
        )

    def near_copy(k, j):
        return frame_copy(0, k, j, near.at[k], mate)

    def first_copy(k, j):
        return frame_copy(1, k, j, first.at[k], jnp.where(is_one, flip(3), flip(1)))

    def second_copy(k, j):
        return frame_copy(2, k, j, second.at[k], flip(6))

    def third_copy(k, j):
        return frame_copy(3, k, j, third.at[k // 2], flip(1))

    def shared(k):
        return lax.rem(k, 2) == side

    def pass_on(k, j):
        @pl.when(is_one | is_two)
        def _():
            first_copy(k, j).start()

        @pl.when(is_three)
        def _():
            second_copy(k, j).start()

        @pl.when(is_three & shared(k))
        def _():
            third_copy(k, j).start()

        near_copy(k, j).start()

    def pick(table, turn):
        found = turn * 0
        for row, others in enumerate(table):
            for column, other in enumerate(others):
                here = (module == row) & (turn == column)
                found = jnp.where(here, (other - row) % modules, found)
        return found

    def fill_for(k, turn):
        gap = jnp.where(k < LATE, pick(SEND_ORDER, turn - 1), pick(LATE_ORDER, turn - 1))
        label = lax.rem(module + gap, modules) * owned + k

        @pl.loop(0, PIECES)
        def _(part):
            fill(label, part, packed.at[label], part * share)
            bin_copy(k, PIECES * gap + part).start()

    def fill_own(k):
        @pl.loop(0, PIECES)
        def _(part):
            first_row = module * per_bin + part * share
            fill(module * owned + k, part, own.at[k], first_row)
            pass_on(k, part)

    one_results = ((2, 0, 1), (2, 4, 0), (4, 2, 0), (3, 4, 1), (4, 3, 1))
    three_results = ((1, 3, 0),)

    def coded_copies(k, stage, slot, frame):
        pairs = ((coded, landed), (coded_peak, landed_peak))
        return [
            pltpu.make_async_remote_copy(
                src_ref=source.at[stage, k],
                dst_ref=target.at[slot, k],
                send_sem=coded_send.at[index],
                recv_sem=coded_recv.at[index, slot, k],
                device_id=(frame, module),
                device_id_type=MESH,
            )
            for index, (source, target) in enumerate(pairs)
        ]

    def send_coded(k, stage, result, values):
        peak = jnp.max(values, axis=0, keepdims=True)
        levels = values * (32767.0 / peak) + 0.5
        coded[stage, k] = levels.astype(jnp.int32).astype(jnp.int16)
        coded_peak[stage, k] = jnp.broadcast_to(peak * (1.0 / 32767.0), (8, frames))
        for copy in coded_copies(k, stage, result[2], flip(result[0])):
            copy.start()

    def decode(k, slot, gap):
        for copy in coded_copies(k, 0, slot, me):
            copy.wait_recv()
        values = landed[slot, k].astype(jnp.int32).astype(f32)
        total[k, place(gap)] = values * landed_peak[slot, k, :1, :]

    def direct_copy(k):
        return pltpu.make_async_remote_copy(
            src_ref=direct.at[k],
            dst_ref=total.at[k, jnp.where(role < 2, place(2), place(-1))],
            send_sem=direct_send.at[0],
            recv_sem=direct_recv.at[k],
            device_id=(mate, module),
            device_id_type=MESH,
        )

    def await_frames(k, flow, target):
        whole_copy(flow, k, own.at[k], target, mate).wait_recv()

    def work(k, step):
        if step == 0:
            await_frames(k, 0, near.at[k])

            @pl.when(is_one)
            def _():
                await_frames(k, 1, first.at[k])
                send_coded(k, 0, one_results[0], gram(first[k], near[k]))

            @pl.when(is_three)
            def _():
                await_frames(k, 1, first.at[k])
                send_coded(k, 0, three_results[0], gram(first[k], own[k]))

        if step == 1:

            @pl.when(is_one)
            def _():
                await_frames(k, 2, second.at[k])
                send_coded(k, 2, one_results[2], gram(second[k], first[k]))

            @pl.when(is_three)
            def _():
                direct[k] = gram(near[k], first[k])
                direct_copy(k).start()

        if step == 2:

            @pl.when(is_one)
            def _():
                send_coded(k, 1, one_results[1], gram(first[k], second[k]))

            @pl.when(is_three)
            def _():
                total[k, place(-2)] = gram(own[k], first[k])

        if step == 3:

            @pl.when(is_one & shared(k))
            def _():
                await_frames(k, 3, third.at[k // 2])
                send_coded(k, 4, one_results[4], gram(second[k], third[k // 2]))
                send_coded(k, 3, one_results[3], gram(third[k // 2], second[k]))

        if step == 4:

            @pl.when(is_one)
            def _():
                direct[k] = gram(near[k], first[k])
                direct_copy(k).start()
                total[k, place(1)] = gram(own[k], first[k])

        if step == 5:
            total[k, mate - me + 2] = gram(own[k], near[k])
            total[k, 2] = gram(own[k], own[k])

    def finish(k):
        @pl.when((role == 0) | is_two)
        def _():
            direct_copy(k).wait_recv()

        @pl.when(role > 0)
        def _():
            decode(k, 0, 2)

        @pl.when(is_two)
        def _():
            decode(k, 1, -2)

        @pl.when(is_three)
        def _():
            decode(k, 1, 1)

    @pl.loop(0, owned)
    def _(k):
        @pl.loop(1, modules)
        def _(turn):
            fill_for(k, turn)

        fill_own(k)

    @pl.when(role == 0)
    def _():
        for k in range(owned):
            total[k, place(-1)] = jnp.zeros((frames, frames), f32)

    @pl.when(role < 2)
    def _():
        for k in range(owned):
            total[k, place(-2)] = jnp.zeros((frames, frames), f32)

    at_end = (module == 0) | (module == modules - 1)

    def choose(values, index):
        found = index * 0 + values[0]
        for spot, value in enumerate(values):
            found = jnp.where(index == spot, value, found)
        return found

    def take(spot):
        end_k, end_column = (choose(values, spot) for values in zip(*END_ARRIVALS))
        middle_k, middle_column = (choose(values, spot) for values in zip(*MIDDLE_ARRIVALS))
        k = jnp.where(at_end, end_k, middle_k)
        gap = modules - pick(HEARD, jnp.where(at_end, end_column, middle_column))

        @pl.loop(0, PIECES)
        def _(part):
            piece = PIECES * gap + part
            bin_copy(k, piece).wait_recv()
            pass_on(k, piece)

    early = 8

    @pl.loop(0, early)
    def _(spot):
        take(spot)

    @pl.loop(0, owned)
    def _(k):
        for stage in range(6):
            work(k, stage)

        @pl.when(k < owned - 1)
        def _():
            take(early + k + jnp.minimum(k, 1))

        @pl.when(k == 0)
        def _():
            take(early + 1 + k)

        @pl.when(k >= 1)
        def _():
            finish(k - 1)

    finish(owned - 1)

    sent = packed.at[pl.ds(0, bins - owned)]
    pltpu.make_async_remote_copy(
        src_ref=sent,
        dst_ref=sent,
        send_sem=bin_send.at[0],
        recv_sem=bin_recv.at[0, 0],
        device_id=(mate, module),
        device_id_type=MESH,
    ).wait_send()
    whole_copy(0, 0, own, near, mate).wait_send()

    def await_coded(rows):
        for index, source in enumerate((coded, coded_peak)):
            pltpu.make_async_remote_copy(
                src_ref=source.at[pl.ds(0, rows)],
                dst_ref=source.at[pl.ds(0, rows)],
                send_sem=coded_send.at[index],
                recv_sem=coded_recv.at[index, 0, 0],
                device_id=(mate, module),
                device_id_type=MESH,
            ).wait_send()

    @pl.when(is_one | is_two)
    def _():
        whole_copy(1, 0, own, first, mate).wait_send()

    @pl.when(is_three)
    def _():
        whole_copy(2, 0, own, second, mate).wait_send()
        whole_copy(3, 0, own.at[pl.ds(0, owned // 2)], third, mate).wait_send()
        await_coded(1)

    @pl.when(is_one)
    def _():
        await_coded(4)

    @pl.when(is_one | is_three)
    def _():
        pltpu.make_async_remote_copy(
            src_ref=direct,
            dst_ref=direct,
            send_sem=direct_send.at[0],
            recv_sem=direct_recv.at[0],
            device_id=(mate, module),
            device_id_type=MESH,
        ).wait_send()


def correlate_square(raw_frames, dark_frame, flat_field, membership):
    frames, pixels = raw_frames.shape
    bins = membership.shape[0]
    modules = lax.axis_size("module")
    per_bin = pixels // bins
    owned = bins // modules
    gathered = per_bin * modules
    slab = 2 * per_bin
    vmem = pl.BlockSpec(memory_space=pltpu.VMEM)
    dma = pltpu.SemaphoreType.DMA
    f32, bf16 = jnp.float32, jnp.bfloat16
    block = (owned, gathered, frames)
    return pl.pallas_call(
        functools.partial(square_kernel, modules),
        out_shape=pltpu.VMEM((owned, 5, frames, frames), f32),
        in_specs=[
            pl.BlockSpec(memory_space=pl.ANY),
            pl.BlockSpec(memory_space=pl.ANY),
            pl.BlockSpec(memory_space=pl.ANY),
            pl.BlockSpec(memory_space=pl.ANY),
        ],
        out_specs=vmem,
        scratch_shapes=[
            pltpu.VMEM((1, pixels), f32),
            pltpu.VMEM((1, pixels), f32),
            pltpu.VMEM((bins, pixels), jnp.int32),
            pltpu.VMEM((2 * pixels // LANES, pixels), bf16),
            pltpu.VMEM((LANES, pixels), bf16),
            pltpu.VMEM((pixels // LANES, LANES), jnp.int32),
            pltpu.SMEM((pixels,), jnp.int32),
            pltpu.VMEM((pixels // slab, frames, slab), jnp.int32),
            pltpu.VMEM((pixels, frames), f32),
            pltpu.VMEM((bins, frames), f32),
            pltpu.VMEM((modules, bins, frames), f32),
            pltpu.VMEM((bins, per_bin, frames), bf16),
            pltpu.VMEM(block, bf16),
            pltpu.VMEM(block, bf16),
            pltpu.VMEM(block, bf16),
            pltpu.VMEM(block, bf16),
            pltpu.VMEM((owned // 2, gathered, frames), bf16),
            pltpu.VMEM((owned, frames, frames), f32),
            pltpu.VMEM((5, owned, frames, frames), jnp.int16),
            pltpu.VMEM((5, owned, 8, frames), f32),
            pltpu.VMEM((2, owned, frames, frames), jnp.int16),
            pltpu.VMEM((2, owned, 8, frames), f32),
            dma((pixels // slab,)),
            dma((3 + pixels // LANES,)),
            dma((modules - 1,)),
            dma((modules - 1,)),
            dma((1,)),
            dma((owned, PIECES * modules)),
            dma((4,)),
            dma((4, owned)),
            dma((1,)),
            dma((owned,)),
            dma((2,)),
            dma((2, 2, owned)),
        ],
        compiler_params=pltpu.CompilerParams(
            collective_id=1, has_side_effects=True, vmem_limit_bytes=SQUARE_BYTES
        ),
    )(raw_frames, dark_frame[None, :], flat_field[None, :], membership)


def per_device(raw_frames, dark_frame, flat_field, membership):
    square = lax.axis_size("frame") == 8 and lax.axis_size("module") == 4
    if square and membership.shape[0] == 16:
        result = correlate_square(raw_frames, dark_frame, flat_field, membership)
    else:
        order = pixel_order(membership)
        turned, sums = turn(raw_frames, dark_frame, flat_field, membership)
        result = correlate_chain(order, turned, sums)
    return result[:, None]


def solution(mesh):
    in_specs = (P("frame", "module"), P("module"), P("module"), P(None, "module"))
    out_specs = P("module", "frame", None, None, None)
    return jax.shard_map(
        per_device, mesh=mesh, in_specs=in_specs, out_specs=out_specs, check_vma=False
    )
```
